32 devices in a mesh: dp: 16 (over z, y, x), mp: 2 (over core).
Axes of the slice: x: 2, y: 2, z: 4, core: 2. Of those that a mesh axis runs over, the one named last changes fastest.
Arguments:
- tokens: bfloat16 [16384, 768], P('dp'), may hold values from -6 to 6
- cotangent: bfloat16 [16384, 768], P('dp'), may hold values from -6 to 6
- seg_lengths: int32 [32, 8], P('dp'), may hold values from 1 to 256, 512 in all within a row
- pad_counts: int32 [32], P('dp'), may hold values from 0 to 64
- qkv_weight: float32 [3, 768, 768], P(None, 'dp', 'mp'), may hold values from -0.3125 to 0.3125
- first_qkv: float32 [3, 768, 768], P(None, 'dp', 'mp'), may hold values from -0.00024414062 to 0.00024414062
- second_qkv: float32 [3, 768, 768], P(None, 'dp', 'mp'), may hold values from 7.4315953e-09 to 2.974051e-08
- average_qkv: float32 [3, 768, 768], P(None, 'dp', 'mp'), may hold values from -0.3125 to 0.3125
- attn_weight: float32 [768, 768], P(('mp', 'dp')), may hold values from -0.625 to 0.625
- first_attn: float32 [768, 768], P(('mp', 'dp')), may hold values from -0.00024414062 to 0.00024414062
- second_attn: float32 [768, 768], P(('mp', 'dp')), may hold values from 7.4315953e-09 to 2.974051e-08
- average_attn: float32 [768, 768], P(('mp', 'dp')), may hold values from -0.625 to 0.625
- up_weight: float32 [768, 3072], P('dp', 'mp'), may hold values from -0.21875 to 0.21875
- first_up: float32 [768, 3072], P('dp', 'mp'), may hold values from -0.00024414062 to 0.00024414062
- second_up: float32 [768, 3072], P('dp', 'mp'), may hold values from 7.4315953e-09 to 2.974051e-08
- average_up: float32 [768, 3072], P('dp', 'mp'), may hold values from -0.21875 to 0.21875
- down_weight: float32 [3072, 768], P(('mp', 'dp')), may hold values from -0.109375 to 0.109375
- first_down: float32 [3072, 768], P(('mp', 'dp')), may hold values from -0.00024414062 to 0.00024414062
- second_down: float32 [3072, 768], P(('mp', 'dp')), may hold values from 7.4315953e-09 to 2.974051e-08
- average_down: float32 [3072, 768], P(('mp', 'dp')), may hold values from -0.109375 to 0.109375
- head_bias: float32 [2, 768], P(None, ('mp', 'dp')), may hold values from -1.75 to 1.75
- first_head: float32 [2, 768], P(None, ('mp', 'dp')), may hold values from -0.00048828125 to 0.00048828125
- second_head: float32 [2, 768], P(None, ('mp', 'dp')), may hold values from 2.974051e-08 to 1.1896204e-07
- average_head: float32 [2, 768], P(None, ('mp', 'dp')), may hold values from -1.75 to 1.75
- hidden_bias: float32 [3072], P(('mp', 'dp')), may hold values from -1.75 to 1.75
- first_hidden: float32 [3072], P(('mp', 'dp')), may hold values from -0.00015258789 to 0.00015258789
- second_hidden: float32 [3072], P(('mp', 'dp')), may hold values from 3.306071e-09 to 1.3224284e-08
- average_hidden: float32 [3072], P(('mp', 'dp')), may hold values from -1.75 to 1.75
- layer_vectors: float32 [6, 768], P(None, 'dp'), may hold values from -0.8 to 2.4
- first_vectors: float32 [6, 768], P(None, 'dp'), may hold values from -0.00048828125 to 0.00048828125
- second_vectors: float32 [6, 768], P(None, 'dp'), may hold values from 2.974051e-08 to 1.1896204e-07
- average_vectors: float32 [6, 768], P(None, 'dp'), may hold values from -3 to 3
Outputs:
- layer_output: bfloat16 [16384, 768], P('dp')
- input_grad: float32 [16384, 768], P('dp')
- grad_norm: float32 [], replicated
- moment_qkv: float32 [3, 768, 768], P(None, 'dp', 'mp')
- square_qkv: float32 [3, 768, 768], P(None, 'dp', 'mp')
- updated_qkv: float32 [3, 768, 768], P(None, 'dp', 'mp')
- smooth_qkv: float32 [3, 768, 768], P(None, 'dp', 'mp')
- moment_attn: float32 [768, 768], P(('mp', 'dp'))
- square_attn: float32 [768, 768], P(('mp', 'dp'))
- updated_attn: float32 [768, 768], P(('mp', 'dp'))
- smooth_attn: float32 [768, 768], P(('mp', 'dp'))
- moment_up: float32 [768, 3072], P('dp', 'mp')
- square_up: float32 [768, 3072], P('dp', 'mp')
- updated_up: float32 [768, 3072], P('dp', 'mp')
- smooth_up: float32 [768, 3072], P('dp', 'mp')
- moment_down: float32 [3072, 768], P(('mp', 'dp'))
- square_down: float32 [3072, 768], P(('mp', 'dp'))
- updated_down: float32 [3072, 768], P(('mp', 'dp'))
- smooth_down: float32 [3072, 768], P(('mp', 'dp'))
- moment_head: float32 [2, 768], P(None, ('mp', 'dp'))
- square_head: float32 [2, 768], P(None, ('mp', 'dp'))
- updated_head: float32 [2, 768], P(None, ('mp', 'dp'))
- smooth_head: float32 [2, 768], P(None, ('mp', 'dp'))
- moment_hidden: float32 [3072], P(('mp', 'dp'))
- square_hidden: float32 [3072], P(('mp', 'dp'))
- updated_hidden: float32 [3072], P(('mp', 'dp'))
- smooth_hidden: float32 [3072], P(('mp', 'dp'))
- moment_vectors: float32 [6, 768], P(None, 'dp')
- square_vectors: float32 [6, 768], P(None, 'dp')
- updated_vectors: float32 [6, 768], P(None, 'dp')
- smooth_vectors: float32 [6, 768], P(None, 'dp')
The draws below stay inside these ranges and needn't reach their ends.
All inputs are finite; a program needn't handle non-finite values.
Results may differ from the reference program's by a relative error of at most 0.015.
The reference program's roundings to bfloat16 on the way count: a program that leaves them out, or rounds other values in their place, can miss the bound.
Values may be sent and summed in bfloat16 or wider, within the bound.
No kernel may reach another device: no remote copies, remote signals or barrier semaphores. Data moves between devices by JAX's collectives and lax.ppermute only.
A program may use at most 192 MiB of HBM per device.

```python
import math
import jax
import jax.numpy as jnp
import numpy as np
from jax import lax

D = 768
H = 12
HD = 64
FF = 3072
SEQ = 512
NSEG = 8
STEP = 7
SEQS = 32
TOKENS = 16384


def draw_layer_vectors(key, part):
    keys_list = jax.random.split(key, 2)
    position = jnp.arange(D, dtype=jnp.float32) / D
    jitter = jax.random.uniform(keys_list[0], (2, D), jnp.float32, 0.8, 1.2)
    rising = 0.5 + position
    biases = jnp.clip(0.2 * jax.random.normal(keys_list[1], (4, D), jnp.float32), -0.8, 0.8)
    gain_rows = rising[None, :] * jitter
    return jnp.stack([gain_rows[0], biases[0], gain_rows[1], biases[1], biases[2], biases[3]], axis=0)


def plant(drawn, own_key, least, high):
    longest = drawn.shape.index(max(drawn.shape))
    spots = []
    for shift in (0, 1):
        where = [jax.random.randint(jax.random.fold_in(own_key, axis), (), 0, length) for axis, length in enumerate(drawn.shape)]
        where[longest] = (where[longest] + shift) % drawn.shape[longest]
        spots.append(tuple(where))
    return drawn.at[spots[0]].set(least).at[spots[1]].set(high)


def block_levels(own_key, shape, cuts, smallest, high):
    level = 1.0
    for dim, shards_of in cuts:
        draws = jax.random.uniform(jax.random.fold_in(jax.random.fold_in(own_key, 6), dim), (shards_of,), jnp.float32, smallest / len(cuts), high / len(cuts))
        level = level * jnp.repeat(jnp.exp(draws), shape[dim] // shards_of).reshape((-1,) + (1,) * (len(shape) - 1 - dim))
    return level


def split_up(amount, total, reach, slope):
    loads = [(1 << 20) // math.isqrt(rank ** slope) + 1 for rank in range(2, amount + 1)]
    rest, holding = total - reach - (amount - 1), [1] * (amount - 1)
    while rest > 0:
        candidates = [i for i in range(amount - 1) if holding[i] < reach]
        whole, remaining = sum([loads[i] for i in candidates]), rest
        for i in candidates:
            more = min(reach - holding[i], max(1, remaining * loads[i] // whole), rest)
            holding[i] = holding[i] + more
            rest = rest - more
    return np.array([reach] + holding)


def uneven(stream_key, count, total, bound, lean):
    if count == 2:
        one = jax.random.randint(stream_key, (), max(1, total - bound), min(bound, total - 1) + 1)
        return jnp.stack([one, total - one])
    tallies = jnp.asarray(split_up(count, total, bound, lean), jnp.int32)
    pairs = (count - 1) // 2
    donor, taker = tallies[1:1 + 2 * pairs:2], tallies[2:2 + 2 * pairs:2]
    slack = jnp.minimum(donor - 1, bound - taker)
    passed = jax.random.randint(jax.random.fold_in(stream_key, 1), (pairs,), 0, 1 << 20) % (slack + 1)
    tallies = tallies.at[1:1 + 2 * pairs:2].set(donor - passed).at[2:2 + 2 * pairs:2].set(taker + passed)
    return tallies[jax.random.permutation(jax.random.fold_in(stream_key, 2), count)]


def scatter_about(own_key, extent, spread, bound, cuts=(), held_as=jnp.bfloat16):
    factor_of = block_levels(own_key, extent, cuts, -0.22, 0.18) if cuts else 1.0
    values = jax.random.normal(own_key, extent, jnp.float32) * spread * factor_of
    return jnp.minimum(jnp.maximum(values, -bound), bound).astype(held_as)


def setup_inputs(seed: int = 0) -> dict:
    seeds = jax.random.split(jax.random.key(seed), 33)
    return {
        "tokens": scatter_about(seeds[0], (TOKENS, D), 1.0, 6.0, ((0, 16),)),
        "cotangent": scatter_about(seeds[1], (TOKENS, D), 1.0, 6.0, ((0, 16),)),
        "seg_lengths": jax.vmap(lambda own: uneven(own, NSEG, SEQ, SEQ // 2, 1))(jax.random.split(seeds[2], SEQS)).reshape((SEQS, NSEG)).astype(jnp.int32),
        "pad_counts": plant(jax.random.randint(seeds[3], (SEQS,), 0, SEQ // 8 + 1), jax.random.fold_in(seeds[3], 1), 0, (SEQ // 8 + 1) - 1).astype(jnp.int32),
        "qkv_weight": scatter_about(seeds[4], (3, D, D), (D // 2) ** -0.5, 0.3125, ((1, 16), (2, 2)), jnp.float32),
        "first_qkv": scatter_about(seeds[5], (3, D, D), (0.1111 / (4 * D * D + 2 * D * FF) ** 0.5), 0.00024414062, ((1, 16), (2, 2)), jnp.float32),
        "second_qkv": jnp.clip(jnp.exp(math.log(2.9740510498754702e-08) - 1.38676955 * jax.random.uniform(seeds[6], (3, D, D), jnp.float32) ** block_levels(seeds[6], (3, D, D), ((1, 16), (2, 2)), -0.2, 0.2)), 7.431595339113528e-09, 2.9740510498754702e-08),
        "average_qkv": scatter_about(seeds[7], (3, D, D), (D // 2) ** -0.5, 0.3125, ((1, 16), (2, 2)), jnp.float32),
        "attn_weight": scatter_about(seeds[8], (D, D), (D // 8) ** -0.5, 0.625, ((0, 32),), jnp.float32),
        "first_attn": scatter_about(seeds[9], (D, D), (0.1111 / (4 * D * D + 2 * D * FF) ** 0.5), 0.00024414062, ((0, 32),), jnp.float32),
        "second_attn": jnp.clip(jnp.exp(math.log(2.9740510498754702e-08) - 1.38676955 * jax.random.uniform(seeds[10], (D, D), jnp.float32) ** block_levels(seeds[10], (D, D), ((0, 32),), -0.2, 0.2)), 7.431595339113528e-09, 2.9740510498754702e-08),
        "average_attn": scatter_about(seeds[11], (D, D), (D // 8) ** -0.5, 0.625, ((0, 32),), jnp.float32),
        "up_weight": scatter_about(seeds[12], (D, FF), D ** -0.5, 0.21875, ((0, 16), (1, 2)), jnp.float32),
        "first_up": scatter_about(seeds[13], (D, FF), (0.1111 / (4 * D * D + 2 * D * FF) ** 0.5), 0.00024414062, ((0, 16), (1, 2)), jnp.float32),
        "second_up": jnp.clip(jnp.exp(math.log(2.9740510498754702e-08) - 1.38676955 * jax.random.uniform(seeds[14], (D, FF), jnp.float32) ** block_levels(seeds[14], (D, FF), ((0, 16), (1, 2)), -0.2, 0.2)), 7.431595339113528e-09, 2.9740510498754702e-08),
        "average_up": scatter_about(seeds[15], (D, FF), D ** -0.5, 0.21875, ((0, 16), (1, 2)), jnp.float32),
        "down_weight": scatter_about(seeds[16], (FF, D), FF ** -0.5, 0.109375, ((0, 32),), jnp.float32),
        "first_down": scatter_about(seeds[17], (FF, D), (0.1111 / (4 * D * D + 2 * D * FF) ** 0.5), 0.00024414062, ((0, 32),), jnp.float32),
        "second_down": jnp.clip(jnp.exp(math.log(2.9740510498754702e-08) - 1.38676955 * jax.random.uniform(seeds[18], (FF, D), jnp.float32) ** block_levels(seeds[18], (FF, D), ((0, 32),), -0.2, 0.2)), 7.431595339113528e-09, 2.9740510498754702e-08),
        "average_down": scatter_about(seeds[19], (FF, D), FF ** -0.5, 0.109375, ((0, 32),), jnp.float32),
        "head_bias": scatter_about(seeds[20], (2, D), 0.3, 1.75, ((1, 32),), jnp.float32),
        "first_head": scatter_about(seeds[21], (2, D), (0.2222 / (4 * D * D + 2 * D * FF) ** 0.5), 0.00048828125, ((1, 32),), jnp.float32),
        "second_head": jnp.clip(jnp.exp(math.log(1.1896204199501881e-07) - 1.3862944 * jax.random.uniform(seeds[22], (2, D), jnp.float32) ** block_levels(seeds[22], (2, D), ((1, 32),), -0.2, 0.2)), 2.9740510498754702e-08, 1.1896204199501881e-07),
        "average_head": scatter_about(seeds[23], (2, D), 0.3, 1.75, ((1, 32),), jnp.float32),
        "hidden_bias": scatter_about(seeds[24], (FF,), 0.3, 1.75, ((0, 32),), jnp.float32),
        "first_hidden": scatter_about(seeds[25], (FF,), (0.0741 / (4 * D * D + 2 * D * FF) ** 0.5), 0.00015258789, ((0, 32),), jnp.float32),
        "second_hidden": jnp.clip(jnp.exp(math.log(1.3224283890167499e-08) - 1.3862944 * jax.random.uniform(seeds[26], (FF,), jnp.float32) ** block_levels(seeds[26], (FF,), ((0, 32),), -0.2, 0.2)), 3.3060709725418747e-09, 1.3224283890167499e-08),
        "average_hidden": scatter_about(seeds[27], (FF,), 0.3, 1.75, ((0, 32),), jnp.float32),
        "layer_vectors": draw_layer_vectors(jax.random.fold_in(seeds[32], 71), 0),
        "first_vectors": scatter_about(seeds[29], (6, D), (0.2222 / (4 * D * D + 2 * D * FF) ** 0.5), 0.00048828125, ((1, 16),), jnp.float32),
        "second_vectors": jnp.clip(jnp.exp(math.log(1.1896204199501881e-07) - 1.3862944 * jax.random.uniform(seeds[30], (6, D), jnp.float32) ** block_levels(seeds[30], (6, D), ((1, 16),), -0.2, 0.2)), 2.9740510498754702e-08, 1.1896204199501881e-07),
        "average_vectors": scatter_about(seeds[31], (6, D), 0.5, 3.0, ((1, 16),), jnp.float32),
    }


@jax.custom_vjp
def low(v):
    return lax.optimization_barrier(v.astype(jnp.bfloat16)).astype(jnp.float32)

@jax.custom_vjp
def low_back(v):
    return v

def low_keep(v):
    return (low(v), None)

def low_pass(kept, grad):
    return (grad,)

def back_keep(v):
    return (v, None)

def back_low(kept, grad):
    return (low(grad),)
low.defvjp(low_keep, low_pass)
low_back.defvjp(back_keep, back_low)
NORM_EPS = 1e-05
SCORE_SCALE = 0.125
LEARN_RATE = 0.03
VECTOR_RATE = 0.4
BETA_ONE = 0.9
BETA_TWO = 0.95
ADAM_EPS = 1e-08
WEIGHT_DECAY = 0.1
EMA_RATE = 0.8
CLIP_NORM = 1.0
GELU_COEF = 0.7978845608028654

def exact_dot(left, right):
    return jnp.dot(left, right, precision=lax.Precision.HIGHEST, preferred_element_type=jnp.float32)

def gelu_tanh(value):
    return 0.5 * value * (1.0 + jnp.tanh(GELU_COEF * (value + 0.044715 * value * value * value)))

def layer_norm(rows, gain, shift):
    row_mean = lax.optimization_barrier(jnp.mean(rows, axis=1, keepdims=True))
    centered = rows - row_mean
    row_var = lax.optimization_barrier(jnp.mean(centered * centered, axis=1, keepdims=True))
    return centered * lax.rsqrt(row_var + NORM_EPS) * gain + shift

def visible_keys(lengths, padding):
    position = jnp.arange(SEQ, dtype=jnp.int32)
    bounds = jnp.cumsum(lengths.astype(jnp.int32)).astype(jnp.int32)
    segment = lax.optimization_barrier(jnp.sum((position[:, None] >= bounds[None, :]).astype(jnp.int32), axis=1))
    padded = position >= SEQ - padding
    same_segment = segment[:, None] == segment[None, :]
    itself = position[:, None] == position[None, :]
    return same_segment & (jnp.logical_not(padded)[None, :] | itself)

def kept_rows(padding):
    position = jnp.arange(SEQ, dtype=jnp.int32)
    return (position < SEQ - padding).astype(jnp.float32)

def attend_one(packed):
    queries, key_rows, value_rows, allowed = packed
    scores = low_back(jnp.einsum('qhe,khe->hqk', queries, key_rows, precision=lax.Precision.HIGHEST) * SCORE_SCALE)
    scores = jnp.where(allowed[None, :, :], scores, -1e+30)
    row_max = lax.optimization_barrier(jnp.max(scores, axis=2, keepdims=True))
    exponent = jnp.exp(scores - row_max)
    probs = low(exponent / lax.optimization_barrier(jnp.sum(exponent, axis=2, keepdims=True)))
    mixed = jnp.einsum('hqk,khe->qhe', probs, value_rows, precision=lax.Precision.HIGHEST)
    return low(low_back(mixed))

def layer_forward(rows, params, allowed):
    qkv_mat, attn_mat, up_mat, down_mat, head_vec, hidden_vec, layer_vec = params
    first_in = low(layer_norm(rows, layer_vec[0], layer_vec[1]))
    queries = low(low_back(exact_dot(first_in, qkv_mat[0])) + head_vec[0])
    key_rows = low(low_back(exact_dot(first_in, qkv_mat[1])))
    value_rows = low(low_back(exact_dot(first_in, qkv_mat[2])) + head_vec[1])
    seq_count = rows.shape[0] // SEQ
    shaped = (seq_count, SEQ, H, HD)
    mixed = lax.map(jax.checkpoint(attend_one), (queries.reshape(shaped), key_rows.reshape(shaped), value_rows.reshape(shaped), allowed))
    mixed = mixed.reshape(rows.shape[0], D)
    hidden_one = rows + low_back(exact_dot(mixed, attn_mat)) + layer_vec[4]
    second_in = low(layer_norm(hidden_one, layer_vec[2], layer_vec[3]))
    activated = low(gelu_tanh(low_back(exact_dot(second_in, up_mat)) + hidden_vec))
    return hidden_one + low_back(exact_dot(activated, down_mat)) + layer_vec[5]

def adam_step(gradient, master, first, second, average, factor, decay_rate, step_rate):
    clipped = gradient * factor
    first_new = BETA_ONE * first + (1.0 - BETA_ONE) * clipped
    second_new = BETA_TWO * second + (1.0 - BETA_TWO) * clipped * clipped
    first_hat = first_new / (1.0 - BETA_ONE ** STEP)
    second_hat = second_new / (1.0 - BETA_TWO ** STEP)
    master_new = master - step_rate * (first_hat / (jnp.sqrt(second_hat) + ADAM_EPS) + decay_rate * master)
    average_new = EMA_RATE * average + (1.0 - EMA_RATE) * master_new
    return (first_new, second_new, master_new, average_new)

def reference(tokens, cotangent, seg_lengths, pad_counts, qkv_weight, first_qkv, second_qkv, average_qkv, attn_weight, first_attn, second_attn, average_attn, up_weight, first_up, second_up, average_up, down_weight, first_down, second_down, average_down, head_bias, first_head, second_head, average_head, hidden_bias, first_hidden, second_hidden, average_hidden, layer_vectors, first_vectors, second_vectors, average_vectors):
    masters = (qkv_weight, attn_weight, up_weight, down_weight, head_bias, hidden_bias, layer_vectors)
    rounded = tuple((low(master) for master in masters))
    seq_count = tokens.shape[0] // SEQ
    group_size = 8 if seq_count % 8 == 0 else 1
    group_count = seq_count // group_size
    rows_all = tokens.astype(jnp.float32).reshape(group_count, group_size * SEQ, D)
    cot_all = cotangent.astype(jnp.float32).reshape(group_count, group_size * SEQ, D)
    length_all = seg_lengths.reshape(group_count, group_size, NSEG)
    padding_all = pad_counts.reshape(group_count, group_size)

    def one_group(totals, inputs):
        group_rows, cot_rows, lengths, padding = inputs
        allowed = jax.vmap(visible_keys)(lengths, padding)
        kept = jax.vmap(kept_rows)(padding).reshape(-1)

        def apply_layer(row_in, *params):
            return layer_forward(row_in, params, allowed)
        output, pullback = jax.vjp(apply_layer, group_rows, *rounded)
        gradients = pullback(cot_rows * kept[:, None])
        summed = tuple((prior + gradient for prior, gradient in zip(totals, gradients[1:])))
        return (summed, (output, gradients[0]))
    zeros = tuple((jnp.zeros(master.shape, jnp.float32) for master in masters))
    totals, (outputs, input_grads) = lax.scan(one_group, zeros, (rows_all, cot_all, length_all, padding_all))
    squares = sum((jnp.sum(gradient * gradient) for gradient in totals))
    grad_norm = jnp.sqrt(squares)
    factor = CLIP_NORM / jnp.maximum(grad_norm, CLIP_NORM)
    moment_qkv, square_qkv, updated_qkv, smooth_qkv = adam_step(totals[0], qkv_weight, first_qkv, second_qkv, average_qkv, factor, WEIGHT_DECAY, LEARN_RATE)
    moment_attn, square_attn, updated_attn, smooth_attn = adam_step(totals[1], attn_weight, first_attn, second_attn, average_attn, factor, WEIGHT_DECAY, LEARN_RATE)
    moment_up, square_up, updated_up, smooth_up = adam_step(totals[2], up_weight, first_up, second_up, average_up, factor, WEIGHT_DECAY, LEARN_RATE)
    moment_down, square_down, updated_down, smooth_down = adam_step(totals[3], down_weight, first_down, second_down, average_down, factor, WEIGHT_DECAY, LEARN_RATE)
    moment_head, square_head, updated_head, smooth_head = adam_step(totals[4], head_bias, first_head, second_head, average_head, factor, 0.0, VECTOR_RATE)
    moment_hidden, square_hidden, updated_hidden, smooth_hidden = adam_step(totals[5], hidden_bias, first_hidden, second_hidden, average_hidden, factor, 0.0, VECTOR_RATE)
    moment_vectors, square_vectors, updated_vectors, smooth_vectors = adam_step(totals[6], layer_vectors, first_vectors, second_vectors, average_vectors, factor, 0.0, VECTOR_RATE)
    layer_output = outputs.reshape(-1, D).astype(jnp.bfloat16)
    input_grad = input_grads.reshape(-1, D)
    return (layer_output, input_grad, grad_norm, moment_qkv, square_qkv, updated_qkv, smooth_qkv, moment_attn, square_attn, updated_attn, smooth_attn, moment_up, square_up, updated_up, smooth_up, moment_down, square_down, updated_down, smooth_down, moment_head, square_head, updated_head, smooth_head, moment_hidden, square_hidden, updated_hidden, smooth_hidden, moment_vectors, square_vectors, updated_vectors, smooth_vectors)
```

```python
import functools

import jax
import jax.numpy as jnp
from jax import lax
from jax.experimental import pallas as pl
from jax.experimental.pallas import tpu as pltpu
from jax.sharding import PartitionSpec as P

HD = 64
PAIR = 128
SEQ = 512
D = 768
HALF = 384
STEP = 7
SMALL = 32

NORM_EPS = 1e-05
SCORE_SCALE = 0.125
LEARN_RATE = 0.03
VECTOR_RATE = 0.4
BETA_ONE = 0.9
BETA_TWO = 0.95
ADAM_EPS = 1e-08
WEIGHT_DECAY = 0.1
EMA_RATE = 0.8
CLIP_NORM = 1.0
GELU_COEF = 0.7978845608028654
GELU_CUBE = 0.044715
MASKED = -1e30

BF = jnp.bfloat16
F32 = jnp.float32
BOTH = ("dp", "mp")


def dot_nn(left, right):
    return lax.dot_general(left, right, (((1,), (0,)), ((), ())), preferred_element_type=F32)


def dot_nt(left, right):
    return lax.dot_general(left, right, (((1,), (1,)), ((), ())), preferred_element_type=F32)


def dot_tn(left, right):
    return lax.dot_general(left, right, (((0,), (0,)), ((), ())), preferred_element_type=F32)


def norm_parts(rows):
    row_mean = jnp.mean(rows, axis=1, keepdims=True)
    centered = rows - row_mean
    inv_std = lax.rsqrt(jnp.mean(centered * centered, axis=1, keepdims=True) + NORM_EPS)
    return (centered * inv_std, inv_std)


def norm_back(grad_in, normed, inv_std, gain):
    scaled = grad_in * gain
    return inv_std * (
        scaled
        - jnp.mean(scaled, axis=1, keepdims=True)
        - normed * jnp.mean(scaled * normed, axis=1, keepdims=True)
    )


def column_sum(value):
    return jnp.sum(value, axis=0, keepdims=True)


def step_bits(count):
    length = count.bit_length() - 1
    high = [(bit, bit) for bit in range(2, length)]
    return high + [(0, 1), (1, 0)]


def step_pairs(count, bits):
    return [
        (index * 2 + core, (index ^ (1 << bits[core])) * 2 + core)
        for index in range(count)
        for core in range(2)
    ]


def slots(count, here, core):
    length = count.bit_length() - 1
    apart = jnp.arange(count, dtype=jnp.int32) ^ here
    low, mid = apart & 1, (apart >> 1) & 1
    first = jnp.where(core == 0, mid, low)
    second = jnp.where(core == 0, low, mid)
    return (first << (length - 1)) | (second << (length - 2)) | (apart >> 2)


def reorder(value, pick):
    flat = dot_nn(pick, value.reshape(value.shape[0], -1)).astype(BF)
    return flat.reshape(value.shape)


def swap_cores(value):
    return lax.ppermute(value, "mp", [(0, 1), (1, 0)])


def gather_pieces(piece, count):
    held = piece[None]
    for bits in step_bits(count):
        got = lax.ppermute(held, BOTH, step_pairs(count, bits))
        held = jnp.concatenate([held, got], axis=0)
    return held


def reduce_pieces(own, other, count):
    got = swap_cores(other)
    half = count // 2
    held_low = own[:half].astype(F32) + got[:half].astype(F32)
    sent = (own[half:].astype(F32) + got[half:].astype(F32)).astype(BF)
    for bits in reversed(step_bits(count)):
        got = lax.ppermute(sent, BOTH, step_pairs(count, bits)).astype(F32)
        total = held_low + got
        half = half // 2
        if half:
            held_low = total[:half]
            sent = total[half:].astype(BF)
    return total[0]


def place_blocks(slot_ref, source, half, rows, qkv, stage, sem, count):
    def one(index, carry):
        src = source.at[slot_ref[half, index]]
        down = pl.ds(pl.multiple_of(index * rows, 16), rows)
        for kind in range(3):
            pltpu.make_async_copy(
                src.at[kind * rows : (kind + 1) * rows], qkv.at[half, kind, down], sem.at[half, 0]
            ).start()
        pltpu.make_async_copy(
            src.at[3 * rows : 4 * rows], stage.at[half, index], sem.at[half, 1]
        ).start()
        return carry

    lax.fori_loop(0, count, one, 0)


def wait_qkv(half, qkv, sem):
    pltpu.make_async_copy(qkv.at[half], qkv.at[half], sem.at[half, 0]).wait()


def wait_attn(half, stage, attn, sem):
    pltpu.make_async_copy(stage.at[half], stage.at[half], sem.at[half, 1]).wait()
    count, rows = stage.shape[1], stage.shape[2]
    part = rows // 2
    for index in range(0, count, 2):
        two = [stage[half, index + k].astype(F32) for k in range(2)]
        at = slice(index * part, (index + 2) * part)
        attn[half, at, :HALF] = jnp.concatenate([one[:part] for one in two], axis=0).astype(BF)
        attn[half, at, HALF:] = jnp.concatenate([one[part:] for one in two], axis=0).astype(BF)


def visible_bias(row_code, key_code):
    key_at = lax.broadcasted_iota(jnp.int32, (SEQ, SEQ), 0)
    row_at = lax.broadcasted_iota(jnp.int32, (SEQ, SEQ), 1)
    return jnp.where((key_code == row_code) | (key_at == row_at), 0.0, MASKED)


def front_kernel(
    placed, count, rows, slot_ref, core_ref, tokens, vectors, heads, row_code, key_code, *rest
):
    if placed:
        qkv, attn = rest[0], rest[1]
        outs, scratch = rest[2:9], rest[9:]
    else:
        own, other = rest[0], rest[1]
        outs, scratch = rest[2:9], rest[9:]
        qkv, attn, stage, sem = scratch[1:5]
    bias = scratch[0]
    first_in, proj, log_total, mixed, hidden_one, second_in, gain = outs
    if not placed:
        place_blocks(slot_ref, own, 0, rows, qkv, stage, sem, count)
        place_blocks(slot_ref, other, 1, rows, qkv, stage, sem, count)
    bias[...] = visible_bias(row_code[...], key_code[...])
    x = tokens[...].astype(F32)
    normed, _ = norm_parts(x)
    first_in[...] = (normed * vectors[0:1, :] + vectors[1:2, :]).astype(BF)
    for half in range(2):
        if not placed:
            wait_qkv(half, qkv, sem)
        value = dot_nn(first_in[...], qkv[half, 0]) + heads[half, 0:1, :]
        proj[half, 0] = (value.astype(BF).astype(F32) * SCORE_SCALE).astype(BF)
        proj[half, 1] = dot_nn(first_in[...], qkv[half, 1]).astype(BF)
        value = dot_nn(first_in[...], qkv[half, 2]) + heads[half, 1:2, :]
        proj[half, 2] = value.astype(BF)
    lane = lax.broadcasted_iota(jnp.int32, (SEQ, PAIR), 1)
    for half in range(2):
        for pair in range(HALF // PAIR):
            at = slice(pair * PAIR, (pair + 1) * PAIR)
            q_pair, k_pair, v_pair = proj[half, 0, :, at], proj[half, 1, :, at], proj[half, 2, :, at]
            v_turned = v_pair.T
            turned = []
            for side in range(2):
                mine = (lane < HD) if side == 0 else (lane >= HD)
                q_side = jnp.where(mine, q_pair, jnp.zeros_like(q_pair))
                scores = dot_nt(k_pair, q_side) + bias[...]
                top = jnp.max(scores, axis=0, keepdims=True)
                exponent = jnp.exp(scores - top)
                total = jnp.sum(exponent, axis=0, keepdims=True)
                index = half * (HALF // HD) + pair * 2 + side
                log_total[index : index + 1, :] = top + jnp.log(total)
                part = dot_nn(v_turned[side * HD : (side + 1) * HD], exponent.astype(BF))
                turned.append(part * (1.0 / total))
            both = jnp.concatenate(turned, axis=0).T
            mixed[:, half * HALF + pair * PAIR : half * HALF + (pair + 1) * PAIR] = both.astype(BF)
    if not placed:
        wait_attn(0, stage, attn, sem)
        wait_attn(1, stage, attn, sem)
    value = dot_nn(mixed[:, :HALF], attn[0]) + dot_nn(mixed[:, HALF:], attn[1])
    hidden = x + value + vectors[4:5, :]
    hidden_one[...] = hidden
    normed, _ = norm_parts(hidden)
    second_in[...] = (normed * vectors[2:3, :] + vectors[3:4, :]).astype(BF)


def middle_kernel(
    aligned,
    count,
    slot_ref,
    core_ref,
    pads_ref,
    second_in,
    hidden_one,
    cotangent,
    vectors,
    bias,
    up,
    down,
    layer_output,
    grad_second,
    grad_hidden,
    up_own,
    up_other,
    down_own,
    down_other,
    out_sum,
    low_grad,
    turned_in,
    act,
    pre_low,
):
    step = pl.program_id(0)

    @pl.when(step == 0)
    def _():
        position = lax.broadcasted_iota(jnp.int32, (SEQ, D), 0)
        kept = position < SEQ - pads_ref[core_ref[0]]
        low_grad[...] = jnp.where(kept, cotangent[...].astype(F32), 0.0).astype(BF)
        out_sum[...] = hidden_one[...] + vectors[5:6, :]
        grad_second[...] = jnp.zeros_like(grad_second)
        turned_in[...] = second_in[...].T

    rows = 256
    sums = jnp.zeros((1, D), F32)
    for chunk in range(SEQ // rows):
        at = slice(chunk * rows, (chunk + 1) * rows)
        pre = dot_nn(second_in[at, :], up[0]) + bias[0]
        square = pre * pre
        bent = jnp.tanh(GELU_COEF * (pre + GELU_CUBE * square * pre))
        half_up = 0.5 + 0.5 * bent
        act[at, :] = (pre * half_up).astype(BF)
        slope = half_up + 0.5 * pre * (1.0 - bent * bent) * (
            GELU_COEF * (1.0 + 3.0 * GELU_CUBE * square)
        )
        grad_pre = dot_nt(low_grad[at, :], down[0]) * slope
        sums = sums + column_sum(grad_pre)
        pre_low[at, :] = grad_pre.astype(BF)
    grad_hidden[0] = sums
    out_sum[...] += dot_nn(act[...], down[0])
    grad_second[...] += dot_nt(pre_low[...], up[0])
    grad_down = dot_tn(act[...], low_grad[...]).astype(BF)
    grad_up = dot_nn(turned_in[...], pre_low[...]).astype(BF)
    up_rows = D // count
    down_rows = 2 * up_rows
    for half, up_out, down_out in ((1, up_other, down_other), (0, up_own, down_own)):
        for part in range(2):

            @pl.when(step == (1 - half) * 2 + part)
            def _(half=half, part=part, up_out=up_out, down_out=down_out):
                if aligned:
                    for index in range(count):
                        up_out[slot_ref[half, index], part * up_rows : (part + 1) * up_rows, :] = (
                            grad_up[index * up_rows : (index + 1) * up_rows, :]
                        )
                    for index in range(count // 2):
                        down_out[slot_ref[half, part * (count // 2) + index]] = grad_down[
                            index * down_rows : (index + 1) * down_rows, :
                        ]
                else:
                    up_out[part] = grad_up
                    down_out[part] = grad_down

    @pl.when(step == 3)
    def _():
        layer_output[...] = out_sum[...].astype(BF)


def back_kernel(
    placed,
    count,
    rows,
    slot_ref,
    core_ref,
    pads_ref,
    tokens,
    cotangent,
    vectors,
    row_code,
    key_code,
    grad_second,
    hidden_one,
    grad_hidden,
    first_in,
    proj,
    log_total,
    mixed,
    *rest,
):
    if placed:
        qkv, attn = rest[0], rest[1]
        outs, scratch = rest[2:], rest[-3:]
        input_grad, qkv_grad, attn_grad, small_own, small_other = outs[:5]
    else:
        own, other = rest[0], rest[1]
        outs, scratch = rest[2:], rest[-7:-4]
        qkv, attn, stage, sem = rest[-4:]
        input_grad, out_own, out_other = outs[:3]
    bias, proj_low, turned_first = scratch
    if not placed:
        place_blocks(slot_ref, own, 0, rows, qkv, stage, sem, count)
        place_blocks(slot_ref, other, 1, rows, qkv, stage, sem, count)
    bias[...] = visible_bias(row_code[...], key_code[...])
    turned_first[...] = first_in[...].T
    position = lax.broadcasted_iota(jnp.int32, (SEQ, D), 0)
    kept = position < SEQ - pads_ref[core_ref[0]]
    grad_out = jnp.where(kept, cotangent[...].astype(F32), 0.0)
    normed, inv_std = norm_parts(hidden_one[...])
    grads = grad_second[...]
    gain_two, shift_two = column_sum(grads * normed), column_sum(grads)
    grad_one = grad_out + norm_back(grads, normed, inv_std, vectors[2:3, :])
    input_grad[...] = grad_one
    shift_attn, shift_down = column_sum(grad_one), column_sum(grad_out)
    grad_low = grad_one.astype(BF)
    if not placed:
        for half in range(2):
            wait_qkv(half, qkv, sem)
            wait_attn(half, stage, attn, sem)
    part_rows = rows // 2
    lane = lax.broadcasted_iota(jnp.int32, (SEQ, PAIR), 1)
    head_grads = []
    for half in range(2):
        columns = slice(half * HALF, (half + 1) * HALF)
        grad_attn = dot_tn(mixed[:, columns], grad_low)
        if placed:
            attn_grad[half] = grad_attn.astype(BF)
        else:
            out = (out_own, out_other)[half]
            for index in range(count):
                piece = grad_attn[index * part_rows : (index + 1) * part_rows, :]
                piece = jnp.concatenate([piece[:, :HALF], piece[:, HALF:]], axis=0)
                out[slot_ref[half, index], 3 * rows : 4 * rows, :] = piece.astype(BF)
        grad_mixed = dot_nt(grad_low, attn[half]).astype(BF)
        sums = [[], []]
        for pair in range(HALF // PAIR):
            at = slice(pair * PAIR, (pair + 1) * PAIR)
            q_pair, k_pair, v_pair = proj[half, 0, :, at], proj[half, 1, :, at], proj[half, 2, :, at]
            g_pair = grad_mixed[:, at]
            k_turned = k_pair.T
            grad_key = jnp.zeros((SEQ, PAIR), F32)
            grad_value = jnp.zeros((SEQ, PAIR), F32)
            turned = []
            for side in range(2):
                mine = (lane < HD) if side == 0 else (lane >= HD)
                q_side = jnp.where(mine, q_pair, jnp.zeros_like(q_pair))
                g_side = jnp.where(mine, g_pair, jnp.zeros_like(g_pair))
                index = half * (HALF // HD) + pair * 2 + side
                scores = dot_nt(k_pair, q_side) + bias[...]
                probs = jnp.exp(scores - log_total[index : index + 1, :])
                grad_probs = dot_nt(v_pair, g_side)
                row_dot = column_sum(probs * grad_probs)
                grad_scores = (probs * (grad_probs - row_dot)).astype(BF)
                grad_value = grad_value + dot_nn(probs.astype(BF), g_side)
                grad_key = grad_key + dot_nn(grad_scores, q_side)
                turned.append(dot_nn(k_turned[side * HD : (side + 1) * HD], grad_scores))
            grad_query = jnp.concatenate(turned, axis=0).T * SCORE_SCALE
            sums[0].append(column_sum(grad_query))
            sums[1].append(column_sum(grad_value))
            proj_low[half, 0, :, at] = grad_query.astype(BF)
            proj_low[half, 1, :, at] = grad_key.astype(BF)
            proj_low[half, 2, :, at] = grad_value.astype(BF)
        head_grads.append([jnp.concatenate(one, axis=1) for one in sums])
    grad_first = jnp.zeros((SEQ, D), F32)
    for half in range(2):
        for kind in range(3):
            grad_first = grad_first + dot_nt(proj_low[half, kind], qkv[half, kind])
            grad_qkv = dot_nn(turned_first[...], proj_low[half, kind]).astype(BF)
            if placed:
                qkv_grad[half, kind] = grad_qkv
            else:
                out = (out_own, out_other)[half]
                for index in range(count):
                    out[slot_ref[half, index], kind * rows : (kind + 1) * rows, :] = grad_qkv[
                        index * rows : (index + 1) * rows, :
                    ]
    normed, inv_std = norm_parts(tokens[...].astype(F32))
    gain_one, shift_one = column_sum(grad_first * normed), column_sum(grad_first)
    input_grad[...] += norm_back(grad_first, normed, inv_std, vectors[0:1, :])
    whole = (gain_one, shift_one, gain_two, shift_two, shift_attn, shift_down)
    for half in range(2):
        lines = [line[:, part * HALF : (part + 1) * HALF] for line in whole for part in range(2)]
        lines += head_grads[half]
        for block in range(2):
            line = grad_hidden[(1 - half) * 2 + block]
            lines += [line[:, :HALF], line[:, HALF:]]
        lines.append(jnp.zeros((SMALL - len(lines), HALF), F32))
        packed = jnp.concatenate(lines, axis=0).astype(BF)
        if placed:
            (small_own, small_other)[half][...] = packed
        else:
            out = (out_own, out_other)[half]
            for index in range(count):
                out[index, 4 * rows :, :] = packed


def adam_step(gradient, master, first, second, average, factor, decay_rate, step_rate):
    clipped = gradient * factor
    first_new = BETA_ONE * first + (1.0 - BETA_ONE) * clipped
    second_new = BETA_TWO * second + (1.0 - BETA_TWO) * clipped * clipped
    first_hat = first_new / (1.0 - BETA_ONE**STEP)
    second_hat = second_new / (1.0 - BETA_TWO**STEP)
    master_new = master - step_rate * (
        first_hat / (jnp.sqrt(second_hat) + ADAM_EPS) + decay_rate * master
    )
    average_new = EMA_RATE * average + (1.0 - EMA_RATE) * master_new
    return (first_new, second_new, master_new, average_new)


def vmem(*shapes):
    return [pltpu.VMEM(shape, dtype) for shape, dtype in shapes]


def params(mib):
    return pltpu.CompilerParams(vmem_limit_bytes=mib << 20)


def whole_spec(shape):
    return pl.BlockSpec(shape, lambda *_: (0,) * len(shape))


def core_spec(shape):
    return pl.BlockSpec(shape, lambda _, slot, core, *more: (core[0],) + (0,) * (len(shape) - 1))


def any_spec():
    return pl.BlockSpec(memory_space=pl.ANY)


def both_halves(own, core):
    other = swap_cores(own)
    first = jnp.where(core == 0, own, other)
    second = jnp.where(core == 0, other, own)
    return jnp.concatenate([first, second], axis=0)


def body(force_plain, *args):
    (tokens, cotangent, seg_lengths, pad_counts) = args[:4]
    groups = [args[4 + 4 * i : 8 + 4 * i] for i in range(7)]
    qkv_w, attn_w, up_w, down_w, head_w, hidden_w, vector_w = (group[0] for group in groups)
    rows = qkv_w.shape[1]
    count = D // rows
    aligned = rows % 16 == 0 and not force_plain
    here, core = lax.axis_index("dp"), lax.axis_index("mp")
    slot = jnp.stack([slots(count, here, core), slots(count, here, 1 - core)], axis=0)
    core_at = core.reshape(1).astype(jnp.int32)

    wide = up_w.shape[1] // 2
    flat = jnp.concatenate(
        [
            up_w[:, :wide].astype(BF),
            up_w[:, wide:].astype(BF),
            down_w.astype(BF),
        ],
        axis=0,
    )
    mine = lax.all_gather(flat, "dp", axis=0, tiled=True).reshape(count, 4 * rows, D)
    small = jnp.concatenate([head_w.reshape(-1), hidden_w, vector_w.reshape(-1)]).astype(BF)
    small_size = small.shape[0]
    small_rows = -(-small_size // HALF)
    small_rows = -(-small_rows // 16) * 16
    small = jnp.pad(small, (0, small_rows * HALF - small_size)).reshape(small_rows, HALF)
    piece = jnp.concatenate(
        [
            qkv_w.astype(BF).reshape(3 * rows, HALF),
            attn_w[:, :HALF].astype(BF),
            attn_w[:, HALF:].astype(BF),
            small,
        ],
        axis=0,
    )
    own = gather_pieces(piece, count)
    other = swap_cores(own)

    picks = [
        (slot[half][:, None] == jnp.arange(count, dtype=jnp.int32)[None, :]).astype(BF)
        for half in range(2)
    ]
    picked = [
        dot_nn(picks[half], held[:, 4 * rows :, :].reshape(count, -1)[:, :small_size])
        for half, held in ((0, own), (1, other))
    ]
    per_head = head_w.shape[1]
    heads = jnp.stack(
        [
            one[:, : 2 * per_head].reshape(count, 2, per_head).transpose(1, 0, 2).reshape(2, HALF)
            for one in picked
        ],
        axis=0,
    )
    per_hidden = hidden_w.shape[0]
    hidden = jnp.concatenate(
        [
            one[:, 2 * per_head : 2 * per_head + per_hidden].reshape(2, 1, D)
            for one in (picked[1], picked[0])
        ],
        axis=0,
    )
    vectors = (
        picked[0][:, 2 * per_head + per_hidden :]
        .reshape(count, 6, rows)
        .transpose(1, 0, 2)
        .reshape(6, D)
    )

    lengths = lax.dynamic_index_in_dim(seg_lengths, core, 0, keepdims=False)
    padding = lax.dynamic_index_in_dim(pad_counts, core, 0, keepdims=False)
    upto = jnp.arange(lengths.shape[0])[:, None] >= jnp.arange(lengths.shape[0])[None, :]
    bounds = jnp.sum(jnp.where(upto, lengths[None, :], 0), axis=1)
    position = jnp.arange(SEQ, dtype=jnp.int32)
    row_code = jnp.sum((position[None, :] >= bounds[:, None]).astype(jnp.int32), axis=0)[None, :]
    key_code = jnp.sum((position[:, None] >= bounds[None, :]).astype(jnp.int32), axis=1)[:, None]
    key_code = jnp.where(position[:, None] >= SEQ - padding, -1, key_code)

    if aligned:
        block_args = (own, other)
        block_specs = [any_spec(), any_spec()]
        block_scratch = vmem(
            ((2, 3, D, HALF), BF), ((2, HALF, D), BF), ((2, count, rows, HALF), BF)
        ) + [
            pltpu.SemaphoreType.DMA((2, 2))
        ]
    else:
        spread = [reorder(held, picks[half]) for half, held in ((0, own), (1, other))]
        qkv_all = jnp.stack(
            [
                one[:, : 3 * rows]
                .reshape(count, 3, rows, HALF)
                .transpose(1, 0, 2, 3)
                .reshape(3, D, HALF)
                for one in spread
            ],
            axis=0,
        )
        attn_all = jnp.stack(
            [
                one[:, 3 * rows : 4 * rows]
                .reshape(count, 2, rows // 2, HALF)
                .transpose(0, 2, 1, 3)
                .reshape(HALF, D)
                for one in spread
            ],
            axis=0,
        )
        block_args = (qkv_all, attn_all)
        block_specs = [whole_spec((2, 3, D, HALF)), whole_spec((2, HALF, D))]
        block_scratch = []

    def shape(dims, dtype):
        return jax.ShapeDtypeStruct(dims, dtype)

    front_outs = [
        shape((SEQ, D), BF),
        shape((2, 3, SEQ, HALF), BF),
        shape((2 * HALF // HD, SEQ), F32),
        shape((SEQ, D), BF),
        shape((SEQ, D), F32),
        shape((SEQ, D), BF),
        shape((8, 128), F32),
    ]
    first_in, proj, log_total, mixed, hidden_one, second_in, _ = pl.pallas_call(
        functools.partial(front_kernel, not aligned, count, rows),
        out_shape=front_outs,
        grid_spec=pltpu.PrefetchScalarGridSpec(
            num_scalar_prefetch=2,
            grid=(1,),
            in_specs=[
                core_spec((SEQ, D)),
                whole_spec((6, D)),
                whole_spec((2, 2, HALF)),
                whole_spec((1, SEQ)),
                whole_spec((SEQ, 1)),
            ]
            + block_specs,
            out_specs=[whole_spec(one.shape) for one in front_outs],
            scratch_shapes=vmem(((SEQ, SEQ), F32)) + block_scratch,
        ),
        compiler_params=params(48),
        cost_estimate=pl.CostEstimate(
            flops=6_000_000_000, bytes_accessed=12_000_000, transcendentals=3_200_000
        ),
        name="front",
    )(slot, core_at, tokens, vectors, heads, row_code, key_code, *block_args)

    theirs = swap_cores(mine)
    up_all = jnp.concatenate(
        [
            one[:, : 2 * rows].reshape(count, 2, rows, D).transpose(1, 0, 2, 3).reshape(2, D, D)
            for one in (theirs, mine)
        ],
        axis=0,
    )
    down_all = jnp.concatenate(
        [one[:, 2 * rows :].reshape(2, D, D) for one in (theirs, mine)], axis=0
    )
    if aligned:
        grad_outs = [shape((count, 2 * rows, D), BF) for _ in range(4)]
    else:
        grad_outs = [shape((2, D, D), BF) for _ in range(4)]
    middle_outs = [shape((SEQ, D), BF), shape((SEQ, D), F32), shape((4, 1, D), F32)] + grad_outs
    (layer_half, grad_second, grad_hidden, up_own, up_other, down_own, down_other) = pl.pallas_call(
        functools.partial(middle_kernel, aligned, count),
        out_shape=middle_outs,
        grid_spec=pltpu.PrefetchScalarGridSpec(
            num_scalar_prefetch=3,
            grid=(4,),
            in_specs=[
                whole_spec((SEQ, D)),
                whole_spec((SEQ, D)),
                core_spec((SEQ, D)),
                whole_spec((6, D)),
                pl.BlockSpec((1, 1, D), lambda i, *_: (i, 0, 0)),
                pl.BlockSpec((1, D, D), lambda i, *_: (i, 0, 0)),
                pl.BlockSpec((1, D, D), lambda i, *_: (i, 0, 0)),
            ],
            out_specs=[
                whole_spec((SEQ, D)),
                whole_spec((SEQ, D)),
                pl.BlockSpec((1, 1, D), lambda i, *_: (i, 0, 0)),
            ]
            + [whole_spec(one.shape) for one in grad_outs],
            scratch_shapes=vmem(
                ((SEQ, D), F32), ((SEQ, D), BF), ((D, SEQ), BF), ((SEQ, D), BF), ((SEQ, D), BF)
            ),
        ),
        compiler_params=params(56),
        cost_estimate=pl.CostEstimate(
            flops=14_500_000_000, bytes_accessed=24_000_000, transcendentals=1_600_000
        ),
        name="middle",
    )(slot, core_at, pad_counts, second_in, hidden_one, cotangent, vectors, hidden, up_all, down_all)
    layer_output = both_halves(layer_half, core)

    if aligned:
        back_outs = [shape((SEQ, D), F32)] + [shape((count, 4 * rows + SMALL, HALF), BF)] * 2
    else:
        back_outs = [
            shape((SEQ, D), F32),
            shape((2, 3, D, HALF), BF),
            shape((2, HALF, D), BF),
            shape((SMALL, HALF), BF),
            shape((SMALL, HALF), BF),
        ]
    done = pl.pallas_call(
        functools.partial(back_kernel, not aligned, count, rows),
        out_shape=back_outs,
        grid_spec=pltpu.PrefetchScalarGridSpec(
            num_scalar_prefetch=3,
            grid=(1,),
            in_specs=[
                core_spec((SEQ, D)),
                core_spec((SEQ, D)),
                whole_spec((6, D)),
                whole_spec((1, SEQ)),
                whole_spec((SEQ, 1)),
                whole_spec((SEQ, D)),
                whole_spec((SEQ, D)),
                whole_spec((4, 1, D)),
                whole_spec((SEQ, D)),
                whole_spec((2, 3, SEQ, HALF)),
                whole_spec((2 * HALF // HD, SEQ)),
                whole_spec((SEQ, D)),
            ]
            + block_specs,
            out_specs=[whole_spec(one.shape) for one in back_outs],
            scratch_shapes=vmem(
                ((SEQ, SEQ), F32), ((2, 3, SEQ, HALF), BF), ((D, SEQ), BF)
            )
            + block_scratch,
        ),
        compiler_params=params(56),
        cost_estimate=pl.CostEstimate(
            flops=10_000_000_000, bytes_accessed=24_000_000, transcendentals=3_200_000
        ),
        name="back",
    )(
        slot,
        core_at,
        pad_counts,
        tokens,
        cotangent,
        vectors,
        row_code,
        key_code,
        grad_second,
        hidden_one,
        grad_hidden,
        first_in,
        proj,
        log_total,
        mixed,
        *block_args,
    )
    input_grad = both_halves(done[0], core)

    if aligned:
        front_own, front_other = done[1], done[2]
    else:
        turned = [pick.T for pick in picks]

        def up_pieces(value, half):
            value = value.reshape(2, count, rows, D).transpose(1, 0, 2, 3).reshape(count, 2 * rows, D)
            return reorder(value, turned[half])

        def down_pieces(value, half):
            return reorder(value.reshape(count, 2 * rows, D), turned[half])

        up_own, up_other = up_pieces(up_own, 0), up_pieces(up_other, 1)
        down_own, down_other = down_pieces(down_own, 0), down_pieces(down_other, 1)
        sent = []
        for half in range(2):
            qkv_part = (
                done[1][half]
                .reshape(3, count, rows, HALF)
                .transpose(1, 0, 2, 3)
                .reshape(count, 3 * rows, HALF)
            )
            attn_part = (
                done[2][half]
                .reshape(count, rows // 2, 2, HALF)
                .transpose(0, 2, 1, 3)
                .reshape(count, rows, HALF)
            )
            small_part = jnp.broadcast_to(done[3 + half][None], (count, SMALL, HALF))
            sent.append(
                reorder(jnp.concatenate([qkv_part, attn_part, small_part], axis=1), turned[half])
            )
        front_own, front_other = sent
    total_down = reduce_pieces(down_own, down_other, count)
    total_up = reduce_pieces(up_own, up_other, count)
    total = reduce_pieces(front_own, front_other, count)
    tail = total[4 * rows :]
    reduced = (
        total[: 3 * rows].reshape(3, rows, HALF),
        jnp.concatenate([total[3 * rows : 3 * rows + rows // 2], total[3 * rows + rows // 2 : 4 * rows]], axis=1),
        jnp.concatenate([total_up[:rows], total_up[rows:]], axis=1),
        total_down,
        lax.dynamic_slice_in_dim(tail[12:14], here * per_head, per_head, 1),
        lax.dynamic_slice_in_dim(tail[14:18].reshape(-1), here * per_hidden, per_hidden, 0),
        lax.dynamic_slice_in_dim(tail[:12].reshape(6, D), here * rows, rows, 1),
    )
    squares = sum(jnp.sum(member * member) for member in reduced[:6]) + 0.5 * jnp.sum(
        reduced[6] * reduced[6]
    )
    spread = lax.all_to_all(
        jnp.broadcast_to(squares, (2 * count, 8, 128)), BOTH, 0, 0, tiled=True
    )
    grad_norm = jnp.sqrt(jnp.sum(spread[:, 0, 0]))
    factor = CLIP_NORM / jnp.maximum(grad_norm, CLIP_NORM)
    results = [layer_output, input_grad, grad_norm]
    for index, group in enumerate(groups):
        decay, rate = (WEIGHT_DECAY, LEARN_RATE) if index < 4 else (0.0, VECTOR_RATE)
        results += adam_step(reduced[index], *group, factor, decay, rate)
    return tuple(results)


FORCE_PLAIN = False


def solution(mesh):
    row, late, wide = P("dp", None), P(("mp", "dp"), None), P("dp", "mp")
    kinds = (
        P(None, "dp", "mp"),
        late,
        wide,
        late,
        P(None, ("mp", "dp")),
        P(("mp", "dp")),
        P(None, "dp"),
    )
    per_parameter = tuple(kind for kind in kinds for _ in range(4))
    return jax.shard_map(
        functools.partial(body, FORCE_PLAIN),
        mesh=mesh,
        in_specs=(row, row, row, P("dp")) + per_parameter,
        out_specs=(row, row, P()) + per_parameter,
        check_vma=False,
    )
```

```python
import functools

import jax
import jax.numpy as jnp
from jax import lax
from jax.experimental import pallas as pl
from jax.experimental.pallas import tpu as pltpu
from jax.sharding import PartitionSpec as P

HD = 64
PAIR = 128
SEQ = 512
D = 768
HALF = 384
STEP = 7
SMALL = 32

NORM_EPS = 1e-05
SCORE_SCALE = 0.125
LEARN_RATE = 0.03
VECTOR_RATE = 0.4
BETA_ONE = 0.9
BETA_TWO = 0.95
ADAM_EPS = 1e-08
WEIGHT_DECAY = 0.1
EMA_RATE = 0.8
CLIP_NORM = 1.0
GELU_COEF = 0.7978845608028654
GELU_CUBE = 0.044715
MASKED = -1e30

BF = jnp.bfloat16
F32 = jnp.float32
BOTH = ("dp", "mp")


def dot_nn(left, right):
    return lax.dot_general(left, right, (((1,), (0,)), ((), ())), preferred_element_type=F32)


def dot_nt(left, right):
    return lax.dot_general(left, right, (((1,), (1,)), ((), ())), preferred_element_type=F32)


def dot_tn(left, right):
    return lax.dot_general(left, right, (((0,), (0,)), ((), ())), preferred_element_type=F32)


def norm_parts(rows):
    row_mean = jnp.mean(rows, axis=1, keepdims=True)
    centered = rows - row_mean
    inv_std = lax.rsqrt(jnp.mean(centered * centered, axis=1, keepdims=True) + NORM_EPS)
    return (centered * inv_std, inv_std)


def norm_back(grad_in, normed, inv_std, gain):
    scaled = grad_in * gain
    return inv_std * (
        scaled
        - jnp.mean(scaled, axis=1, keepdims=True)
        - normed * jnp.mean(scaled * normed, axis=1, keepdims=True)
    )


def column_sum(value):
    return jnp.sum(value, axis=0, keepdims=True)


def step_bits(count):
    length = count.bit_length() - 1
    high = [(bit, bit) for bit in reversed(range(2, length))]
    return high + [(0, 1), (1, 0)]


def step_pairs(count, bits):
    return [
        (index * 2 + core, (index ^ (1 << bits[core])) * 2 + core)
        for index in range(count)
        for core in range(2)
    ]


def slots(count, here, core):
    length = count.bit_length() - 1
    apart = jnp.arange(count, dtype=jnp.int32) ^ here
    low, mid = apart & 1, (apart >> 1) & 1
    first = jnp.where(core == 0, mid, low)
    second = jnp.where(core == 0, low, mid)
    place = (first << (length - 1)) | (second << (length - 2))
    for bit in range(2, length):
        place = place | (((apart >> bit) & 1) << (length - 1 - bit))
    return place


def reorder(value, pick):
    flat = dot_nn(pick, value.reshape(value.shape[0], -1)).astype(BF)
    return flat.reshape(value.shape)


def swap_cores(value):
    return lax.ppermute(value, "mp", [(0, 1), (1, 0)])


def after(value, *others):
    return lax.optimization_barrier((value,) + others)[0]


def join(made, *gots):
    joined = lax.optimization_barrier(tuple(made) + gots)
    return (list(joined[: len(made)]), *joined[len(made) :])


class Gatherer:
    def __init__(self, piece, count):
        self.count, self.held, self.got = count, piece[None], None
        self.bits = step_bits(count)

    def send(self, *others):
        if others:
            self.held = after(self.held, *others)
        return lax.ppermute(self.held, BOTH, step_pairs(self.count, self.bits.pop(0)))

    def take(self, got):
        if self.bits:
            self.held = jnp.concatenate([self.held, got], axis=0)
        else:
            self.got = got

    def parts(self):
        return (self.held, self.got, swap_cores(self.held), swap_cores(self.got))


class Reducer:
    def __init__(self, own, other, count):
        self.count, self.half = count, count // 2
        self.bits = list(reversed(step_bits(count)))
        got = swap_cores(other)
        half = self.half
        self.kept = own[:half].astype(F32) + got[:half].astype(F32)
        self.sent = (own[half:].astype(F32) + got[half:].astype(F32)).astype(BF)

    def send(self):
        return lax.ppermute(self.sent, BOTH, step_pairs(self.count, self.bits.pop(0)))

    def take(self, got):
        self.half //= 2
        total = self.kept + got.astype(F32)
        self.kept, self.sent = total[: self.half], total[self.half :].astype(BF)

    def finish(self):
        while len(self.bits) > 1:
            self.take(self.send())
        return (self.kept[0], self.send()[0])


def fetch(slot, held, got, send):
    half = held.shape[0]

    @pl.when(slot < half)
    def _():
        send(held.at[slot])

    @pl.when(slot >= half)
    def _():
        send(got.at[slot - half])


def drain(ref, sem):
    pltpu.make_async_copy(ref, ref, sem).wait()


def visible_bias(row_code, key_code):
    key_at = lax.broadcasted_iota(jnp.int32, (SEQ, SEQ), 0)
    row_at = lax.broadcasted_iota(jnp.int32, (SEQ, SEQ), 1)
    return jnp.where((key_code == row_code) | (key_at == row_at), 0.0, MASKED)


def pack_kernel(qkv_w, attn_w, up_w, down_w, head_w, hidden_w, vector_w, piece, up, down, small):
    rows = qkv_w.shape[1]
    part = rows // 2
    for kind in range(3):
        piece[kind * rows : (kind + 1) * rows, :] = qkv_w[kind].astype(BF)
    both = jnp.concatenate([attn_w[:, :HALF], attn_w[:, HALF:]], axis=0)
    piece[3 * rows : 3 * rows + 2 * part, :] = both.astype(BF)
    small[...] = jnp.zeros_like(small)
    small[0:6, :rows] = vector_w[...]
    small[6:8, :part] = head_w[...]
    small[8:9, : 2 * rows] = hidden_w[...]
    piece[4 * rows :, :] = small[...].astype(BF)
    up[:rows, :] = up_w[:, :D].astype(BF)
    up[rows:, :] = up_w[:, D:].astype(BF)
    down[...] = down_w[...].astype(BF)


def front_kernel(placed, count, rows, slot_ref, core_ref, tokens, row_code, key_code, *rest):
    if placed:
        vectors, heads, qkv, attn = rest[:4]
        outs, scratch = rest[4:10], rest[10:]
    else:
        parts = rest[:4]
        outs, scratch = rest[4:10], rest[15:]
        vectors, heads, hidden, qkv_out, attn_out = rest[10:15]
        qkv, attn, stage, sem = scratch[1:]
    bias = scratch[0]
    first_in, proj, log_total, mixed, hidden_one, second_in = outs
    if not placed:

        def place(index, carry):
            for half in range(2):
                down = pl.ds(pl.multiple_of(index * rows, 16), rows)

                def send(src, half=half, down=down):
                    for kind in range(3):
                        pltpu.make_async_copy(
                            src.at[kind * rows : (kind + 1) * rows],
                            qkv.at[half, kind, down],
                            sem.at[half],
                        ).start()
                    pltpu.make_async_copy(
                        src.at[3 * rows :], stage.at[half, index], sem.at[2 + half]
                    ).start()

                fetch(slot_ref[half, index], parts[2 * half], parts[2 * half + 1], send)
            return carry

        lax.fori_loop(0, count, place, 0)
    bias[...] = visible_bias(row_code[...], key_code[...])
    x = tokens[...].astype(F32)
    normed, _ = norm_parts(x)
    if not placed:
        part = rows // 2
        drain(stage.at[0], sem.at[2])
        drain(stage.at[1], sem.at[3])
        for half in range(2):
            for index in range(count):
                tail = stage[half, index, rows:, :].astype(F32)
                if half == 0:
                    vectors[0:6, index * rows : (index + 1) * rows] = tail[0:6, :rows]
                heads[half, :, index * part : (index + 1) * part] = tail[6:8, :part]
                block = (1 - half) * 2 + index // (count // 2)
                start = (index % (count // 2)) * 2 * rows
                hidden[block, :, start : start + 2 * rows] = tail[8:9, : 2 * rows]
            for index in range(0, count, 2):
                two = [stage[half, index + k, :rows, :].astype(F32) for k in range(2)]
                at = slice(index * part, (index + 2) * part)
                left = jnp.concatenate([one[:part] for one in two], axis=0)
                right = jnp.concatenate([one[part:] for one in two], axis=0)
                attn[half, at, :HALF] = left.astype(BF)
                attn[half, at, HALF:] = right.astype(BF)
        pltpu.make_async_copy(attn, attn_out, sem.at[4]).start()
    first_in[...] = (normed * vectors[0:1, :] + vectors[1:2, :]).astype(BF)
    for half in range(2):
        if not placed:
            drain(qkv.at[half], sem.at[half])
        value = dot_nn(first_in[...], qkv[half, 0]) + heads[half, 0:1, :]
        proj[half, 0] = (value.astype(BF).astype(F32) * SCORE_SCALE).astype(BF)
        proj[half, 1] = dot_nn(first_in[...], qkv[half, 1]).astype(BF)
        value = dot_nn(first_in[...], qkv[half, 2]) + heads[half, 1:2, :]
        proj[half, 2] = value.astype(BF)
    if not placed:
        pltpu.make_async_copy(qkv, qkv_out, sem.at[5]).start()
    lane = lax.broadcasted_iota(jnp.int32, (SEQ, PAIR), 1)
    for half in range(2):
        for pair in range(HALF // PAIR):
            at = slice(pair * PAIR, (pair + 1) * PAIR)
            q_pair, k_pair, v_pair = proj[half, 0, :, at], proj[half, 1, :, at], proj[half, 2, :, at]
            v_turned = v_pair.T
            turned = []
            for side in range(2):
                mine = (lane < HD) if side == 0 else (lane >= HD)
                q_side = jnp.where(mine, q_pair, jnp.zeros_like(q_pair))
                scores = dot_nt(k_pair, q_side) + bias[...]
                top = jnp.max(scores, axis=0, keepdims=True)
                exponent = jnp.exp(scores - top)
                total = jnp.sum(exponent, axis=0, keepdims=True)
                index = half * (HALF // HD) + pair * 2 + side
                log_total[index : index + 1, :] = top + jnp.log(total)
                part = dot_nn(v_turned[side * HD : (side + 1) * HD], exponent.astype(BF))
                turned.append(part * (1.0 / total))
            both = jnp.concatenate(turned, axis=0).T
            mixed[:, half * HALF + pair * PAIR : half * HALF + (pair + 1) * PAIR] = both.astype(BF)
    value = dot_nn(mixed[:, :HALF], attn[0]) + dot_nn(mixed[:, HALF:], attn[1])
    hidden_row = x + value + vectors[4:5, :]
    hidden_one[...] = hidden_row
    normed, _ = norm_parts(hidden_row)
    second_in[...] = (normed * vectors[2:3, :] + vectors[3:4, :]).astype(BF)
    if not placed:
        pltpu.make_async_copy(attn, attn_out, sem.at[4]).wait()
        pltpu.make_async_copy(qkv, qkv_out, sem.at[5]).wait()


def kept_grad(cotangent, core_ref, pads_ref):
    position = lax.broadcasted_iota(jnp.int32, (SEQ, D), 0)
    kept = position < SEQ - pads_ref[core_ref[0]]
    return jnp.where(kept, cotangent[...].astype(F32), 0.0)


def up_kernel(placed, count, slot_ref, core_ref, pads_ref, second_in, cotangent, bias, *rest):
    rows = D // count
    step = pl.program_id(0)
    if placed:
        up, act, slope, grad_down, low_grad = rest
        up_block = up.at[0]
    else:
        parts = rest[:4]
        act, slope, up_out, down_own, down_other = rest[4:9]
        low_grad, up, made, sem = rest[9:]
        up_block = up.at[step]

        @pl.when(step == 0)
        def _():
            for half in (1, 0):

                def place(index, carry, half=half):
                    down = pl.ds(pl.multiple_of(index * rows, 16), rows)

                    def send(src):
                        for part in range(2):
                            block = (1 - half) * 2 + part
                            pltpu.make_async_copy(
                                src.at[part * rows : (part + 1) * rows],
                                up.at[block, down],
                                sem.at[block],
                            ).start()

                    fetch(slot_ref[half, index], parts[2 * half], parts[2 * half + 1], send)
                    return carry

                lax.fori_loop(0, count, place, 0)

    @pl.when(step == 0)
    def _():
        low_grad[...] = kept_grad(cotangent, core_ref, pads_ref).astype(BF)

    if not placed:
        drain(up_block, sem.at[step])
        pltpu.make_async_copy(up_block, up_out.at[step], sem.at[4]).start()
    chunk_rows = 256
    for chunk in range(SEQ // chunk_rows):
        at = slice(chunk * chunk_rows, (chunk + 1) * chunk_rows)
        pre = dot_nn(second_in[at, :], up_block[...]) + bias[0]
        square = pre * pre
        bent = jnp.tanh(GELU_COEF * (pre + GELU_CUBE * square * pre))
        half_up = 0.5 + 0.5 * bent
        act[0, at, :] = (pre * half_up).astype(BF)
        inner = GELU_COEF * (1.0 + 3.0 * GELU_CUBE * square)
        slope[0, at, :] = (half_up + 0.5 * pre * (1.0 - bent * bent) * inner).astype(BF)
    grad = dot_tn(act[0], low_grad[...]).astype(BF)
    if placed:
        grad_down[0] = grad
        return
    turn = lax.rem(step, 2)

    @pl.when(step >= 2)
    def _():
        drain(made.at[turn], sem.at[5 + turn])

    made[turn] = grad
    for half, out in ((1, down_other), (0, down_own)):

        @pl.when(step // 2 == 1 - half)
        def _(half=half, out=out):
            for index in range(count // 2):
                pltpu.make_async_copy(
                    made.at[turn, index * 2 * rows : (index + 1) * 2 * rows],
                    out.at[slot_ref[half, turn * (count // 2) + index]],
                    sem.at[5 + turn],
                ).start()

    @pl.when(step == 3)
    def _():
        drain(made.at[0], sem.at[5])
        drain(made.at[1], sem.at[6])
        drain(up, sem.at[4])


def down_kernel(
    placed,
    count,
    slot_ref,
    core_ref,
    pads_ref,
    second_in,
    hidden_one,
    cotangent,
    vectors,
    act,
    slope,
    up,
    *rest,
):
    rows = D // count
    step = pl.program_id(0)
    if placed:
        down, layer_output, grad_second, grad_hidden, grad_up = rest[:5]
        low_grad, out_sum, turned_in = rest[5:]
        down_block = down.at[0]
    else:
        parts = rest[:4]
        layer_output, grad_second, grad_hidden, up_own, up_other = rest[4:9]
        low_grad, out_sum, turned_in, down, made, sem = rest[9:]
        down_block = down.at[step]

        @pl.when(step == 0)
        def _():
            for half in (1, 0):

                def place(index, carry, half=half):
                    block = (1 - half) * 2 + index // (count // 2)
                    start = lax.rem(index, count // 2) * 2 * rows

                    def send(src):
                        pltpu.make_async_copy(
                            src,
                            down.at[block, pl.ds(pl.multiple_of(start, 16), 2 * rows)],
                            sem.at[block],
                        ).start()

                    fetch(slot_ref[half, index], parts[2 * half], parts[2 * half + 1], send)
                    return carry

                lax.fori_loop(0, count, place, 0)

    @pl.when(step == 0)
    def _():
        low_grad[...] = kept_grad(cotangent, core_ref, pads_ref).astype(BF)
        turned_in[...] = second_in[...].T
        out_sum[...] = hidden_one[...] + vectors[5:6, :]
        grad_second[...] = jnp.zeros_like(grad_second)

    if not placed:
        drain(down_block, sem.at[step])
    grad_pre = dot_nt(low_grad[...], down_block[...]) * slope[0].astype(F32)
    grad_hidden[0] = column_sum(grad_pre)
    pre_low = grad_pre.astype(BF)
    out_sum[...] += dot_nn(act[0], down_block[...])
    grad_second[...] += dot_nt(pre_low, up[0])
    grad = dot_nn(turned_in[...], pre_low).astype(BF)

    @pl.when(step == 3)
    def _():
        layer_output[...] = out_sum[...].astype(BF)

    if placed:
        grad_up[0] = grad
        return
    turn = lax.rem(step, 2)

    @pl.when(step >= 2)
    def _():
        drain(made.at[turn], sem.at[4 + turn])

    made[turn] = grad
    for half, out in ((1, up_other), (0, up_own)):

        @pl.when(step // 2 == 1 - half)
        def _(half=half, out=out):
            down_at = pl.ds(pl.multiple_of(turn * rows, 16), rows)
            for index in range(count):
                pltpu.make_async_copy(
                    made.at[turn, index * rows : (index + 1) * rows],
                    out.at[slot_ref[half, index], down_at],
                    sem.at[4 + turn],
                ).start()

    @pl.when(step == 3)
    def _():
        drain(made.at[0], sem.at[4])
        drain(made.at[1], sem.at[5])


def attend_back_kernel(
    core_ref,
    pads_ref,
    cotangent,
    vectors,
    row_code,
    key_code,
    grad_second,
    hidden_one,
    proj,
    log_total,
    mixed,
    attn,
    grad_one_out,
    proj_low,
    grad_attn,
    lines,
    head_lines,
    bias,
):
    bias[...] = visible_bias(row_code[...], key_code[...])
    grad_out = kept_grad(cotangent, core_ref, pads_ref)
    normed, inv_std = norm_parts(hidden_one[...])
    grads = grad_second[...]
    lines[0:1, :], lines[1:2, :] = column_sum(grads * normed), column_sum(grads)
    grad_one = grad_out + norm_back(grads, normed, inv_std, vectors[2:3, :])
    grad_one_out[...] = grad_one
    lines[2:3, :], lines[3:4, :] = column_sum(grad_one), column_sum(grad_out)
    grad_low = grad_one.astype(BF)
    lane = lax.broadcasted_iota(jnp.int32, (SEQ, PAIR), 1)
    for half in range(2):
        grad_attn[half] = dot_tn(mixed[:, half * HALF : (half + 1) * HALF], grad_low).astype(BF)
        grad_mixed = dot_nt(grad_low, attn[half]).astype(BF)
        for pair in range(HALF // PAIR):
            at = slice(pair * PAIR, (pair + 1) * PAIR)
            q_pair, k_pair, v_pair = proj[half, 0, :, at], proj[half, 1, :, at], proj[half, 2, :, at]
            g_pair = grad_mixed[:, at]
            k_turned = k_pair.T
            grad_key = jnp.zeros((SEQ, PAIR), F32)
            grad_value = jnp.zeros((SEQ, PAIR), F32)
            turned = []
            for side in range(2):
                mine = (lane < HD) if side == 0 else (lane >= HD)
                q_side = jnp.where(mine, q_pair, jnp.zeros_like(q_pair))
                g_side = jnp.where(mine, g_pair, jnp.zeros_like(g_pair))
                index = half * (HALF // HD) + pair * 2 + side
                scores = dot_nt(k_pair, q_side) + bias[...]
                probs = jnp.exp(scores - log_total[index : index + 1, :])
                grad_probs = dot_nt(v_pair, g_side)
                row_dot = column_sum(probs * grad_probs)
                grad_scores = (probs * (grad_probs - row_dot)).astype(BF)
                grad_value = grad_value + dot_nn(probs.astype(BF), g_side)
                grad_key = grad_key + dot_nn(grad_scores, q_side)
                turned.append(dot_nn(k_turned[side * HD : (side + 1) * HD], grad_scores))
            grad_query = jnp.concatenate(turned, axis=0).T * SCORE_SCALE
            head_lines[half, 0:1, at] = column_sum(grad_query)
            head_lines[half, 1:2, at] = column_sum(grad_value)
            proj_low[half, 0, :, at] = grad_query.astype(BF)
            proj_low[half, 1, :, at] = grad_key.astype(BF)
            proj_low[half, 2, :, at] = grad_value.astype(BF)


def first_back_kernel(
    placed,
    count,
    slot_ref,
    core_ref,
    tokens,
    vectors,
    first_in,
    proj_low,
    qkv,
    grad_one,
    grad_attn,
    lines,
    head_lines,
    grad_hidden,
    input_grad,
    *rest,
):
    if placed:
        qkv_grad, first_lines = rest
    else:
        outs, small, sums = rest[:2], rest[2], rest[3]
        rows = D // count
        part = rows // 2
    turned_first = first_in[...].T
    grad_first = jnp.zeros((SEQ, D), F32)
    for half in range(2):
        for kind in range(3):
            grad_first = grad_first + dot_nt(proj_low[half, kind], qkv[half, kind])
            grad_qkv = dot_nn(turned_first, proj_low[half, kind]).astype(BF)
            if placed:
                qkv_grad[half, kind] = grad_qkv
                continue
            for index in range(count):
                outs[half][slot_ref[half, index], kind * rows : (kind + 1) * rows, :] = grad_qkv[
                    index * rows : (index + 1) * rows, :
                ]
    normed, inv_std = norm_parts(tokens[...].astype(F32))
    gain_one, shift_one = column_sum(grad_first * normed), column_sum(grad_first)
    input_grad[...] = grad_one[...] + norm_back(grad_first, normed, inv_std, vectors[0:1, :])
    if placed:
        first_lines[0:1, :], first_lines[1:2, :] = gain_one, shift_one
        return
    sums[0:1, :], sums[1:2, :] = gain_one, shift_one
    sums[2:6, :] = lines[0:4, :]
    small[...] = jnp.zeros_like(small)
    for half in range(2):
        whole = grad_attn[half].astype(F32)
        for index in range(count):
            block, start = (1 - half) * 2 + index // (count // 2), (index % (count // 2)) * 2 * rows
            slot = slot_ref[half, index]
            piece = whole[index * part : (index + 1) * part, :]
            piece = jnp.concatenate([piece[:, :HALF], piece[:, HALF:]], axis=0)
            outs[half][slot, 3 * rows : 4 * rows, :] = piece.astype(BF)
            small[0:6, :rows] = sums[0:6, index * rows : (index + 1) * rows]
            small[6:8, :part] = head_lines[half, :, index * part : (index + 1) * part]
            small[8:9, : 2 * rows] = grad_hidden[block, :, start : start + 2 * rows]
            outs[half][slot, 4 * rows :, :] = small[...].astype(BF)


def close_kernel(rows, total_down, total_up, kept, got, total, squares):
    value = kept[...] + got[...].astype(F32)
    total[...] = value
    part = jnp.sum(total_down[...] * total_down[...]) + jnp.sum(total_up[...] * total_up[...])
    row = lax.broadcasted_iota(jnp.int32, value.shape, 0)
    weight = jnp.where((row >= 4 * rows) & (row < 4 * rows + 6), 0.5, 1.0)
    part = part + jnp.sum(value * value * weight)
    squares[...] = jnp.full(squares.shape, part, F32)


def adam_step(gradient, master, first, second, average, factor, decay_rate, step_rate):
    clipped = gradient * factor
    first_new = BETA_ONE * first + (1.0 - BETA_ONE) * clipped
    second_new = BETA_TWO * second + (1.0 - BETA_TWO) * clipped * clipped
    first_hat = first_new / (1.0 - BETA_ONE**STEP)
    second_hat = second_new / (1.0 - BETA_TWO**STEP)
    master_new = master - step_rate * (
        first_hat / (jnp.sqrt(second_hat) + ADAM_EPS) + decay_rate * master
    )
    average_new = EMA_RATE * average + (1.0 - EMA_RATE) * master_new
    return (first_new, second_new, master_new, average_new)


def update_kernel(rows, spread, total_down, total_up, total, *rest):
    state, norm, results = rest[:28], rest[28], rest[29:]
    grad_norm = jnp.sqrt(jnp.sum(spread[...], axis=0))[0:1, 0:1]
    norm[...] = jnp.broadcast_to(grad_norm, norm.shape)
    factor = CLIP_NORM / jnp.maximum(grad_norm, CLIP_NORM)
    part = rows // 2

    def apply(index, at, gradient):
        decay, rate = (WEIGHT_DECAY, LEARN_RATE) if index < 4 else (0.0, VECTOR_RATE)
        values = adam_step(
            gradient, *[state[4 * index + k][at] for k in range(4)], factor, decay, rate
        )
        for k in range(4):
            results[4 * index + k][at] = values[k]

    for kind in range(3):
        apply(0, (kind,), total[kind * rows : (kind + 1) * rows, :])
    for side in range(2):
        start = 3 * rows + side * part
        columns = slice(side * HALF, (side + 1) * HALF)
        apply(1, (slice(None), columns), total[start : start + part, :])
        columns = slice(side * D, (side + 1) * D)
        apply(2, (slice(None), columns), total_up[side * rows : (side + 1) * rows, :])
    every = (slice(None), slice(None))
    apply(3, every, total_down[...])
    apply(4, every, total[4 * rows + 6 : 4 * rows + 8, :part])
    apply(5, every, total[4 * rows + 8 : 4 * rows + 9, : 2 * rows])
    apply(6, every, total[4 * rows : 4 * rows + 6, :rows])


def vmem(*shapes):
    return [pltpu.VMEM(shape, dtype) for shape, dtype in shapes]


def shape(dims, dtype):
    return jax.ShapeDtypeStruct(dims, dtype)


def whole_spec(dims):
    return pl.BlockSpec(dims, lambda *_: (0,) * len(dims))


def block_spec(dims):
    return pl.BlockSpec((1,) + dims, lambda i, *_: (i,) + (0,) * len(dims))


def any_spec(_=None):
    return pl.BlockSpec(memory_space=pl.ANY)


def call(body, name, prefetch, grid, args, specs, outs, out_specs, scratch, mib, cost):
    flops, touched, special = cost
    return pl.pallas_call(
        body,
        out_shape=outs,
        grid_spec=pltpu.PrefetchScalarGridSpec(
            num_scalar_prefetch=len(prefetch),
            grid=(grid,),
            in_specs=specs,
            out_specs=out_specs,
            scratch_shapes=scratch,
        ),
        compiler_params=pltpu.CompilerParams(vmem_limit_bytes=mib << 20),
        cost_estimate=pl.CostEstimate(
            flops=flops, bytes_accessed=touched, transcendentals=special
        ),
        name=name,
    )(*prefetch, *args)


def both_halves(own, core):
    other = swap_cores(own)
    first = jnp.where(core == 0, own, other)
    second = jnp.where(core == 0, other, own)
    return jnp.concatenate([first, second], axis=0)


def body(force_plain, *args):
    (tokens, cotangent, seg_lengths, pad_counts) = args[:4]
    groups = [args[4 + 4 * i : 8 + 4 * i] for i in range(7)]
    qkv_w, attn_w, up_w, down_w, head_w, hidden_w, vector_w = (group[0] for group in groups)
    rows = qkv_w.shape[1]
    part = rows // 2
    count = D // rows
    placed = bool(rows % 16) or force_plain
    here, core = lax.axis_index("dp"), lax.axis_index("mp")
    slot = jnp.stack([slots(count, here, core), slots(count, here, 1 - core)], axis=0)
    core_at = core.reshape(1).astype(jnp.int32)

    packed = [shape((4 * rows + 16, HALF), BF), shape((2 * rows, D), BF), shape((2 * rows, D), BF)]
    pack_args = (qkv_w, attn_w, up_w, down_w, head_w, hidden_w.reshape(1, -1), vector_w)
    piece, up_piece, down_piece = call(
        pack_kernel,
        "pack",
        (),
        1,
        pack_args,
        [whole_spec(one.shape) for one in pack_args],
        packed,
        [whole_spec(one.shape) for one in packed],
        vmem(((16, HALF), F32)),
        60,
        (1, 1_400_000, 0),
    )
    front_hops, up_hops, down_hops = (
        Gatherer(one, count) for one in (piece, up_piece, down_piece)
    )
    high = len(front_hops.bits) - 2
    front_hops.take(front_hops.send())
    for _ in range(high):
        front_got, up_got = front_hops.send(), up_hops.send(front_hops.held)
        _, front_got, up_got = join((), front_got, up_got)
        front_hops.take(front_got)
        up_hops.take(up_got)
    front_got, up_got = front_hops.send(), up_hops.send()
    for _ in range(high):
        down_hops.take(down_hops.send(up_hops.held))
    _, front_got, up_got, down_hops.held = join((), front_got, up_got, down_hops.held)
    front_hops.take(front_got)
    up_hops.take(up_got)
    front_parts, up_hops.held, down_hops.held = join(
        front_hops.parts(), up_hops.held, down_hops.held
    )
    up_got, down_got = up_hops.send(), down_hops.send()

    lengths = lax.dynamic_index_in_dim(seg_lengths, core, 0, keepdims=False)
    padding = lax.dynamic_index_in_dim(pad_counts, core, 0, keepdims=False)
    upto = jnp.arange(lengths.shape[0])[:, None] >= jnp.arange(lengths.shape[0])[None, :]
    bounds = jnp.sum(jnp.where(upto, lengths[None, :], 0), axis=1)
    position = jnp.arange(SEQ, dtype=jnp.int32)
    row_code = jnp.sum((position[None, :] >= bounds[:, None]).astype(jnp.int32), axis=0)[None, :]
    key_code = jnp.sum((position[:, None] >= bounds[None, :]).astype(jnp.int32), axis=1)[:, None]
    key_code = jnp.where(position[:, None] >= SEQ - padding, -1, key_code)

    rows_spec = pl.BlockSpec((SEQ, D), lambda _, slot, core, *more: (core[0], 0))
    rows_spec_two = pl.BlockSpec((SEQ, D), lambda _, core, *more: (core[0], 0))
    qkv_shape, attn_shape = (2, 3, D, HALF), (2, HALF, D)
    front_outs = [
        shape((SEQ, D), BF),
        shape((2, 3, SEQ, HALF), BF),
        shape((2 * HALF // HD, SEQ), F32),
        shape((SEQ, D), BF),
        shape((SEQ, D), F32),
        shape((SEQ, D), BF),
    ]
    out_specs = [whole_spec(one.shape) for one in front_outs]
    scratch = vmem(((SEQ, SEQ), F32))
    if placed:
        picks = [
            (slot[half][:, None] == jnp.arange(count, dtype=jnp.int32)[None, :]).astype(BF)
            for half in range(2)
        ]

        def spread(parts):
            return [
                reorder(jnp.concatenate(parts[2 * half : 2 * half + 2], axis=0), picks[half])
                for half in range(2)
            ]

        both = spread(front_parts)
        tails = [one[:, 4 * rows :].astype(F32) for one in both]
        vectors = jnp.pad(tails[0][:, :6, :rows].transpose(1, 0, 2).reshape(6, D), ((0, 2), (0, 0)))
        heads = jnp.stack(
            [one[:, 6:8, :part].transpose(1, 0, 2).reshape(2, HALF) for one in tails], axis=0
        )
        hidden = jnp.concatenate(
            [one[:, 8, : 2 * rows].reshape(2, 1, D) for one in (tails[1], tails[0])], axis=0
        )
        qkv_all = jnp.stack(
            [
                one[:, : 3 * rows]
                .reshape(count, 3, rows, HALF)
                .transpose(1, 0, 2, 3)
                .reshape(3, D, HALF)
                for one in both
            ],
            axis=0,
        )
        attn_all = jnp.stack(
            [
                one[:, 3 * rows : 4 * rows]
                .reshape(count, 2, part, HALF)
                .transpose(0, 2, 1, 3)
                .reshape(HALF, D)
                for one in both
            ],
            axis=0,
        )
        more = (vectors, heads, qkv_all, attn_all)
        more_specs = [whole_spec(one.shape) for one in more]
    else:
        more = front_parts
        more_specs = [any_spec()] * 4
        extra = [
            shape((8, D), F32),
            shape((2, 2, HALF), F32),
            shape((4, 1, D), F32),
        ]
        front_outs += extra + [shape(qkv_shape, BF), shape(attn_shape, BF)]
        out_specs += [whole_spec(one.shape) for one in extra] + [any_spec()] * 2
        scratch += vmem((qkv_shape, BF), (attn_shape, BF), ((2, count, rows + 16, HALF), BF))
        scratch += [pltpu.SemaphoreType.DMA((6,))]
    done = call(
        functools.partial(front_kernel, placed, count, rows),
        "front",
        (slot, core_at),
        1,
        (tokens, row_code, key_code) + tuple(more),
        [rows_spec, whole_spec((1, SEQ)), whole_spec((SEQ, 1))] + more_specs,
        front_outs,
        out_specs,
        scratch,
        48,
        (6_000_000_000, 16_000_000, 3_200_000),
    )
    done, up_got, down_got = join(done, up_got, down_got)
    up_hops.take(up_got)
    up_parts = up_hops.parts()
    down_hops.take(down_got)
    down_got = down_hops.send()
    first_in, proj, log_total, mixed, hidden_one, second_in = done[:6]
    if not placed:
        vectors, heads, hidden, qkv_all, attn_all = done[6:]

    blocks = shape((4, SEQ, D), BF)
    pieces = shape((count, 2 * rows, D), BF)
    square_blocks = shape((4, D, D), BF)
    if placed:
        both = spread(up_parts)
        up_all = jnp.concatenate(
            [
                one.reshape(count, 2, rows, D).transpose(1, 0, 2, 3).reshape(2, D, D)
                for one in (both[1], both[0])
            ],
            axis=0,
        )
        more, more_specs = (up_all,), [block_spec((D, D))]
        outs = [blocks, blocks, square_blocks]
        out_specs = [block_spec((SEQ, D)), block_spec((SEQ, D)), block_spec((D, D))]
        scratch = vmem(((SEQ, D), BF))
    else:
        more, more_specs = up_parts, [any_spec()] * 4
        outs = [blocks, blocks, square_blocks, pieces, pieces]
        out_specs = [block_spec((SEQ, D)), block_spec((SEQ, D))] + [any_spec()] * 3
        scratch = vmem(((SEQ, D), BF), ((4, D, D), BF), ((2, D, D), BF))
        scratch += [pltpu.SemaphoreType.DMA((7,))]
    done = call(
        functools.partial(up_kernel, placed, count),
        "up",
        (slot, core_at, pad_counts),
        4,
        (second_in, cotangent, hidden) + tuple(more),
        [whole_spec((SEQ, D)), rows_spec, block_spec((1, D))] + more_specs,
        outs,
        out_specs,
        scratch,
        48,
        (4_900_000_000, 20_000_000, 1_600_000),
    )
    done, down_got = join(done, down_got)
    down_hops.take(down_got)
    down_parts = down_hops.parts()
    act, slope = done[:2]
    turned = [pick.T for pick in picks] if placed else None
    if placed:
        down_own, down_other = (
            reorder(done[2][2 * start : 2 * start + 2].reshape(count, 2 * rows, D), turned[half])
            for half, start in ((0, 1), (1, 0))
        )
    else:
        up_all, down_own, down_other = done[2:]
    down_sum = Reducer(down_own, down_other, count)
    down_got = down_sum.send()

    if placed:
        both = spread(down_parts)
        down_all = jnp.concatenate([one.reshape(2, D, D) for one in (both[1], both[0])], axis=0)
        more, more_specs = (down_all,), [block_spec((D, D))]
    else:
        more, more_specs = down_parts, [any_spec()] * 4
    outs = [shape((SEQ, D), BF), shape((SEQ, D), F32), shape((4, 1, D), F32)]
    out_specs = [whole_spec((SEQ, D)), whole_spec((SEQ, D)), block_spec((1, D))]
    scratch = vmem(((SEQ, D), BF), ((SEQ, D), F32), ((D, SEQ), BF))
    if placed:
        outs += [square_blocks]
        out_specs += [block_spec((D, D))]
    else:
        outs += [pieces, pieces]
        out_specs += [any_spec()] * 2
        scratch += vmem(((4, D, D), BF), ((2, D, D), BF)) + [pltpu.SemaphoreType.DMA((6,))]
    done = call(
        functools.partial(down_kernel, placed, count),
        "down",
        (slot, core_at, pad_counts),
        4,
        (second_in, hidden_one, cotangent, vectors, act, slope, up_all)
        + tuple(more),
        [
            whole_spec((SEQ, D)),
            whole_spec((SEQ, D)),
            rows_spec,
            whole_spec((8, D)),
            block_spec((SEQ, D)),
            block_spec((SEQ, D)),
            block_spec((D, D)),
        ]
        + more_specs,
        outs,
        out_specs,
        scratch,
        56,
        (9_700_000_000, 24_000_000, 0),
    )
    done, down_got = join(done, down_got)
    layer_half, grad_second, grad_hidden = done[:3]
    layer_output = both_halves(layer_half, core)
    if placed:

        def up_pieces(value, half):
            value = value.reshape(2, count, rows, D).transpose(1, 0, 2, 3)
            return reorder(value.reshape(count, 2 * rows, D), turned[half])

        up_own, up_other = up_pieces(done[3][2:], 0), up_pieces(done[3][:2], 1)
    else:
        up_own, up_other = done[3:]
    up_sum = Reducer(up_own, up_other, count)
    down_sum.take(down_got)
    down_got, up_got = down_sum.send(), up_sum.send()

    outs = [
        shape((SEQ, D), F32),
        shape((2, 3, SEQ, HALF), BF),
        shape(attn_shape, BF),
        shape((8, D), F32),
        shape((2, 2, HALF), F32),
    ]
    done = call(
        attend_back_kernel,
        "attend_back",
        (core_at, pad_counts),
        1,
        (
            cotangent,
            vectors,
            row_code,
            key_code,
            grad_second,
            hidden_one,
            proj,
            log_total,
            mixed,
            attn_all,
        ),
        [
            rows_spec_two,
            whole_spec((8, D)),
            whole_spec((1, SEQ)),
            whole_spec((SEQ, 1)),
            whole_spec((SEQ, D)),
            whole_spec((SEQ, D)),
            whole_spec((2, 3, SEQ, HALF)),
            whole_spec((2 * HALF // HD, SEQ)),
            whole_spec((SEQ, D)),
            whole_spec(attn_shape),
        ],
        outs,
        [whole_spec(one.shape) for one in outs],
        vmem(((SEQ, SEQ), F32)),
        48,
        (6_400_000_000, 16_000_000, 3_200_000),
    )
    done, down_got, up_got = join(done, down_got, up_got)
    grad_one, proj_low, grad_attn, lines, head_lines = done
    down_sum.take(down_got)
    up_sum.take(up_got)
    down_got, up_got = down_sum.send(), up_sum.send()
    if placed:
        outs = [shape((SEQ, D), F32), shape(qkv_shape, BF), shape((8, D), F32)]
        scratch = []
    else:
        outs = [shape((SEQ, D), F32)] + [shape((count, 4 * rows + 16, HALF), BF)] * 2
        scratch = vmem(((16, HALF), F32), ((8, D), F32))
    done = call(
        functools.partial(first_back_kernel, placed, count),
        "first_back",
        (slot, core_at),
        1,
        (
            tokens,
            vectors,
            first_in,
            proj_low,
            qkv_all,
            grad_one,
            grad_attn,
            lines,
            head_lines,
            grad_hidden,
        ),
        [
            rows_spec,
            whole_spec((8, D)),
            whole_spec((SEQ, D)),
            whole_spec((2, 3, SEQ, HALF)),
            whole_spec(qkv_shape),
            whole_spec((SEQ, D)),
            whole_spec(attn_shape),
            whole_spec((8, D)),
            whole_spec((2, 2, HALF)),
            whole_spec((4, 1, D)),
        ],
        outs,
        [whole_spec(one.shape) for one in outs],
        scratch,
        48,
        (3_700_000_000, 18_000_000, 0),
    )
    done, down_got, up_got = join(done, down_got, up_got)
    down_sum.take(down_got)
    up_sum.take(up_got)
    input_grad = both_halves(done[0], core)
    if placed:
        whole_lines = jnp.concatenate([done[2][:2], lines[:4]], axis=0)
        sent = []
        for half in range(2):
            qkv_part = (
                done[1][half]
                .reshape(3, count, rows, HALF)
                .transpose(1, 0, 2, 3)
                .reshape(count, 3 * rows, HALF)
            )
            attn_part = (
                grad_attn[half]
                .reshape(count, part, 2, HALF)
                .transpose(0, 2, 1, 3)
                .reshape(count, rows, HALF)
            )
            start = (1 - half) * 2

            def widen(value):
                return jnp.pad(value, ((0, 0), (0, 0), (0, HALF - value.shape[2])))

            small = jnp.concatenate(
                [
                    widen(whole_lines.reshape(6, count, rows).transpose(1, 0, 2)),
                    widen(head_lines[half].reshape(2, count, part).transpose(1, 0, 2)),
                    widen(grad_hidden[start : start + 2].reshape(count, 1, 2 * rows)),
                    jnp.zeros((count, 7, HALF), F32),
                ],
                axis=1,
            ).astype(BF)
            sent.append(reorder(jnp.concatenate([qkv_part, attn_part, small], axis=1), turned[half]))
        front_own, front_other = sent
    else:
        front_own, front_other = done[1:]
    front_sum = Reducer(front_own, front_other, count)

    kept, got = down_sum.finish()
    total_down = kept + got.astype(F32)
    kept, got = up_sum.finish()
    total_up = kept + got.astype(F32)
    kept, got = front_sum.finish()
    outs = [shape(kept.shape, F32), shape((2 * count, 8, 128), F32)]
    close_args = (total_down, total_up, kept, got)
    total, squares = call(
        functools.partial(close_kernel, rows),
        "close",
        (),
        1,
        close_args,
        [whole_spec(one.shape) for one in close_args],
        outs,
        [whole_spec(one.shape) for one in outs],
        [],
        16,
        (1_000_000, 1_200_000, 0),
    )
    spread_squares = lax.all_to_all(squares, BOTH, 0, 0, tiled=True)
    state = []
    for index, group in enumerate(groups):
        state += [one.reshape(1, -1) if index == 5 else one for one in group]
    update_args = (spread_squares, total_down, total_up, total) + tuple(state)
    outs = [shape((8, 128), F32)] + [shape(one.shape, F32) for one in state]
    results = call(
        functools.partial(update_kernel, rows),
        "update",
        (),
        1,
        update_args,
        [whole_spec(one.shape) for one in update_args],
        outs,
        [whole_spec(one.shape) for one in outs],
        [],
        60,
        (5_000_000, 8_000_000, 500_000),
    )
    grad_norm = results[0][0, 0]
    results = [
        one.reshape(-1) if 20 <= index < 24 else one for index, one in enumerate(results[1:])
    ]
    return (layer_output, input_grad, grad_norm, *results)


FORCE_PLAIN = False


def solution(mesh):
    row, late, wide = P("dp", None), P(("mp", "dp"), None), P("dp", "mp")
    kinds = (
        P(None, "dp", "mp"),
        late,
        wide,
        late,
        P(None, ("mp", "dp")),
        P(("mp", "dp")),
        P(None, "dp"),
    )
    per_parameter = tuple(kind for kind in kinds for _ in range(4))
    return jax.shard_map(
        functools.partial(body, FORCE_PLAIN),
        mesh=mesh,
        in_specs=(row, row, row, P("dp")) + per_parameter,
        out_specs=(row, row, P()) + per_parameter,
        check_vma=False,
    )
```

```python
import functools

import jax
import jax.numpy as jnp
from jax import lax
from jax.experimental import pallas as pl
from jax.experimental.pallas import tpu as pltpu
from jax.sharding import PartitionSpec as P

HD = 64
PAIR = 128
SEQ = 512
D = 768
HALF = 384
STEP = 7
SMALL = 32

NORM_EPS = 1e-05
SCORE_SCALE = 0.125
LEARN_RATE = 0.03
VECTOR_RATE = 0.4
BETA_ONE = 0.9
BETA_TWO = 0.95
ADAM_EPS = 1e-08
WEIGHT_DECAY = 0.1
EMA_RATE = 0.8
CLIP_NORM = 1.0
GELU_COEF = 0.7978845608028654
GELU_CUBE = 0.044715
MASKED = -1e30

BF = jnp.bfloat16
F32 = jnp.float32
BOTH = ("dp", "mp")


def dot_nn(left, right):
    return lax.dot_general(left, right, (((1,), (0,)), ((), ())), preferred_element_type=F32)


def dot_nt(left, right):
    return lax.dot_general(left, right, (((1,), (1,)), ((), ())), preferred_element_type=F32)


def dot_tn(left, right):
    return lax.dot_general(left, right, (((0,), (0,)), ((), ())), preferred_element_type=F32)


def norm_parts(rows):
    row_mean = jnp.mean(rows, axis=1, keepdims=True)
    centered = rows - row_mean
    inv_std = lax.rsqrt(jnp.mean(centered * centered, axis=1, keepdims=True) + NORM_EPS)
    return (centered * inv_std, inv_std)


def norm_back(grad_in, normed, inv_std, gain):
    scaled = grad_in * gain
    return inv_std * (
        scaled
        - jnp.mean(scaled, axis=1, keepdims=True)
        - normed * jnp.mean(scaled * normed, axis=1, keepdims=True)
    )


def column_sum(value):
    return jnp.sum(value, axis=0, keepdims=True)


def step_bits(count):
    length = count.bit_length() - 1
    high = [(bit, bit) for bit in reversed(range(2, length))]
    return high + [(0, 1), (1, 0)]


def step_pairs(count, bits):
    return [
        (index * 2 + core, (index ^ (1 << bits[core])) * 2 + core)
        for index in range(count)
        for core in range(2)
    ]


def slots(count, here, core):
    length = count.bit_length() - 1
    apart = jnp.arange(count, dtype=jnp.int32) ^ here
    low, mid = apart & 1, (apart >> 1) & 1
    first = jnp.where(core == 0, mid, low)
    second = jnp.where(core == 0, low, mid)
    place = (first << (length - 1)) | (second << (length - 2))
    for bit in range(2, length):
        place = place | (((apart >> bit) & 1) << (length - 1 - bit))
    return place


def reorder(value, pick):
    flat = dot_nn(pick, value.reshape(value.shape[0], -1)).astype(BF)
    return flat.reshape(value.shape)


def swap_cores(value):
    return lax.ppermute(value, "mp", [(0, 1), (1, 0)])


def after(value, *others):
    return lax.optimization_barrier((value,) + others)[0]


def join(made, *gots):
    joined = lax.optimization_barrier(tuple(made) + gots)
    return (list(joined[: len(made)]), *joined[len(made) :])


class Gatherer:
    def __init__(self, piece, count):
        self.count, self.held, self.got = count, piece[None], None
        self.bits = step_bits(count)

    def send(self, *others):
        if others:
            self.held = after(self.held, *others)
        return lax.ppermute(self.held, BOTH, step_pairs(self.count, self.bits.pop(0)))

    def take(self, got):
        if self.bits:
            self.held = jnp.concatenate([self.held, got], axis=0)
        else:
            self.got = got

    def parts(self):
        return (self.held, self.got, swap_cores(self.held), swap_cores(self.got))


class Reducer:
    def __init__(self, own, other, count):
        self.count, self.half = count, count // 2
        self.bits = list(reversed(step_bits(count)))
        got = swap_cores(other)
        half = self.half
        self.kept = own[:half].astype(F32) + got[:half].astype(F32)
        self.sent = (own[half:].astype(F32) + got[half:].astype(F32)).astype(BF)

    def send(self):
        return lax.ppermute(self.sent, BOTH, step_pairs(self.count, self.bits.pop(0)))

    def take(self, got):
        self.half //= 2
        total = self.kept + got.astype(F32)
        self.kept, self.sent = total[: self.half], total[self.half :].astype(BF)

    def finish(self):
        while len(self.bits) > 1:
            self.take(self.send())
        return (self.kept[0], self.send()[0])


def fetch(slot, held, got, send):
    half = held.shape[0]

    @pl.when(slot < half)
    def _():
        send(held.at[slot])

    @pl.when(slot >= half)
    def _():
        send(got.at[slot - half])


def drain(ref, sem):
    pltpu.make_async_copy(ref, ref, sem).wait()


def own_rows(ref, core_ref):
    return ref[pl.ds(pl.multiple_of(core_ref[0] * SEQ, SEQ), SEQ), :]


def visible_bias(row_code, key_code):
    key_at = lax.broadcasted_iota(jnp.int32, (SEQ, SEQ), 0)
    row_at = lax.broadcasted_iota(jnp.int32, (SEQ, SEQ), 1)
    return jnp.where((key_code == row_code) | (key_at == row_at), 0.0, MASKED)


def pack_kernel(qkv_w, attn_w, up_w, down_w, head_w, hidden_w, vector_w, piece, up, down, small):
    rows = qkv_w.shape[1]
    part = rows // 2
    for kind in range(3):
        piece[kind * rows : (kind + 1) * rows, :] = qkv_w[kind].astype(BF)
    both = jnp.concatenate([attn_w[:, :HALF], attn_w[:, HALF:]], axis=0)
    piece[3 * rows : 3 * rows + 2 * part, :] = both.astype(BF)
    small[...] = jnp.zeros_like(small)
    small[0:6, :rows] = vector_w[...]
    small[6:8, :part] = head_w[...]
    small[8:9, : 2 * rows] = hidden_w[...]
    piece[4 * rows :, :] = small[...].astype(BF)
    up[0] = up_w[:, :D].astype(BF)
    up[1] = up_w[:, D:].astype(BF)
    down[...] = down_w[...].astype(BF)


def front_kernel(placed, count, rows, slot_ref, core_ref, tokens, row_code, key_code, *rest):
    if placed:
        vectors, heads, qkv, attn = rest[:4]
        outs, bias = rest[4:10], rest[10]
    else:
        parts = rest[:4]
        outs = rest[4:10]
        vectors, heads, hidden, qkv, attn = rest[10:15]
        bias, stage, sem = rest[15:]
    first_in, proj, log_total, mixed, hidden_one, second_in = outs
    if not placed:

        def place(index, carry):
            for half in range(2):
                down = pl.ds(pl.multiple_of(index * rows, 16), rows)

                def send(src, half=half, down=down):
                    pltpu.make_async_copy(
                        src.at[3 * rows :], stage.at[half, index], sem.at[2 + half]
                    ).start()
                    for kind in range(3):
                        pltpu.make_async_copy(
                            src.at[kind * rows : (kind + 1) * rows],
                            qkv.at[half, kind, down],
                            sem.at[half],
                        ).start()

                fetch(slot_ref[half, index], parts[2 * half], parts[2 * half + 1], send)
            return carry

        lax.fori_loop(0, count, place, 0)
    bias[...] = visible_bias(row_code[...], key_code[...])
    x = own_rows(tokens, core_ref).astype(F32)
    normed, _ = norm_parts(x)
    if not placed:
        part = rows // 2
        drain(stage.at[0], sem.at[2])
        drain(stage.at[1], sem.at[3])
        for half in range(2):
            for index in range(count):
                tail = stage[half, index, rows:, :].astype(F32)
                if half == 0:
                    vectors[0:6, index * rows : (index + 1) * rows] = tail[0:6, :rows]
                heads[half, :, index * part : (index + 1) * part] = tail[6:8, :part]
                block = (1 - half) * 2 + index // (count // 2)
                start = (index % (count // 2)) * 2 * rows
                hidden[block, :, start : start + 2 * rows] = tail[8:9, : 2 * rows]
            for index in range(0, count, 2):
                two = [stage[half, index + k, :rows, :].astype(F32) for k in range(2)]
                at = slice(index * part, (index + 2) * part)
                left = jnp.concatenate([one[:part] for one in two], axis=0)
                right = jnp.concatenate([one[part:] for one in two], axis=0)
                attn[half, at, :HALF] = left.astype(BF)
                attn[half, at, HALF:] = right.astype(BF)
    first_in[...] = (normed * vectors[0:1, :] + vectors[1:2, :]).astype(BF)
    for half in range(2):
        if not placed:
            drain(qkv.at[half], sem.at[half])
        value = dot_nn(first_in[...], qkv[half, 0]) + heads[half, 0:1, :]
        proj[half, 0] = (value.astype(BF).astype(F32) * SCORE_SCALE).astype(BF)
        proj[half, 1] = dot_nn(first_in[...], qkv[half, 1]).astype(BF)
        value = dot_nn(first_in[...], qkv[half, 2]) + heads[half, 1:2, :]
        proj[half, 2] = value.astype(BF)
    lane = lax.broadcasted_iota(jnp.int32, (SEQ, PAIR), 1)
    for half in range(2):
        for pair in range(HALF // PAIR):
            at = slice(pair * PAIR, (pair + 1) * PAIR)
            q_pair, k_pair, v_pair = proj[half, 0, :, at], proj[half, 1, :, at], proj[half, 2, :, at]
            v_turned = v_pair.T
            turned = []
            for side in range(2):
                mine = (lane < HD) if side == 0 else (lane >= HD)
                q_side = jnp.where(mine, q_pair, jnp.zeros_like(q_pair))
                scores = dot_nt(k_pair, q_side) + bias[...]
                top = jnp.max(scores, axis=0, keepdims=True)
                exponent = jnp.exp(scores - top)
                total = jnp.sum(exponent, axis=0, keepdims=True)
                index = half * (HALF // HD) + pair * 2 + side
                log_total[index : index + 1, :] = top + jnp.log(total)
                part = dot_nn(v_turned[side * HD : (side + 1) * HD], exponent.astype(BF))
                turned.append(part * (1.0 / total))
            both = jnp.concatenate(turned, axis=0).T
            mixed[:, half * HALF + pair * PAIR : half * HALF + (pair + 1) * PAIR] = both.astype(BF)
    value = dot_nn(mixed[:, :HALF], attn[0]) + dot_nn(mixed[:, HALF:], attn[1])
    hidden_row = x + value + vectors[4:5, :]
    hidden_one[...] = hidden_row
    normed, _ = norm_parts(hidden_row)
    second_in[...] = (normed * vectors[2:3, :] + vectors[3:4, :]).astype(BF)


def kept_grad(cotangent, core_ref, pads_ref):
    position = lax.broadcasted_iota(jnp.int32, (SEQ, D), 0)
    kept = position < SEQ - pads_ref[core_ref[0]]
    return jnp.where(kept, own_rows(cotangent, core_ref).astype(F32), 0.0)


def up_kernel(placed, count, slot_ref, core_ref, pads_ref, second_in, cotangent, bias, *rest):
    rows = D // count
    if placed:
        up, act, slope, grad_down, low_grad = rest
    else:
        parts = rest[:4]
        act, slope, up, down_own, down_other, low_grad, sem = rest[4:]
        for half in (1, 0):

            def place(index, carry, half=half):
                down = pl.ds(pl.multiple_of(index * rows, 16), rows)
                first = (1 - half) * 2

                def send(src):
                    pltpu.make_async_copy(
                        src, up.at[first : first + 2, down], sem.at[1 - half]
                    ).start()

                fetch(slot_ref[half, index], parts[2 * half], parts[2 * half + 1], send)
                return carry

            lax.fori_loop(0, count, place, 0)
    low_grad[...] = kept_grad(cotangent, core_ref, pads_ref).astype(BF)
    chunk_rows = 256
    for block in range(4):
        if not placed and block % 2 == 0:
            drain(up.at[block : block + 2], sem.at[block // 2])
        for chunk in range(SEQ // chunk_rows):
            at = slice(chunk * chunk_rows, (chunk + 1) * chunk_rows)
            pre = dot_nn(second_in[at, :], up[block]) + bias[block]
            square = pre * pre
            bent = jnp.tanh(pre * (GELU_COEF + GELU_COEF * GELU_CUBE * square))
            half_up = 0.5 + 0.5 * bent
            gelu = pre * half_up
            act[block, at, :] = gelu.astype(BF)
            inner = pre * (2.0 * GELU_COEF + 6.0 * GELU_COEF * GELU_CUBE * square)
            slope[block, at, :] = (half_up + half_up * (inner - half_up * inner)).astype(BF)
        grad = dot_tn(act[block], low_grad[...]).astype(BF)
        if placed:
            grad_down[block] = grad
            continue
        half, part = 1 - block // 2, block % 2
        out = (down_own, down_other)[half]
        for index in range(count // 2):
            out[slot_ref[half, part * (count // 2) + index]] = grad[
                index * 2 * rows : (index + 1) * 2 * rows, :
            ]


def down_kernel(
    placed,
    count,
    slot_ref,
    core_ref,
    pads_ref,
    second_in,
    hidden_one,
    cotangent,
    vectors,
    act,
    slope,
    up,
    *rest,
):
    rows = D // count
    if placed:
        down, layer_output, grad_second, grad_hidden, grad_up, low_grad, turned_in, out_sum = rest
    else:
        parts = rest[:4]
        layer_output, grad_second, grad_hidden, up_own, up_other = rest[4:9]
        low_grad, turned_in, out_sum, down, sem = rest[9:]
        for half in (1, 0):

            def place(index, carry, half=half):
                block = (1 - half) * 2 + index // (count // 2)
                start = lax.rem(index, count // 2) * 2 * rows

                def send(src):
                    pltpu.make_async_copy(
                        src,
                        down.at[block, pl.ds(pl.multiple_of(start, 16), 2 * rows)],
                        sem.at[block],
                    ).start()

                fetch(slot_ref[half, index], parts[2 * half], parts[2 * half + 1], send)
                return carry

            lax.fori_loop(0, count, place, 0)
    low_grad[...] = kept_grad(cotangent, core_ref, pads_ref).astype(BF)
    turned_in[...] = second_in[...].T
    for block in range(4):
        if not placed:
            drain(down.at[block], sem.at[block])
        grad_pre = dot_nt(low_grad[...], down[block]) * slope[block].astype(F32)
        grad_hidden[block] = column_sum(grad_pre)
        pre_low = grad_pre.astype(BF)
        grad = dot_nn(turned_in[...], pre_low).astype(BF)
        part_out = dot_nn(act[block], down[block])
        part_grad = dot_nt(pre_low, up[block])
        if block == 0:
            out_sum[...] = hidden_one[...] + vectors[5:6, :] + part_out
            grad_second[...] = part_grad
        elif block < 3:
            out_sum[...] += part_out
            grad_second[...] += part_grad
        else:
            layer_output[...] = (out_sum[...] + part_out).astype(BF)
            grad_second[...] += part_grad
        if placed:
            grad_up[block] = grad
            continue
        half, part = 1 - block // 2, block % 2
        out = (up_own, up_other)[half]
        for index in range(count):
            out[slot_ref[half, index], part * rows : (part + 1) * rows, :] = grad[
                index * rows : (index + 1) * rows, :
            ]


def attend_back_kernel(
    core_ref,
    pads_ref,
    cotangent,
    vectors,
    row_code,
    key_code,
    grad_second,
    hidden_one,
    proj,
    log_total,
    mixed,
    attn,
    grad_one_out,
    proj_low,
    grad_attn,
    lines,
    head_lines,
    bias,
):
    bias[...] = visible_bias(row_code[...], key_code[...])
    grad_out = kept_grad(cotangent, core_ref, pads_ref)
    normed, inv_std = norm_parts(hidden_one[...])
    grads = grad_second[...]
    lines[0:1, :], lines[1:2, :] = column_sum(grads * normed), column_sum(grads)
    grad_one = grad_out + norm_back(grads, normed, inv_std, vectors[2:3, :])
    grad_one_out[...] = grad_one
    lines[2:3, :], lines[3:4, :] = column_sum(grad_one), column_sum(grad_out)
    grad_low = grad_one.astype(BF)
    lane = lax.broadcasted_iota(jnp.int32, (SEQ, PAIR), 1)
    for half in range(2):
        grad_attn[half] = dot_tn(mixed[:, half * HALF : (half + 1) * HALF], grad_low).astype(BF)
        grad_mixed = dot_nt(grad_low, attn[half]).astype(BF)
        for pair in range(HALF // PAIR):
            at = slice(pair * PAIR, (pair + 1) * PAIR)
            q_pair, k_pair, v_pair = proj[half, 0, :, at], proj[half, 1, :, at], proj[half, 2, :, at]
            g_pair = grad_mixed[:, at]
            k_turned = k_pair.T
            grad_key = jnp.zeros((SEQ, PAIR), F32)
            grad_value = jnp.zeros((SEQ, PAIR), F32)
            turned = []
            for side in range(2):
                mine = (lane < HD) if side == 0 else (lane >= HD)
                q_side = jnp.where(mine, q_pair, jnp.zeros_like(q_pair))
                g_side = jnp.where(mine, g_pair, jnp.zeros_like(g_pair))
                index = half * (HALF // HD) + pair * 2 + side
                scores = dot_nt(k_pair, q_side) + bias[...]
                probs = jnp.exp(scores - log_total[index : index + 1, :])
                grad_probs = dot_nt(v_pair, g_side)
                row_dot = column_sum(probs * grad_probs)
                grad_scores = (probs * (grad_probs - row_dot)).astype(BF)
                grad_value = grad_value + dot_nn(probs.astype(BF), g_side)
                grad_key = grad_key + dot_nn(grad_scores, q_side)
                turned.append(dot_nn(k_turned[side * HD : (side + 1) * HD], grad_scores))
            grad_query = jnp.concatenate(turned, axis=0).T * SCORE_SCALE
            head_lines[half, 0:1, at] = column_sum(grad_query)
            head_lines[half, 1:2, at] = column_sum(grad_value)
            proj_low[half, 0, :, at] = grad_query.astype(BF)
            proj_low[half, 1, :, at] = grad_key.astype(BF)
            proj_low[half, 2, :, at] = grad_value.astype(BF)


def first_back_kernel(
    placed,
    count,
    slot_ref,
    core_ref,
    tokens,
    vectors,
    first_in,
    proj_low,
    qkv,
    grad_one,
    grad_attn,
    lines,
    head_lines,
    grad_hidden,
    input_grad,
    *rest,
):
    if placed:
        qkv_grad, first_lines = rest
    else:
        outs, small, sums = rest[:2], rest[2], rest[3]
        rows = D // count
        part = rows // 2
    turned_first = first_in[...].T
    grad_first = jnp.zeros((SEQ, D), F32)
    for half in range(2):
        for kind in range(3):
            grad_first = grad_first + dot_nt(proj_low[half, kind], qkv[half, kind])
            grad_qkv = dot_nn(turned_first, proj_low[half, kind]).astype(BF)
            if placed:
                qkv_grad[half, kind] = grad_qkv
                continue
            for index in range(count):
                outs[half][slot_ref[half, index], kind * rows : (kind + 1) * rows, :] = grad_qkv[
                    index * rows : (index + 1) * rows, :
                ]
    normed, inv_std = norm_parts(own_rows(tokens, core_ref).astype(F32))
    gain_one, shift_one = column_sum(grad_first * normed), column_sum(grad_first)
    input_grad[...] = grad_one[...] + norm_back(grad_first, normed, inv_std, vectors[0:1, :])
    if placed:
        first_lines[0:1, :], first_lines[1:2, :] = gain_one, shift_one
        return
    sums[0:1, :], sums[1:2, :] = gain_one, shift_one
    sums[2:6, :] = lines[0:4, :]
    small[...] = jnp.zeros_like(small)
    for half in range(2):
        whole = grad_attn[half].astype(F32)
        for index in range(count):
            block, start = (1 - half) * 2 + index // (count // 2), (index % (count // 2)) * 2 * rows
            slot = slot_ref[half, index]
            piece = whole[index * part : (index + 1) * part, :]
            piece = jnp.concatenate([piece[:, :HALF], piece[:, HALF:]], axis=0)
            outs[half][slot, 3 * rows : 4 * rows, :] = piece.astype(BF)
            small[0:6, :rows] = sums[0:6, index * rows : (index + 1) * rows]
            small[6:8, :part] = head_lines[half, :, index * part : (index + 1) * part]
            small[8:9, : 2 * rows] = grad_hidden[block, :, start : start + 2 * rows]
            outs[half][slot, 4 * rows :, :] = small[...].astype(BF)


def close_kernel(rows, total_down, total_up, kept, got, total, squares):
    value = kept[...] + got[...].astype(F32)
    total[...] = value
    part = jnp.sum(total_down[...] * total_down[...]) + jnp.sum(total_up[...] * total_up[...])
    row = lax.broadcasted_iota(jnp.int32, value.shape, 0)
    weight = jnp.where((row >= 4 * rows) & (row < 4 * rows + 6), 0.5, 1.0)
    part = part + jnp.sum(value * value * weight)
    squares[...] = jnp.full(squares.shape, part, F32)


def adam_step(gradient, master, first, second, average, factor, decay_rate, step_rate):
    clipped = gradient * factor
    first_new = BETA_ONE * first + (1.0 - BETA_ONE) * clipped
    second_new = BETA_TWO * second + (1.0 - BETA_TWO) * clipped * clipped
    first_hat = first_new / (1.0 - BETA_ONE**STEP)
    second_hat = second_new / (1.0 - BETA_TWO**STEP)
    master_new = master - step_rate * (
        first_hat / (jnp.sqrt(second_hat) + ADAM_EPS) + decay_rate * master
    )
    average_new = EMA_RATE * average + (1.0 - EMA_RATE) * master_new
    return (first_new, second_new, master_new, average_new)


def update_kernel(rows, spread, total_down, total_up, total, *rest):
    state, norm, results = rest[:28], rest[28], rest[29:]
    grad_norm = jnp.sqrt(jnp.sum(spread[...], axis=0))[0:1, 0:1]
    norm[...] = jnp.broadcast_to(grad_norm, norm.shape)
    factor = CLIP_NORM / jnp.maximum(grad_norm, CLIP_NORM)
    part = rows // 2

    def apply(index, at, gradient):
        decay, rate = (WEIGHT_DECAY, LEARN_RATE) if index < 4 else (0.0, VECTOR_RATE)
        values = adam_step(
            gradient, *[state[4 * index + k][at] for k in range(4)], factor, decay, rate
        )
        for k in range(4):
            results[4 * index + k][at] = values[k]

    for kind in range(3):
        apply(0, (kind,), total[kind * rows : (kind + 1) * rows, :])
    for side in range(2):
        start = 3 * rows + side * part
        columns = slice(side * HALF, (side + 1) * HALF)
        apply(1, (slice(None), columns), total[start : start + part, :])
        columns = slice(side * D, (side + 1) * D)
        apply(2, (slice(None), columns), total_up[side * rows : (side + 1) * rows, :])
    every = (slice(None), slice(None))
    apply(3, every, total_down[...])
    apply(4, every, total[4 * rows + 6 : 4 * rows + 8, :part])
    apply(5, every, total[4 * rows + 8 : 4 * rows + 9, : 2 * rows])
    apply(6, every, total[4 * rows : 4 * rows + 6, :rows])


def vmem(*shapes):
    return [pltpu.VMEM(shape, dtype) for shape, dtype in shapes]


def shape(dims, dtype):
    return jax.ShapeDtypeStruct(dims, dtype)


def whole_spec(dims):
    return pl.BlockSpec(dims, lambda *_: (0,) * len(dims))


VECTOR = pl.BlockSpec(memory_space=pltpu.VMEM)
SCALAR = pl.BlockSpec(memory_space=pltpu.SMEM)
ANYWHERE = pl.BlockSpec(memory_space=pl.ANY)


def call(body, name, args, specs, outs, scratch, mib, cost, streamed=False):
    flops, touched, special = cost
    if streamed:
        more = {
            "grid": (1,),
            "in_specs": [whole_spec(one.shape) for one in args],
            "out_specs": [whole_spec(one.shape) for one in outs],
        }
    else:
        more = {"in_specs": specs, "out_specs": [VECTOR] * len(outs)}
    return pl.pallas_call(
        body,
        out_shape=outs,
        scratch_shapes=scratch,
        compiler_params=pltpu.CompilerParams(vmem_limit_bytes=mib << 20),
        cost_estimate=pl.CostEstimate(
            flops=flops, bytes_accessed=touched, transcendentals=special
        ),
        name=name,
        **more,
    )(*args)


def both_halves(own, core):
    other = swap_cores(own)
    first = jnp.where(core == 0, own, other)
    second = jnp.where(core == 0, other, own)
    return jnp.concatenate([first, second], axis=0)


def body(force_plain, *args):
    (tokens, cotangent, seg_lengths, pad_counts) = args[:4]
    groups = [args[4 + 4 * i : 8 + 4 * i] for i in range(7)]
    qkv_w, attn_w, up_w, down_w, head_w, hidden_w, vector_w = (group[0] for group in groups)
    rows = qkv_w.shape[1]
    part = rows // 2
    count = D // rows
    placed = bool(rows % 16) or force_plain
    here, core = lax.axis_index("dp"), lax.axis_index("mp")
    slot = jnp.stack([slots(count, here, core), slots(count, here, 1 - core)], axis=0)
    core_at = core.reshape(1).astype(jnp.int32)

    packed = [shape((4 * rows + 16, HALF), BF), shape((2, rows, D), BF), shape((2 * rows, D), BF)]
    pack_args = (qkv_w, attn_w, up_w, down_w, head_w, hidden_w.reshape(1, -1), vector_w)
    piece, up_piece, down_piece = call(
        pack_kernel,
        "pack",
        pack_args,
        None,
        packed,
        vmem(((16, HALF), F32)),
        60,
        (1, 1_400_000, 0),
        True,
    )
    front_hops, up_hops, down_hops = (
        Gatherer(one, count) for one in (piece, up_piece, down_piece)
    )
    high = len(front_hops.bits) - 2
    front_hops.take(front_hops.send())
    for _ in range(high):
        front_got, up_got = front_hops.send(), up_hops.send(front_hops.held)
        _, front_got, up_got = join((), front_got, up_got)
        front_hops.take(front_got)
        up_hops.take(up_got)
    front_got, up_got = front_hops.send(), up_hops.send()
    for _ in range(high):
        down_hops.take(down_hops.send(up_hops.held))
    _, front_got, up_got, down_hops.held = join((), front_got, up_got, down_hops.held)
    front_hops.take(front_got)
    up_hops.take(up_got)
    front_parts, up_hops.held, down_hops.held = join(
        front_hops.parts(), up_hops.held, down_hops.held
    )
    up_got, down_got = up_hops.send(), down_hops.send()

    lengths = lax.dynamic_index_in_dim(seg_lengths, core, 0, keepdims=False)
    padding = lax.dynamic_index_in_dim(pad_counts, core, 0, keepdims=False)
    upto = jnp.arange(lengths.shape[0])[:, None] >= jnp.arange(lengths.shape[0])[None, :]
    bounds = jnp.sum(jnp.where(upto, lengths[None, :], 0), axis=1)
    position = jnp.arange(SEQ, dtype=jnp.int32)
    row_code = jnp.sum((position[None, :] >= bounds[:, None]).astype(jnp.int32), axis=0)[None, :]
    key_code = jnp.sum((position[:, None] >= bounds[None, :]).astype(jnp.int32), axis=1)[:, None]
    key_code = jnp.where(position[:, None] >= SEQ - padding, -1, key_code)

    qkv_shape, attn_shape = (2, 3, D, HALF), (2, HALF, D)
    front_outs = [
        shape((SEQ, D), BF),
        shape((2, 3, SEQ, HALF), BF),
        shape((2 * HALF // HD, SEQ), F32),
        shape((SEQ, D), BF),
        shape((SEQ, D), F32),
        shape((SEQ, D), BF),
    ]
    scratch = vmem(((SEQ, SEQ), F32))
    if placed:
        picks = [
            (slot[half][:, None] == jnp.arange(count, dtype=jnp.int32)[None, :]).astype(BF)
            for half in range(2)
        ]

        def spread(parts):
            return [
                reorder(jnp.concatenate(parts[2 * half : 2 * half + 2], axis=0), picks[half])
                for half in range(2)
            ]

        both = spread(front_parts)
        tails = [one[:, 4 * rows :].astype(F32) for one in both]
        vectors = jnp.pad(tails[0][:, :6, :rows].transpose(1, 0, 2).reshape(6, D), ((0, 2), (0, 0)))
        heads = jnp.stack(
            [one[:, 6:8, :part].transpose(1, 0, 2).reshape(2, HALF) for one in tails], axis=0
        )
        hidden = jnp.concatenate(
            [one[:, 8, : 2 * rows].reshape(2, 1, D) for one in (tails[1], tails[0])], axis=0
        )
        qkv_all = jnp.stack(
            [
                one[:, : 3 * rows]
                .reshape(count, 3, rows, HALF)
                .transpose(1, 0, 2, 3)
                .reshape(3, D, HALF)
                for one in both
            ],
            axis=0,
        )
        attn_all = jnp.stack(
            [
                one[:, 3 * rows : 4 * rows]
                .reshape(count, 2, part, HALF)
                .transpose(0, 2, 1, 3)
                .reshape(HALF, D)
                for one in both
            ],
            axis=0,
        )
        more = (vectors, heads, qkv_all, attn_all)
        more_specs = [VECTOR] * 4
    else:
        more = front_parts
        more_specs = [ANYWHERE] * 4
        extra = [
            shape((8, D), F32),
            shape((2, 2, HALF), F32),
            shape((4, 1, D), F32),
        ]
        front_outs += extra + [shape(qkv_shape, BF), shape(attn_shape, BF)]
        scratch += vmem(((2, count, rows + 16, HALF), BF)) + [pltpu.SemaphoreType.DMA((4,))]
    done = call(
        functools.partial(front_kernel, placed, count, rows),
        "front",
        (slot, core_at, tokens, row_code, key_code) + tuple(more),
        [SCALAR] * 2 + [VECTOR] * 3 + more_specs,
        front_outs,
        scratch,
        16,
        (6_000_000_000, 16_000_000, 3_200_000),
    )
    done, up_got, down_got = join(done, up_got, down_got)
    up_hops.take(up_got)
    up_parts = up_hops.parts()
    down_hops.take(down_got)
    down_got = down_hops.send()
    first_in, proj, log_total, mixed, hidden_one, second_in = done[:6]
    if not placed:
        vectors, heads, hidden, qkv_all, attn_all = done[6:]

    blocks = shape((4, SEQ, D), BF)
    pieces = shape((count, 2 * rows, D), BF)
    square_blocks = shape((4, D, D), BF)
    if placed:
        both = spread(up_parts)
        up_all = jnp.concatenate(
            [
                one.reshape(count, 2, rows, D).transpose(1, 0, 2, 3).reshape(2, D, D)
                for one in (both[1], both[0])
            ],
            axis=0,
        )
        more, more_specs = (up_all,), [VECTOR]
        outs = [blocks, blocks, square_blocks]
        scratch = vmem(((SEQ, D), BF))
    else:
        more, more_specs = up_parts, [ANYWHERE] * 4
        outs = [blocks, blocks, square_blocks, pieces, pieces]
        scratch = vmem(((SEQ, D), BF)) + [pltpu.SemaphoreType.DMA((2,))]
    done = call(
        functools.partial(up_kernel, placed, count),
        "up",
        (slot, core_at, pad_counts, second_in, cotangent, hidden) + tuple(more),
        [SCALAR] * 3 + [VECTOR] * 3 + more_specs,
        outs,
        scratch,
        12,
        (4_900_000_000, 20_000_000, 1_600_000),
    )
    done, down_got = join(done, down_got)
    down_hops.take(down_got)
    down_parts = down_hops.parts()
    act, slope = done[:2]
    turned = [pick.T for pick in picks] if placed else None
    if placed:
        down_own, down_other = (
            reorder(done[2][2 * start : 2 * start + 2].reshape(count, 2 * rows, D), turned[half])
            for half, start in ((0, 1), (1, 0))
        )
    else:
        up_all, down_own, down_other = done[2:]
    down_sum = Reducer(down_own, down_other, count)
    down_got = down_sum.send()

    if placed:
        both = spread(down_parts)
        down_all = jnp.concatenate([one.reshape(2, D, D) for one in (both[1], both[0])], axis=0)
        more, more_specs = (down_all,), [VECTOR]
    else:
        more, more_specs = down_parts, [ANYWHERE] * 4
    outs = [shape((SEQ, D), BF), shape((SEQ, D), F32), shape((4, 1, D), F32)]
    scratch = vmem(((SEQ, D), BF), ((D, SEQ), BF), ((SEQ, D), F32))
    if placed:
        outs += [square_blocks]
    else:
        outs += [pieces, pieces]
        scratch += vmem(((4, D, D), BF)) + [pltpu.SemaphoreType.DMA((4,))]
    done = call(
        functools.partial(down_kernel, placed, count),
        "down",
        (slot, core_at, pad_counts, second_in, hidden_one, cotangent, vectors, act, slope, up_all)
        + tuple(more),
        [SCALAR] * 3 + [VECTOR] * 7 + more_specs,
        outs,
        scratch,
        20,
        (9_700_000_000, 24_000_000, 0),
    )
    done, down_got = join(done, down_got)
    layer_half, grad_second, grad_hidden = done[:3]
    layer_output = both_halves(layer_half, core)
    if placed:

        def up_pieces(value, half):
            value = value.reshape(2, count, rows, D).transpose(1, 0, 2, 3)
            return reorder(value.reshape(count, 2 * rows, D), turned[half])

        up_own, up_other = up_pieces(done[3][2:], 0), up_pieces(done[3][:2], 1)
    else:
        up_own, up_other = done[3:]
    up_sum = Reducer(up_own, up_other, count)
    down_sum.take(down_got)
    down_got, up_got = down_sum.send(), up_sum.send()

    outs = [
        shape((SEQ, D), F32),
        shape((2, 3, SEQ, HALF), BF),
        shape(attn_shape, BF),
        shape((8, D), F32),
        shape((2, 2, HALF), F32),
    ]
    done = call(
        attend_back_kernel,
        "attend_back",
        (
            core_at,
            pad_counts,
            cotangent,
            vectors,
            row_code,
            key_code,
            grad_second,
            hidden_one,
            proj,
            log_total,
            mixed,
            attn_all,
        ),
        [SCALAR] * 2 + [VECTOR] * 10,
        outs,
        vmem(((SEQ, SEQ), F32)),
        14,
        (6_400_000_000, 16_000_000, 3_200_000),
    )
    done, down_got, up_got = join(done, down_got, up_got)
    grad_one, proj_low, grad_attn, lines, head_lines = done
    down_sum.take(down_got)
    up_sum.take(up_got)
    down_got, up_got = down_sum.send(), up_sum.send()
    if placed:
        outs = [shape((SEQ, D), F32), shape(qkv_shape, BF), shape((8, D), F32)]
        scratch = []
    else:
        outs = [shape((SEQ, D), F32)] + [shape((count, 4 * rows + 16, HALF), BF)] * 2
        scratch = vmem(((16, HALF), F32), ((8, D), F32))
    done = call(
        functools.partial(first_back_kernel, placed, count),
        "first_back",
        (
            slot,
            core_at,
            tokens,
            vectors,
            first_in,
            proj_low,
            qkv_all,
            grad_one,
            grad_attn,
            lines,
            head_lines,
            grad_hidden,
        ),
        [SCALAR] * 2 + [VECTOR] * 10,
        outs,
        scratch,
        14,
        (3_700_000_000, 18_000_000, 0),
    )
    done, down_got, up_got = join(done, down_got, up_got)
    down_sum.take(down_got)
    up_sum.take(up_got)
    input_grad = both_halves(done[0], core)
    if placed:
        whole_lines = jnp.concatenate([done[2][:2], lines[:4]], axis=0)
        sent = []
        for half in range(2):
            qkv_part = (
                done[1][half]
                .reshape(3, count, rows, HALF)
                .transpose(1, 0, 2, 3)
                .reshape(count, 3 * rows, HALF)
            )
            attn_part = (
                grad_attn[half]
                .reshape(count, part, 2, HALF)
                .transpose(0, 2, 1, 3)
                .reshape(count, rows, HALF)
            )
            start = (1 - half) * 2

            def widen(value):
                return jnp.pad(value, ((0, 0), (0, 0), (0, HALF - value.shape[2])))

            small = jnp.concatenate(
                [
                    widen(whole_lines.reshape(6, count, rows).transpose(1, 0, 2)),
                    widen(head_lines[half].reshape(2, count, part).transpose(1, 0, 2)),
                    widen(grad_hidden[start : start + 2].reshape(count, 1, 2 * rows)),
                    jnp.zeros((count, 7, HALF), F32),
                ],
                axis=1,
            ).astype(BF)
            sent.append(reorder(jnp.concatenate([qkv_part, attn_part, small], axis=1), turned[half]))
        front_own, front_other = sent
    else:
        front_own, front_other = done[1:]
    front_sum = Reducer(front_own, front_other, count)

    kept, got = down_sum.finish()
    total_down = kept + got.astype(F32)
    kept, got = up_sum.finish()
    total_up = kept + got.astype(F32)
    kept, got = front_sum.finish()
    outs = [shape(kept.shape, F32), shape((2 * count, 8, 128), F32)]
    close_args = (total_down, total_up, kept, got)
    total, squares = call(
        functools.partial(close_kernel, rows),
        "close",
        close_args,
        [VECTOR] * 4,
        outs,
        [],
        16,
        (1_000_000, 1_200_000, 0),
    )
    spread_squares = lax.all_to_all(squares, BOTH, 0, 0, tiled=True)
    state = []
    for index, group in enumerate(groups):
        state += [one.reshape(1, -1) if index == 5 else one for one in group]
    update_args = (spread_squares, total_down, total_up, total) + tuple(state)
    outs = [shape((8, 128), F32)] + [shape(one.shape, F32) for one in state]
    results = call(
        functools.partial(update_kernel, rows),
        "update",
        update_args,
        None,
        outs,
        [],
        60,
        (5_000_000, 8_000_000, 500_000),
        True,
    )
    grad_norm = results[0][0, 0]
    results = [
        one.reshape(-1) if 20 <= index < 24 else one for index, one in enumerate(results[1:])
    ]
    return (layer_output, input_grad, grad_norm, *results)


FORCE_PLAIN = False


def solution(mesh):
    row, late, wide = P("dp", None), P(("mp", "dp"), None), P("dp", "mp")
    kinds = (
        P(None, "dp", "mp"),
        late,
        wide,
        late,
        P(None, ("mp", "dp")),
        P(("mp", "dp")),
        P(None, "dp"),
    )
    per_parameter = tuple(kind for kind in kinds for _ in range(4))
    return jax.shard_map(
        functools.partial(body, FORCE_PLAIN),
        mesh=mesh,
        in_specs=(row, row, row, P("dp")) + per_parameter,
        out_specs=(row, row, P()) + per_parameter,
        check_vma=False,
    )
```

```python
import functools

import jax
import jax.numpy as jnp
from jax import lax
from jax.experimental import pallas as pl
from jax.experimental.pallas import tpu as pltpu
from jax.sharding import PartitionSpec as P

HD = 64
PAIR = 128
SEQ = 512
D = 768
HALF = 384
STEP = 7
SMALL = 32

NORM_EPS = 1e-05
SCORE_SCALE = 0.125
LEARN_RATE = 0.03
VECTOR_RATE = 0.4
BETA_ONE = 0.9
BETA_TWO = 0.95
ADAM_EPS = 1e-08
WEIGHT_DECAY = 0.1
EMA_RATE = 0.8
CLIP_NORM = 1.0
GELU_COEF = 0.7978845608028654
GELU_CUBE = 0.044715
MASKED = -1e30

BF = jnp.bfloat16
F32 = jnp.float32
BOTH = ("dp", "mp")


def dot_nn(left, right):
    return lax.dot_general(left, right, (((1,), (0,)), ((), ())), preferred_element_type=F32)


def dot_nt(left, right):
    return lax.dot_general(left, right, (((1,), (1,)), ((), ())), preferred_element_type=F32)


def dot_tn(left, right):
    return lax.dot_general(left, right, (((0,), (0,)), ((), ())), preferred_element_type=F32)


def norm_parts(rows):
    row_mean = jnp.mean(rows, axis=1, keepdims=True)
    centered = rows - row_mean
    inv_std = lax.rsqrt(jnp.mean(centered * centered, axis=1, keepdims=True) + NORM_EPS)
    return (centered * inv_std, inv_std)


def norm_back(grad_in, normed, inv_std, gain):
    scaled = grad_in * gain
    return inv_std * (
        scaled
        - jnp.mean(scaled, axis=1, keepdims=True)
        - normed * jnp.mean(scaled * normed, axis=1, keepdims=True)
    )


def column_sum(value):
    return jnp.sum(value, axis=0, keepdims=True)


def step_bits(count):
    length = count.bit_length() - 1
    high = [(bit, bit) for bit in reversed(range(2, length))]
    return high + [(0, 1), (1, 0)]


def step_pairs(count, bits):
    return [
        (index * 2 + core, (index ^ (1 << bits[core])) * 2 + core)
        for index in range(count)
        for core in range(2)
    ]


def slots(count, here, core):
    length = count.bit_length() - 1
    apart = jnp.arange(count, dtype=jnp.int32) ^ here
    low, mid = apart & 1, (apart >> 1) & 1
    first = jnp.where(core == 0, mid, low)
    second = jnp.where(core == 0, low, mid)
    place = (first << (length - 1)) | (second << (length - 2))
    for bit in range(2, length):
        place = place | (((apart >> bit) & 1) << (length - 1 - bit))
    return place


def reorder(value, pick):
    flat = dot_nn(pick, value.reshape(value.shape[0], -1)).astype(BF)
    return flat.reshape(value.shape)


def swap_cores(value):
    return lax.ppermute(value, "mp", [(0, 1), (1, 0)])


def after(value, *others):
    return lax.optimization_barrier((value,) + others)[0]


def join(made, *gots):
    joined = lax.optimization_barrier(tuple(made) + gots)
    return (list(joined[: len(made)]), *joined[len(made) :])


class Gatherer:
    def __init__(self, piece, count):
        self.count, self.held, self.got = count, piece[None], None
        self.bits = step_bits(count)

    def send(self, *others):
        if others:
            self.held = after(self.held, *others)
        return lax.ppermute(self.held, BOTH, step_pairs(self.count, self.bits.pop(0)))

    def take(self, got):
        if self.bits:
            self.held = jnp.concatenate([self.held, got], axis=0)
        else:
            self.got = got


class Reducer:
    def __init__(self, own, got, count):
        self.count = count
        self.bits = list(reversed(step_bits(count)))
        half, self.half = count // 2, count // 4
        if not isinstance(own, tuple):
            own, got = (own[:half], own[half:]), (got[:half], got[half:])
        self.keep(own[0], got[0])
        sent = own[1].astype(F32) + got[1].astype(F32)
        self.low, self.high = sent[: self.half].astype(BF), sent[self.half :].astype(BF)
        self.pairs = step_pairs(count, self.bits.pop(0))

    def keep(self, own, got):
        self.kept = own.astype(F32) + got.astype(F32)

    def send_high(self):
        return lax.ppermute(self.high, BOTH, self.pairs)

    def send_low(self, *others):
        return lax.ppermute(after(self.low, *others), BOTH, self.pairs)

    def take_high(self, got):
        self.sent = (self.kept[self.half :] + got.astype(F32)).astype(BF)

    def take_low(self, got):
        self.kept = self.kept[: self.half] + got.astype(F32)

    def send(self):
        return lax.ppermute(self.sent, BOTH, step_pairs(self.count, self.bits.pop(0)))

    def take(self, got):
        self.half //= 2
        total = self.kept + got.astype(F32)
        self.kept, self.sent = total[: self.half], total[self.half :].astype(BF)

    def finish(self):
        while len(self.bits) > 1:
            self.take(self.send())
        return (self.kept[0], self.send()[0])


def fetch(slot, held, got, send):
    half = held.shape[0]

    @pl.when(slot < half)
    def _():
        send(held.at[slot])

    @pl.when(slot >= half)
    def _():
        send(got.at[slot - half])


def drain(ref, sem):
    pltpu.make_async_copy(ref, ref, sem).wait()


def pack_kernel(qkv_w, attn_w, up_w, down_w, head_w, hidden_w, vector_w, piece, up, down, small):
    rows = qkv_w.shape[1]
    part = rows // 2
    for kind in range(3):
        piece[kind * rows : (kind + 1) * rows, :] = qkv_w[kind].astype(BF)
    both = jnp.concatenate([attn_w[:, :HALF], attn_w[:, HALF:]], axis=0)
    piece[3 * rows : 3 * rows + 2 * part, :] = both.astype(BF)
    small[...] = jnp.zeros_like(small)
    small[0:6, :rows] = vector_w[...]
    small[6:8, :part] = head_w[...]
    small[8:9, : 2 * rows] = hidden_w[...]
    piece[4 * rows :, :] = small[...].astype(BF)
    up[0] = up_w[:, :D].astype(BF)
    up[1] = up_w[:, D:].astype(BF)
    down[...] = down_w[...].astype(BF)


def prepare_kernel(
    core_ref, pads_ref, tokens, cotangent, row_code, key_code, x_out, normed_out, inv_out, low_grad, bias, buffer, sem
):
    at = pl.ds(pl.multiple_of(core_ref[0] * SEQ, SEQ), SEQ)
    copies = [
        pltpu.make_async_copy(tokens.at[at], x_out, sem.at[0]),
        pltpu.make_async_copy(cotangent.at[at], buffer, sem.at[1]),
    ]
    for copy in copies:
        copy.start()
    key_at = lax.broadcasted_iota(jnp.int32, (SEQ, SEQ), 0)
    row_at = lax.broadcasted_iota(jnp.int32, (SEQ, SEQ), 1)
    seen = (key_code[...] == row_code[...]) | (key_at == row_at)
    bias[...] = jnp.where(seen, 0.0, MASKED)
    copies[0].wait()
    normed, inv_std = norm_parts(x_out[...].astype(F32))
    normed_out[...], inv_out[...] = normed, inv_std
    copies[1].wait()
    position = lax.broadcasted_iota(jnp.int32, (SEQ, D), 0)
    kept = position < SEQ - pads_ref[core_ref[0]]
    low_grad[...] = jnp.where(kept, buffer[...].astype(F32), 0.0).astype(BF)


def attend(proj, bias, log_total, mixed):
    lane = lax.broadcasted_iota(jnp.int32, (SEQ, PAIR), 1)
    for pair in range(HALF // PAIR):
        at = slice(pair * PAIR, (pair + 1) * PAIR)
        q_pair, k_pair, v_pair = proj[0, :, at], proj[1, :, at], proj[2, :, at]
        v_turned = v_pair.T
        turned = []
        for side in range(2):
            mine = (lane < HD) if side == 0 else (lane >= HD)
            q_side = jnp.where(mine, q_pair, jnp.zeros_like(q_pair))
            scores = dot_nt(k_pair, q_side) + bias[...]
            top = jnp.max(scores, axis=0, keepdims=True)
            exponent = jnp.exp(scores - top)
            total = jnp.sum(exponent, axis=0, keepdims=True)
            index = pair * 2 + side
            log_total[index : index + 1, :] = top + jnp.log(total)
            part = dot_nn(v_turned[side * HD : (side + 1) * HD], exponent.astype(BF))
            turned.append(part * (1.0 / total))
        mixed[:, at] = jnp.concatenate(turned, axis=0).T.astype(BF)


def front_kernel(placed, half, count, rows, slot_ref, *rest):
    rest = list(rest)
    take = lambda amount: [rest.pop(0) for _ in range(amount)]
    if half == 0:
        x, normed, bias = take(3)
        if placed:
            (vectors,) = take(1)
    else:
        first_in, before, bias, vectors = take(4)
    if placed:
        heads, qkv, attn = take(3)
    else:
        parts = take(2)
    if half == 0:
        first_in, after_out = take(2)
    else:
        after_out, second_in, turned_in = take(3)
    proj, log_total, mixed = take(3)
    if not placed:
        if half == 0:
            (vectors,) = take(1)
        heads, hidden, qkv, attn, stage, sem = take(6)
        part = rows // 2

        def place(index, carry):
            down = pl.ds(pl.multiple_of(index * rows, 16), rows)

            def send(src):
                pltpu.make_async_copy(src.at[3 * rows :], stage.at[index], sem.at[1]).start()
                for kind in range(3):
                    pltpu.make_async_copy(
                        src.at[kind * rows : (kind + 1) * rows], qkv.at[kind, down], sem.at[0]
                    ).start()

            fetch(slot_ref[half, index], parts[0], parts[1], send)
            return carry

        lax.fori_loop(0, count, place, 0)
        drain(stage, sem.at[1])
        for index in range(count):
            tail = stage[index, rows:, :].astype(F32)
            if half == 0:
                vectors[0:6, index * rows : (index + 1) * rows] = tail[0:6, :rows]
            heads[:, index * part : (index + 1) * part] = tail[6:8, :part]
            start = (index % (count // 2)) * 2 * rows
            hidden[index // (count // 2), :, start : start + 2 * rows] = tail[8:9, : 2 * rows]
        for index in range(0, count, 2):
            two = [stage[index + k, :rows, :].astype(F32) for k in range(2)]
            at = slice(index * part, (index + 2) * part)
            left = jnp.concatenate([one[:part] for one in two], axis=0)
            right = jnp.concatenate([one[part:] for one in two], axis=0)
            attn[at, :HALF] = left.astype(BF)
            attn[at, HALF:] = right.astype(BF)
    if half == 0:
        first_in[...] = (normed[...] * vectors[0:1, :] + vectors[1:2, :]).astype(BF)
    if not placed:
        drain(qkv, sem.at[0])
    value = dot_nn(first_in[...], qkv[0]) + heads[0:1, :]
    proj[0] = (value.astype(BF).astype(F32) * SCORE_SCALE).astype(BF)
    proj[1] = dot_nn(first_in[...], qkv[1]).astype(BF)
    proj[2] = (dot_nn(first_in[...], qkv[2]) + heads[1:2, :]).astype(BF)
    attend(proj, bias, log_total, mixed)
    value = dot_nn(mixed[...], attn[...])
    if half == 0:
        after_out[...] = x[...].astype(F32) + value + vectors[4:5, :]
        return
    value = before[...] + value
    after_out[...] = value
    normed, _ = norm_parts(value)
    entered = (normed * vectors[2:3, :] + vectors[3:4, :]).astype(BF)
    second_in[...] = entered
    turned_in[...] = entered.T


def up_kernel(placed, half, count, slot_ref, second_in, low_grad, bias, *rest):
    rows = D // count
    if placed:
        up, act, slope, grad_down = rest
    else:
        held, got, act, slope, up, grad_kept, grad_sent, sem = rest

        def place(index, carry):
            down = pl.ds(pl.multiple_of(index * rows, 16), rows)

            def send(src):
                pltpu.make_async_copy(src, up.at[:, down], sem).start()

            fetch(slot_ref[half, index], held, got, send)
            return carry

        lax.fori_loop(0, count, place, 0)
        drain(up, sem)
    chunk_rows = 256
    for block in range(2):
        for chunk in range(SEQ // chunk_rows):
            at = slice(chunk * chunk_rows, (chunk + 1) * chunk_rows)
            pre = dot_nn(second_in[at, :], up[block]) + bias[block]
            square = pre * pre
            bent = jnp.tanh(pre * (GELU_COEF + GELU_COEF * GELU_CUBE * square))
            half_up = 0.5 + 0.5 * bent
            gelu = pre * half_up
            act[block, at, :] = gelu.astype(BF)
            inner = pre * (2.0 * GELU_COEF + 6.0 * GELU_COEF * GELU_CUBE * square)
            slope[block, at, :] = (half_up + half_up * (inner - half_up * inner)).astype(BF)
        grad = dot_tn(act[block], low_grad[...]).astype(BF)
        if placed:
            grad_down[block] = grad
            continue
        for index in range(count // 2):
            piece = grad[index * 2 * rows : (index + 1) * 2 * rows, :]
            slot = slot_ref[half, block * (count // 2) + index]

            @pl.when(slot < count // 2)
            def _(slot=slot, piece=piece):
                grad_kept[slot] = piece

            @pl.when(slot >= count // 2)
            def _(slot=slot, piece=piece):
                grad_sent[slot - count // 2] = piece


def down_kernel(
    placed, half, count, slot_ref, turned_in, low_grad, vectors, act, slope, up, before_out, *rest
):
    rows = D // count
    rest = list(rest)
    take = lambda amount: [rest.pop(0) for _ in range(amount)]
    if half == 0:
        (before_grad,) = take(1)
    if placed:
        down, out, grad_second, grad_hidden, grad_up = rest
    else:
        held, got, out, grad_second, grad_hidden, grad_up, down, sem = rest

        def place(index, carry):
            block = index // (count // 2)
            start = pl.multiple_of(lax.rem(index, count // 2) * 2 * rows, 16)

            def send(src):
                pltpu.make_async_copy(
                    src, down.at[block, pl.ds(start, 2 * rows)], sem.at[block]
                ).start()

            fetch(slot_ref[half, index], held, got, send)
            return carry

        lax.fori_loop(0, count, place, 0)
    parts_out, parts_grad = [], []
    for block in range(2):
        if not placed:
            drain(down.at[block], sem.at[block])
        grad_pre = dot_nt(low_grad[...], down[block]) * slope[block].astype(F32)
        grad_hidden[block] = column_sum(grad_pre)
        pre_low = grad_pre.astype(BF)
        grad = dot_nn(turned_in[...], pre_low).astype(BF)
        part_out = dot_nn(act[block], down[block])
        part_grad = dot_nt(pre_low, up[block])
        if half == 1 and block == 0:
            out[...] = before_out[...] + vectors[5:6, :] + part_out
            grad_second[...] = part_grad
        elif half == 1:
            out[...] += part_out
            grad_second[...] += part_grad
        elif block == 0:
            parts_out.append(part_out)
            grad_second[...] = before_grad[...] + part_grad
        else:
            out[...] = (before_out[...] + (parts_out[0] + part_out)).astype(BF)
            grad_second[...] += part_grad
        if placed:
            grad_up[block] = grad
            continue
        for index in range(count):
            grad_up[slot_ref[half, index], block * rows : (block + 1) * rows, :] = grad[
                index * rows : (index + 1) * rows, :
            ]


def attend_back(proj, log_total, mixed, attn, bias, grad_low, proj_low, grad_attn, head_lines):
    lane = lax.broadcasted_iota(jnp.int32, (SEQ, PAIR), 1)
    grad_attn[...] = dot_tn(mixed[...], grad_low).astype(BF)
    grad_mixed = dot_nt(grad_low, attn[...]).astype(BF)
    for pair in range(HALF // PAIR):
        at = slice(pair * PAIR, (pair + 1) * PAIR)
        q_pair, k_pair, v_pair = proj[0, :, at], proj[1, :, at], proj[2, :, at]
        g_pair = grad_mixed[:, at]
        k_turned = k_pair.T
        grad_key = jnp.zeros((SEQ, PAIR), F32)
        grad_value = jnp.zeros((SEQ, PAIR), F32)
        turned = []
        for side in range(2):
            mine = (lane < HD) if side == 0 else (lane >= HD)
            q_side = jnp.where(mine, q_pair, jnp.zeros_like(q_pair))
            g_side = jnp.where(mine, g_pair, jnp.zeros_like(g_pair))
            index = pair * 2 + side
            scores = dot_nt(k_pair, q_side) + bias[...]
            probs = jnp.exp(scores - log_total[index : index + 1, :])
            grad_probs = dot_nt(v_pair, g_side)
            row_dot = column_sum(probs * grad_probs)
            grad_scores = (probs * (grad_probs - row_dot)).astype(BF)
            grad_value = grad_value + dot_nn(probs.astype(BF), g_side)
            grad_key = grad_key + dot_nn(grad_scores, q_side)
            turned.append(dot_nn(k_turned[side * HD : (side + 1) * HD], grad_scores))
        grad_query = jnp.concatenate(turned, axis=0).T * SCORE_SCALE
        head_lines[0:1, at] = column_sum(grad_query)
        head_lines[1:2, at] = column_sum(grad_value)
        proj_low[0, :, at] = grad_query.astype(BF)
        proj_low[1, :, at] = grad_key.astype(BF)
        proj_low[2, :, at] = grad_value.astype(BF)


def first_part(proj_low, qkv):
    total = dot_nt(proj_low[0], qkv[0])
    for kind in range(1, 3):
        total = total + dot_nt(proj_low[kind], qkv[kind])
    return total


def pieces_out(half, count, slot_ref, turned_first, proj_low, grad_attn, lines, head_lines, grad_hidden, out, small):
    rows = D // count
    part = rows // 2
    for kind in range(3):
        grad_qkv = dot_nn(turned_first[...], proj_low[kind]).astype(BF)
        for index in range(count):
            out[slot_ref[half, index], kind * rows : (kind + 1) * rows, :] = grad_qkv[
                index * rows : (index + 1) * rows, :
            ]
    small[...] = jnp.zeros_like(small)
    whole = grad_attn[...].astype(F32)
    for index in range(count):
        start = (index % (count // 2)) * 2 * rows
        slot = slot_ref[half, index]
        piece = whole[index * part : (index + 1) * part, :]
        piece = jnp.concatenate([piece[:, :HALF], piece[:, HALF:]], axis=0)
        out[slot, 3 * rows : 4 * rows, :] = piece.astype(BF)
        small[0:6, :rows] = lines[0:6, index * rows : (index + 1) * rows]
        small[6:8, :part] = head_lines[:, index * part : (index + 1) * part]
        small[8:9, : 2 * rows] = grad_hidden[index // (count // 2), :, start : start + 2 * rows]
        out[slot, 4 * rows :, :] = small[...].astype(BF)


def back_own_kernel(
    low_grad,
    vectors,
    grad_second,
    hidden_one,
    proj,
    log_total,
    mixed,
    attn,
    qkv,
    bias,
    grad_one_out,
    grad_low_out,
    proj_low,
    grad_attn,
    lines,
    head_lines,
    grad_first,
):
    grad_out = low_grad[...].astype(F32)
    normed, inv_std = norm_parts(hidden_one[...])
    grads = grad_second[...]
    lines[2:3, :], lines[3:4, :] = column_sum(grads * normed), column_sum(grads)
    grad_one = grad_out + norm_back(grads, normed, inv_std, vectors[2:3, :])
    grad_one_out[...] = grad_one
    lines[4:5, :], lines[5:6, :] = column_sum(grad_one), column_sum(grad_out)
    grad_low = grad_one.astype(BF)
    grad_low_out[...] = grad_low
    attend_back(proj, log_total, mixed, attn, bias, grad_low, proj_low, grad_attn, head_lines)
    grad_first[...] = first_part(proj_low, qkv)


def back_other_kernel(
    placed,
    count,
    slot_ref,
    grad_low,
    vectors,
    proj,
    log_total,
    mixed,
    attn,
    qkv,
    bias,
    before_first,
    grad_one,
    before_lines,
    normed,
    inv_std,
    first_in,
    grad_hidden,
    input_grad,
    turned_first,
    lines,
    *rest,
):
    if placed:
        proj_low, grad_attn, head_lines = rest
    else:
        out, proj_low, grad_attn, head_lines, small = rest
    attend_back(proj, log_total, mixed, attn, bias, grad_low[...], proj_low, grad_attn, head_lines)
    grad_first = before_first[...] + first_part(proj_low, qkv)
    lines[...] = before_lines[...]
    lines[0:1, :] = column_sum(grad_first * normed[...])
    lines[1:2, :] = column_sum(grad_first)
    back = norm_back(grad_first, normed[...], inv_std[...], vectors[0:1, :])
    input_grad[...] = grad_one[...] + back
    turned_first[...] = first_in[...].T
    if not placed:
        pieces_out(
            1, count, slot_ref, turned_first, proj_low, grad_attn, lines, head_lines, grad_hidden, out, small
        )


def pieces_kernel(count, slot_ref, turned_first, proj_low, grad_attn, lines, head_lines, grad_hidden, out, small):
    pieces_out(
        0, count, slot_ref, turned_first, proj_low, grad_attn, lines, head_lines, grad_hidden, out, small
    )


def close_kernel(rows, total_down, total_up, kept, got, total, squares):
    value = kept[...] + got[...].astype(F32)
    total[...] = value
    part = jnp.sum(total_down[...] * total_down[...]) + jnp.sum(total_up[...] * total_up[...])
    row = lax.broadcasted_iota(jnp.int32, value.shape, 0)
    weight = jnp.where((row >= 4 * rows) & (row < 4 * rows + 6), 0.5, 1.0)
    part = part + jnp.sum(value * value * weight)
    squares[...] = jnp.full(squares.shape, part, F32)


def adam_step(gradient, master, first, second, average, factor, decay_rate, step_rate):
    clipped = gradient * factor
    first_new = BETA_ONE * first + (1.0 - BETA_ONE) * clipped
    second_new = BETA_TWO * second + (1.0 - BETA_TWO) * clipped * clipped
    first_hat = first_new / (1.0 - BETA_ONE**STEP)
    second_hat = second_new / (1.0 - BETA_TWO**STEP)
    master_new = master - step_rate * (
        first_hat / (jnp.sqrt(second_hat) + ADAM_EPS) + decay_rate * master
    )
    average_new = EMA_RATE * average + (1.0 - EMA_RATE) * master_new
    return (first_new, second_new, master_new, average_new)


def update_kernel(rows, spread, total_down, total_up, total, *rest):
    state, norm, results = rest[:28], rest[28], rest[29:]
    grad_norm = jnp.sqrt(jnp.sum(spread[...], axis=0))[0:1, 0:1]
    norm[...] = grad_norm
    factor = CLIP_NORM / jnp.maximum(grad_norm, CLIP_NORM)
    part = rows // 2

    def apply(index, at, gradient):
        decay, rate = (WEIGHT_DECAY, LEARN_RATE) if index < 4 else (0.0, VECTOR_RATE)
        values = adam_step(
            gradient, *[state[4 * index + k][at] for k in range(4)], factor, decay, rate
        )
        for k in range(4):
            results[4 * index + k][at] = values[k]

    for kind in range(3):
        apply(0, (kind,), total[kind * rows : (kind + 1) * rows, :])
    for side in range(2):
        start = 3 * rows + side * part
        columns = slice(side * HALF, (side + 1) * HALF)
        apply(1, (slice(None), columns), total[start : start + part, :])
        columns = slice(side * D, (side + 1) * D)
        apply(2, (slice(None), columns), total_up[side * rows : (side + 1) * rows, :])
    every = (slice(None), slice(None))
    apply(3, every, total_down[...])
    apply(4, every, total[4 * rows + 6 : 4 * rows + 8, :part])
    apply(5, every, total[4 * rows + 8 : 4 * rows + 9, : 2 * rows])
    apply(6, every, total[4 * rows : 4 * rows + 6, :rows])


def vmem(*shapes):
    return [pltpu.VMEM(shape, dtype) for shape, dtype in shapes]


def shape(dims, dtype):
    return jax.ShapeDtypeStruct(dims, dtype)


def whole_spec(dims):
    return pl.BlockSpec(dims, lambda *_: (0,) * len(dims))


VECTOR = pl.BlockSpec(memory_space=pltpu.VMEM)
SCALAR = pl.BlockSpec(memory_space=pltpu.SMEM)
ANYWHERE = pl.BlockSpec(memory_space=pl.ANY)


def call(body, name, args, specs, outs, scratch, mib, cost, streamed=False):
    flops, touched, special = cost
    if streamed:
        more = {
            "grid": (1,),
            "in_specs": [whole_spec(one.shape) for one in args],
            "out_specs": [whole_spec(one.shape) for one in outs],
        }
    else:
        more = {"in_specs": specs, "out_specs": [VECTOR] * len(outs)}
    return pl.pallas_call(
        body,
        out_shape=outs,
        scratch_shapes=scratch,
        compiler_params=pltpu.CompilerParams(vmem_limit_bytes=mib << 20),
        cost_estimate=pl.CostEstimate(
            flops=flops, bytes_accessed=touched, transcendentals=special
        ),
        name=name,
        **more,
    )(*args)


def both_halves(own, core):
    other = swap_cores(own)
    first = jnp.where(core == 0, own, other)
    second = jnp.where(core == 0, other, own)
    return jnp.concatenate([first, second], axis=0)


def body(force_plain, *args):
    (tokens, cotangent, seg_lengths, pad_counts) = args[:4]
    groups = [args[4 + 4 * i : 8 + 4 * i] for i in range(7)]
    qkv_w, attn_w, up_w, down_w, head_w, hidden_w, vector_w = (group[0] for group in groups)
    rows = qkv_w.shape[1]
    part = rows // 2
    count = D // rows
    placed = bool(rows % 16) or force_plain
    here, core = lax.axis_index("dp"), lax.axis_index("mp")
    slot = jnp.stack([slots(count, here, core), slots(count, here, 1 - core)], axis=0)
    core_at = core.reshape(1).astype(jnp.int32)

    packed = [shape((4 * rows + 16, HALF), BF), shape((2, rows, D), BF), shape((2 * rows, D), BF)]
    pack_args = (qkv_w, attn_w, up_w, down_w, head_w, hidden_w.reshape(1, -1), vector_w)
    piece, up_piece, down_piece = call(
        pack_kernel,
        "pack",
        pack_args,
        None,
        packed,
        vmem(((16, HALF), F32)),
        60,
        (1, 1_400_000, 0),
        True,
    )
    front_hops, up_hops, down_hops = (
        Gatherer(one, count) for one in (piece, up_piece, down_piece)
    )
    lengths = lax.dynamic_index_in_dim(seg_lengths, core, 0, keepdims=False)
    padding = lax.dynamic_index_in_dim(pad_counts, core, 0, keepdims=False)
    upto = jnp.arange(lengths.shape[0])[:, None] >= jnp.arange(lengths.shape[0])[None, :]
    bounds = jnp.sum(jnp.where(upto, lengths[None, :], 0), axis=1)
    position = jnp.arange(SEQ, dtype=jnp.int32)
    row_code = jnp.sum((position[None, :] >= bounds[:, None]).astype(jnp.int32), axis=0)[None, :]
    key_code = jnp.sum((position[:, None] >= bounds[None, :]).astype(jnp.int32), axis=1)[:, None]
    key_code = jnp.where(position[:, None] >= SEQ - padding, -1, key_code)

    rows_bf, rows_f32 = shape((SEQ, D), BF), shape((SEQ, D), F32)
    half_bf = shape((SEQ, HALF), BF)

    high = len(front_hops.bits) - 2
    front_got = front_hops.send()
    prepared = call(
        prepare_kernel,
        "prepare",
        (core_at, pad_counts, tokens, cotangent, row_code, key_code),
        [SCALAR] * 2 + [ANYWHERE] * 2 + [VECTOR] * 2,
        [rows_bf, rows_f32, shape((SEQ, 1), F32), rows_bf, shape((SEQ, SEQ), F32)],
        vmem(((SEQ, D), BF)) + [pltpu.SemaphoreType.DMA((2,))],
        12,
        (3_000_000, 9_000_000, 0),
    )
    prepared, front_got, slot = join(prepared, front_got, slot)
    x_own, normed, inv_std, low_grad, bias = prepared
    front_hops.take(front_got)
    for _ in range(high):
        front_got, up_got = front_hops.send(), up_hops.send(front_hops.held)
        _, front_got, up_got = join((), front_got, up_got)
        front_hops.take(front_got)
        up_hops.take(up_got)
    front_got, up_got = front_hops.send(), up_hops.send()
    for _ in range(high):
        down_hops.take(down_hops.send(up_hops.held))
    front_swap = swap_cores(front_hops.held)
    _, front_got, up_got, front_swap, down_hops.held = join(
        (), front_got, up_got, front_swap, down_hops.held
    )
    up_hops.take(up_got)
    front_swap_got = swap_cores(front_got)
    up_got = up_hops.send()

    if placed:
        picks = [
            (slot[half][:, None] == jnp.arange(count, dtype=jnp.int32)[None, :]).astype(BF)
            for half in range(2)
        ]
        turned = [pick.T for pick in picks]

    def spread(held, got, half):
        return reorder(jnp.concatenate([held, got], axis=0), picks[half])

    def front_more(held, got, half):
        if not placed:
            return (), (held, got), [ANYWHERE] * 2
        one = spread(held, got, half)
        tail = one[:, 4 * rows :].astype(F32)
        vectors = tail[:, :6, :rows].transpose(1, 0, 2).reshape(6, D)
        heads = tail[:, 6:8, :part].transpose(1, 0, 2).reshape(2, HALF)
        hidden = tail[:, 8, : 2 * rows].reshape(2, 1, D)
        qkv = one[:, : 3 * rows].reshape(count, 3, rows, HALF).transpose(1, 0, 2, 3)
        attn = one[:, 3 * rows : 4 * rows].reshape(count, 2, part, HALF).transpose(0, 2, 1, 3)
        more = (heads, qkv.reshape(3, D, HALF), attn.reshape(HALF, D))
        return (jnp.pad(vectors, ((0, 2), (0, 0))), hidden), more, [VECTOR] * 3

    extra_outs = [
        shape((2, HALF), F32),
        shape((2, 1, D), F32),
        shape((3, D, HALF), BF),
        shape((HALF, D), BF),
    ]
    attend_outs = [shape((3, SEQ, HALF), BF), shape((HALF // HD, SEQ), F32), half_bf]
    stage_scratch = vmem(((count, rows + 16, HALF), BF)) + [pltpu.SemaphoreType.DMA((2,))]
    front_cost = (3_000_000_000, 9_000_000, 1_600_000)

    early, more, more_specs = front_more(front_hops.held, front_got, 0)
    done = call(
        functools.partial(front_kernel, placed, 0, count, rows),
        "front_own",
        (slot, x_own, normed, bias) + early[:1] + more,
        [SCALAR] + [VECTOR] * (3 + len(early[:1])) + more_specs,
        [rows_bf, rows_f32] + attend_outs + ([] if placed else [shape((8, D), F32)] + extra_outs),
        [] if placed else stage_scratch,
        12,
        front_cost,
    )
    done, front_swap_got, down_hops.held = join(done, front_swap_got, down_hops.held)
    first_in, before = done[:2]
    proj, log_total, mixed = [done[2]], [done[3]], [done[4]]
    if placed:
        vectors, hidden = early[0], [early[1]]
        qkv_all, attn_all = [more[1]], [more[2]]
    else:
        vectors, hidden = done[5], [done[7]]
        qkv_all, attn_all = [done[8]], [done[9]]
    down_got = down_hops.send()

    early, more, more_specs = front_more(front_swap, front_swap_got, 1)
    up_swap = swap_cores(up_hops.held)
    done = call(
        functools.partial(front_kernel, placed, 1, count, rows),
        "front_other",
        (slot, first_in, before, bias, vectors) + more,
        [SCALAR] + [VECTOR] * 4 + more_specs,
        [rows_f32, rows_bf, shape((D, SEQ), BF)] + attend_outs + ([] if placed else extra_outs),
        [] if placed else stage_scratch,
        12,
        front_cost,
    )
    done, up_got, down_got, up_swap = join(done, up_got, down_got, up_swap)
    hidden_one, second_in, turned_in = done[:3]
    proj.append(done[3])
    log_total.append(done[4])
    mixed.append(done[5])
    if placed:
        hidden.append(early[1])
        qkv_all.append(more[1])
        attn_all.append(more[2])
    else:
        hidden.append(done[7])
        qkv_all.append(done[8])
        attn_all.append(done[9])
    down_hops.take(down_got)
    down_got = down_hops.send()
    down_swap = swap_cores(down_hops.held)
    up_parts = [(up_hops.held, up_got), (up_swap, swap_cores(up_got))]

    blocks = shape((2, SEQ, D), BF)
    pieces = shape((count, 2 * rows, D), BF)
    squares_of = shape((2, D, D), BF)
    act, slope, up_all, down_grad = {}, {}, {}, {}
    for half in (1, 0):
        if placed:
            one = spread(*up_parts[half], half)
            up_all[half] = one.transpose(1, 0, 2, 3).reshape(2, D, D)
            more, more_specs, outs = (up_all[half],), [VECTOR], [blocks, blocks, squares_of]
        else:
            more, more_specs = up_parts[half], [ANYWHERE] * 2
            outs = [blocks, blocks, squares_of] + [shape((count // 2, 2 * rows, D), BF)] * 2
        done = call(
            functools.partial(up_kernel, placed, half, count),
            ("up_own", "up_other")[half],
            (slot, second_in, low_grad, hidden[half]) + tuple(more),
            [SCALAR] + [VECTOR] * 3 + more_specs,
            outs,
            [] if placed else [pltpu.SemaphoreType.DMA],
            8,
            (1_000_000_000, 4_000_000, 100_000),
        )
        if half == 1:
            done, down_swap = join(done, down_swap)
            second_in = after(second_in, done[0])
        else:
            done, down_got = join(done, down_got)
        act[half], slope[half] = done[:2]
        if placed:
            value = reorder(done[2].reshape(count, 2 * rows, D), turned[half])
            down_grad[half] = (value[: count // 2], value[count // 2 :])
        else:
            up_all[half], down_grad[half] = done[2], tuple(done[3:])
        if half == 1:
            swapped = tuple(swap_cores(one) for one in down_grad[1])
    down_sum = Reducer(down_grad[0], swapped, count)
    down_parts = [(down_hops.held, down_got), (down_swap, swap_cores(down_got))]
    high_got = down_sum.send_high()

    grad_hidden, up_grad = {}, {}
    before = (hidden_one,)
    for half in (1, 0):
        if placed:
            more = (spread(*down_parts[half], half).reshape(2, D, D),)
            more_specs = [VECTOR]
        else:
            more, more_specs = down_parts[half], [ANYWHERE] * 2
        done = call(
            functools.partial(down_kernel, placed, half, count),
            ("down_own", "down_other")[half],
            (slot, turned_in, low_grad, vectors, act[half], slope[half], up_all[half])
            + before
            + tuple(more),
            [SCALAR] + [VECTOR] * (6 + len(before)) + more_specs,
            [
                rows_f32 if half else rows_bf,
                rows_f32,
                shape((2, 1, D), F32),
                squares_of if placed else pieces,
            ],
            [] if placed else vmem(((2, D, D), BF)) + [pltpu.SemaphoreType.DMA((2,))],
            14,
            (1_000_000_000, 4_000_000, 0),
        )
        if half == 1:
            done, high_got, kept_got = join(done, high_got, swapped[0])
            low_got = down_sum.send_low(high_got)
            down_sum.keep(down_grad[0][0], kept_got)
            down_sum.take_high(high_got)
            down_got = down_sum.send()
        else:
            done, low_got = join(done, low_got)
            down_sum.take_low(low_got)
        before = tuple(done[:2])
        grad_hidden[half] = done[2]
        up_grad[half] = done[3]
        if placed:
            value = done[3].reshape(2, count, rows, D).transpose(1, 0, 2, 3)
            up_grad[half] = reorder(value.reshape(count, 2 * rows, D), turned[half])
        if half == 1:
            swapped = swap_cores(up_grad[1])
    layer_half, grad_second = before
    up_sum = Reducer(up_grad[0], swapped, count)
    high_got = up_sum.send_high()

    proj_outs = [shape((3, SEQ, HALF), BF), shape((HALF, D), BF)]
    line_outs = [shape((8, D), F32), shape((2, HALF), F32)]
    done = call(
        back_own_kernel,
        "back_own",
        (
            low_grad,
            vectors,
            grad_second,
            hidden_one,
            proj[0],
            log_total[0],
            mixed[0],
            attn_all[0],
            qkv_all[0],
            bias,
        ),
        [VECTOR] * 10,
        [rows_f32, rows_bf] + proj_outs + line_outs + [rows_f32],
        [],
        12,
        (3_900_000_000, 9_000_000, 1_600_000),
    )
    done, down_got, high_got = join(done, down_got, high_got)
    grad_one, grad_low, proj_low_own, grad_attn_own, lines, head_lines_own, grad_first = done
    low_got = up_sum.send_low(high_got)
    up_sum.take_high(high_got)
    up_got = up_sum.send()
    down_sum.take(down_got)
    down_got = down_sum.send()
    front_pieces = shape((count, 4 * rows + 16, HALF), BF)
    small_scratch = vmem(((16, HALF), F32))
    outs = [rows_f32, shape((D, SEQ), BF), line_outs[0]]
    if placed:
        outs += proj_outs + line_outs[1:]
        scratch = []
    else:
        outs += [front_pieces]
        scratch = vmem(((3, SEQ, HALF), BF), ((HALF, D), BF), ((2, HALF), F32)) + small_scratch
    done = call(
        functools.partial(back_other_kernel, placed, count),
        "back_other",
        (
            slot,
            grad_low,
            vectors,
            proj[1],
            log_total[1],
            mixed[1],
            attn_all[1],
            qkv_all[1],
            bias,
            grad_first,
            grad_one,
            lines,
            normed,
            inv_std,
            first_in,
            grad_hidden[1],
        ),
        [SCALAR] + [VECTOR] * 15,
        outs,
        scratch,
        12,
        (5_000_000_000, 12_000_000, 1_600_000),
    )
    done, low_got, up_got, down_got = join(done, low_got, up_got, down_got)
    input_half, turned_first, lines = done[:3]
    up_sum.take_low(low_got)
    up_sum.take(up_got)
    down_sum.take(down_got)
    if placed:

        def widen(value):
            return jnp.pad(value, ((0, 0), (0, 0), (0, HALF - value.shape[2])))

        def front_pieces_of(half, proj_low, grad_attn, head_lines):
            grads = [dot_nn(turned_first, proj_low[kind]) for kind in range(3)]
            grads = jnp.stack([one.reshape(count, rows, HALF) for one in grads], axis=1)
            attn_part = grad_attn.reshape(count, part, 2, HALF).transpose(0, 2, 1, 3)
            parts = [
                grads.astype(BF).reshape(count, 3 * rows, HALF),
                attn_part.reshape(count, rows, HALF),
                widen(lines[:6].reshape(6, count, rows).transpose(1, 0, 2)).astype(BF),
                widen(head_lines.reshape(2, count, part).transpose(1, 0, 2)).astype(BF),
                widen(grad_hidden[half].reshape(count, 1, 2 * rows)).astype(BF),
                jnp.zeros((count, 7, HALF), BF),
            ]
            return reorder(jnp.concatenate(parts, axis=1), turned[half])

        front_own = front_pieces_of(0, proj_low_own, grad_attn_own, head_lines_own)
        swapped = swap_cores(front_pieces_of(1, *done[3:]))
    else:
        swapped = swap_cores(done[3])
        (front_own,) = call(
            functools.partial(pieces_kernel, count),
            "pieces",
            (slot, turned_first, proj_low_own, grad_attn_own, lines, head_lines_own, grad_hidden[0]),
            [SCALAR] + [VECTOR] * 6,
            [front_pieces],
            small_scratch,
            8,
            (1_000_000_000, 6_000_000, 0),
        )
        front_own, swapped = lax.optimization_barrier((front_own, swapped))
    front_sum = Reducer(front_own, swapped, count)
    high_got = front_sum.send_high()
    low_got = front_sum.send_low()
    front_sum.take_high(high_got)
    front_got = front_sum.send()
    front_sum.take_low(low_got)
    front_sum.take(front_got)
    layer_output = both_halves(layer_half, core)
    input_grad = both_halves(input_half, core)

    kept, got = down_sum.finish()
    total_down = kept + got.astype(F32)
    kept, got = up_sum.finish()
    total_up = kept + got.astype(F32)
    kept, got = front_sum.finish()
    outs = [shape(kept.shape, F32), shape((2 * count, 8, 128), F32)]
    close_args = (total_down, total_up, kept, got)
    total, squares = call(
        functools.partial(close_kernel, rows),
        "close",
        close_args,
        [VECTOR] * 4,
        outs,
        [],
        16,
        (1_000_000, 1_200_000, 0),
    )
    spread_squares = lax.all_to_all(squares, BOTH, 0, 0, tiled=True)
    state = []
    for index, group in enumerate(groups):
        state += [one.reshape(1, -1) if index == 5 else one for one in group]
    update_args = (spread_squares, total_down, total_up, total) + tuple(state)
    outs = [shape((1, 1), F32)] + [shape(one.shape, F32) for one in state]
    results = call(
        functools.partial(update_kernel, rows),
        "update",
        update_args,
        None,
        outs,
        [],
        60,
        (5_000_000, 8_000_000, 500_000),
        True,
    )
    grad_norm = results[0].reshape(())
    results = [
        one.reshape(-1) if 20 <= index < 24 else one for index, one in enumerate(results[1:])
    ]
    return (layer_output, input_grad, grad_norm, *results)


FORCE_PLAIN = False


def solution(mesh):
    row, late, wide = P("dp", None), P(("mp", "dp"), None), P("dp", "mp")
    kinds = (
        P(None, "dp", "mp"),
        late,
        wide,
        late,
        P(None, ("mp", "dp")),
        P(("mp", "dp")),
        P(None, "dp"),
    )
    per_parameter = tuple(kind for kind in kinds for _ in range(4))
    return jax.shard_map(
        functools.partial(body, FORCE_PLAIN),
        mesh=mesh,
        in_specs=(row, row, row, P("dp")) + per_parameter,
        out_specs=(row, row, P()) + per_parameter,
        check_vma=False,
    )
```

```python
import functools

import jax
import jax.numpy as jnp
from jax import lax
from jax.experimental import pallas as pl
from jax.experimental.pallas import tpu as pltpu
from jax.sharding import PartitionSpec as P

HD = 64
PAIR = 128
SEQ = 512
D = 768
HALF = 384
STEP = 7
SMALL = 32

NORM_EPS = 1e-05
SCORE_SCALE = 0.125
LEARN_RATE = 0.03
VECTOR_RATE = 0.4
BETA_ONE = 0.9
BETA_TWO = 0.95
ADAM_EPS = 1e-08
WEIGHT_DECAY = 0.1
EMA_RATE = 0.8
CLIP_NORM = 1.0
GELU_COEF = 0.7978845608028654
GELU_CUBE = 0.044715
MASKED = -1e30

BF = jnp.bfloat16
F32 = jnp.float32
BOTH = ("dp", "mp")


def dot_nn(left, right):
    return lax.dot_general(left, right, (((1,), (0,)), ((), ())), preferred_element_type=F32)


def dot_nt(left, right):
    return lax.dot_general(left, right, (((1,), (1,)), ((), ())), preferred_element_type=F32)


def dot_tn(left, right):
    return lax.dot_general(left, right, (((0,), (0,)), ((), ())), preferred_element_type=F32)


def norm_parts(rows):
    row_mean = jnp.mean(rows, axis=1, keepdims=True)
    centered = rows - row_mean
    inv_std = lax.rsqrt(jnp.mean(centered * centered, axis=1, keepdims=True) + NORM_EPS)
    return (centered * inv_std, inv_std)


def norm_back(grad_in, normed, inv_std, gain):
    scaled = grad_in * gain
    return inv_std * (
        scaled
        - jnp.mean(scaled, axis=1, keepdims=True)
        - normed * jnp.mean(scaled * normed, axis=1, keepdims=True)
    )


def column_sum(value):
    return jnp.sum(value, axis=0, keepdims=True)


def step_bits(count):
    length = count.bit_length() - 1
    high = [(bit, bit) for bit in reversed(range(2, length))]
    return high + [(0, 1), (1, 0)]


def late_bits(count):
    bits = step_bits(count)
    return bits[-2:-1] + bits[:-2] + bits[-1:]


def step_pairs(count, bits):
    return [
        (index * 2 + core, (index ^ (1 << bits[core])) * 2 + core)
        for index in range(count)
        for core in range(2)
    ]


def slots(count, here, core, steps):
    apart = jnp.arange(count, dtype=jnp.int32) ^ here
    place = jnp.zeros_like(apart)
    for at, bits in enumerate(steps):
        bit = jnp.where(core == 0, (apart >> bits[0]) & 1, (apart >> bits[1]) & 1)
        place = place | (bit << at)
    return place


def reorder(value, pick):
    flat = dot_nn(pick, value.reshape(value.shape[0], -1)).astype(BF)
    return flat.reshape(value.shape)


def swap_cores(value):
    return lax.ppermute(value, "mp", [(0, 1), (1, 0)])


def after(value, *others):
    return lax.optimization_barrier((value,) + others)[0]


def join(made, *gots):
    joined = lax.optimization_barrier(tuple(made) + gots)
    return (list(joined[: len(made)]), *joined[len(made) :])


class Gatherer:
    def __init__(self, piece, count, steps):
        self.count, self.held, self.got = count, piece[None], None
        self.bits = list(steps)

    def send(self, *others):
        if others:
            self.held = after(self.held, *others)
        return lax.ppermute(self.held, BOTH, step_pairs(self.count, self.bits.pop(0)))

    def take(self, got):
        if self.bits:
            self.held = jnp.concatenate([self.held, got], axis=0)
        else:
            self.got = got


class Reducer:
    def __init__(self, own, got, count):
        self.count = count
        self.bits = list(reversed(step_bits(count)))
        self.half = count // 2
        if not isinstance(own, tuple):
            own, got = (own[: self.half], own[self.half :]), (got[: self.half], got[self.half :])
        self.keep(own[0], got[0])
        self.sent = (own[1].astype(F32) + got[1].astype(F32)).astype(BF)

    def keep(self, own, got):
        self.kept = own.astype(F32) + got.astype(F32)

    def pairs(self):
        return step_pairs(self.count, self.bits.pop(0))

    def send(self):
        return lax.ppermute(self.sent, BOTH, self.pairs())

    def take(self, got):
        self.half //= 2
        total = self.kept + got.astype(F32)
        self.kept, self.sent = total[: self.half], total[self.half :].astype(BF)

    def send_parts(self):
        pairs, half = self.pairs(), self.half // 2
        return [lax.ppermute(one, BOTH, pairs) for one in (self.sent[half:], self.sent[:half])]

    def take_high(self, got):
        self.half //= 2
        self.sent = (self.kept[self.half :] + got.astype(F32)).astype(BF)

    def take_low(self, got):
        self.kept = self.kept[: self.half] + got.astype(F32)

    def finish(self):
        while len(self.bits) > 1:
            self.take(self.send())
        return (self.kept[0], self.send()[0])


def pick(slot, held, got, *at):
    half = held.shape[0]
    inner = slot & (half - 1)
    return jnp.where(slot < half, held[(inner, *at)], got[(inner, *at)])


def put(slot, kept, sent, piece, start):
    half = kept.shape[0]
    at = slice(start, start + piece.shape[0])

    @pl.when(slot < half)
    def _():
        kept[slot, at, :] = piece

    @pl.when(slot >= half)
    def _():
        sent[slot - half, at, :] = piece


def pack_kernel(qkv_w, attn_w, up_w, down_w, head_w, hidden_w, vector_w, piece, up, down, small):
    rows = qkv_w.shape[1]
    part = rows // 2
    for kind in range(3):
        piece[kind * rows : (kind + 1) * rows, :] = qkv_w[kind].astype(BF)
    both = jnp.concatenate([attn_w[:, :HALF], attn_w[:, HALF:]], axis=0)
    piece[3 * rows : 3 * rows + 2 * part, :] = both.astype(BF)
    small[...] = jnp.zeros_like(small)
    small[0:6, :rows] = vector_w[...]
    small[6:8, :part] = head_w[...]
    small[8:9, : 2 * rows] = hidden_w[...]
    piece[4 * rows :, :] = small[...].astype(BF)
    up[0] = up_w[:, :D].astype(BF)
    up[1] = up_w[:, D:].astype(BF)
    down[...] = down_w[...].astype(BF)


def prepare_kernel(
    core_ref, pads_ref, tokens, cotangent, row_code, key_code, x_out, normed_out, inv_out, low_grad, bias, buffer, sem
):
    at = pl.ds(pl.multiple_of(core_ref[0] * SEQ, SEQ), SEQ)
    copies = [
        pltpu.make_async_copy(tokens.at[at], x_out, sem.at[0]),
        pltpu.make_async_copy(cotangent.at[at], buffer, sem.at[1]),
    ]
    for copy in copies:
        copy.start()
    key_at = lax.broadcasted_iota(jnp.int32, (SEQ, SEQ), 0)
    row_at = lax.broadcasted_iota(jnp.int32, (SEQ, SEQ), 1)
    seen = (key_code[...] == row_code[...]) | (key_at == row_at)
    bias[...] = jnp.where(seen, 0.0, MASKED)
    copies[0].wait()
    normed, inv_std = norm_parts(x_out[...].astype(F32))
    normed_out[...], inv_out[...] = normed, inv_std
    copies[1].wait()
    position = lax.broadcasted_iota(jnp.int32, (SEQ, D), 0)
    kept = position < SEQ - pads_ref[core_ref[0]]
    low_grad[...] = jnp.where(kept, buffer[...].astype(F32), 0.0).astype(BF)


def attend(proj, bias, log_total, mixed):
    lane = lax.broadcasted_iota(jnp.int32, (SEQ, PAIR), 1)
    for pair in range(HALF // PAIR):
        at = slice(pair * PAIR, (pair + 1) * PAIR)
        q_pair, k_pair, v_pair = proj[0, :, at], proj[1, :, at], proj[2, :, at]
        v_turned = v_pair.T
        turned = []
        for side in range(2):
            mine = (lane < HD) if side == 0 else (lane >= HD)
            q_side = jnp.where(mine, q_pair, jnp.zeros_like(q_pair))
            scores = dot_nt(k_pair, q_side) + bias[...]
            top = jnp.max(scores, axis=0, keepdims=True)
            exponent = jnp.exp(scores - top)
            total = jnp.sum(exponent, axis=0, keepdims=True)
            index = pair * 2 + side
            log_total[index : index + 1, :] = top + jnp.log(total)
            part = dot_nn(v_turned[side * HD : (side + 1) * HD], exponent.astype(BF))
            turned.append(part * (1.0 / total))
        mixed[:, at] = jnp.concatenate(turned, axis=0).T.astype(BF)


def front_kernel(placed, half, count, rows, slot_ref, *rest):
    rest = list(rest)
    take = lambda amount: [rest.pop(0) for _ in range(amount)]
    if half == 0:
        x, normed, bias = take(3)
        if placed:
            (vectors,) = take(1)
    else:
        first_in, before, bias, vectors = take(4)
    if placed:
        heads, qkv, attn = take(3)
    else:
        parts = take(2)
    if half == 0:
        first_in, after_out = take(2)
    else:
        after_out, second_in, turned_in = take(3)
    proj, log_total, mixed = take(3)
    if not placed:
        if half == 0:
            (vectors,) = take(1)
        heads, hidden, qkv, attn = take(4)
        held, got = parts
        part = rows // 2
        sides = []
        for index in range(count):
            slot = slot_ref[half, index]
            for kind in range(3):
                qkv[kind, index * rows : (index + 1) * rows, :] = pick(
                    slot, held, got, slice(kind * rows, (kind + 1) * rows)
                )
            sides.append(pick(slot, held, got, slice(3 * rows, 4 * rows)).astype(F32))
            tail = pick(slot, held, got, slice(4 * rows, 4 * rows + 16)).astype(F32)
            if half == 0:
                vectors[0:6, index * rows : (index + 1) * rows] = tail[0:6, :rows]
            heads[:, index * part : (index + 1) * part] = tail[6:8, :part]
            start = (index % (count // 2)) * 2 * rows
            hidden[index // (count // 2), :, start : start + 2 * rows] = tail[8:9, : 2 * rows]
            if index % 2:
                at = slice((index - 1) * part, (index + 1) * part)
                left = jnp.concatenate([one[:part] for one in sides], axis=0)
                right = jnp.concatenate([one[part:] for one in sides], axis=0)
                attn[at, :HALF] = left.astype(BF)
                attn[at, HALF:] = right.astype(BF)
                sides = []
    if half == 0:
        first_in[...] = (normed[...] * vectors[0:1, :] + vectors[1:2, :]).astype(BF)
    value = dot_nn(first_in[...], qkv[0]) + heads[0:1, :]
    proj[0] = (value.astype(BF).astype(F32) * SCORE_SCALE).astype(BF)
    proj[1] = dot_nn(first_in[...], qkv[1]).astype(BF)
    proj[2] = (dot_nn(first_in[...], qkv[2]) + heads[1:2, :]).astype(BF)
    attend(proj, bias, log_total, mixed)
    value = dot_nn(mixed[...], attn[...])
    if half == 0:
        after_out[...] = x[...].astype(F32) + value + vectors[4:5, :]
        return
    value = before[...] + value
    after_out[...] = value
    normed, _ = norm_parts(value)
    entered = (normed * vectors[2:3, :] + vectors[3:4, :]).astype(BF)
    second_in[...] = entered
    turned_in[...] = entered.T


def up_kernel(placed, half, count, slot_ref, second_in, low_grad, bias, *rest):
    rows = D // count
    if placed:
        up, act, slope, grad_down = rest
    else:
        held, got, act, slope, up, grad_kept, grad_sent = rest
        for index in range(count):
            slot = slot_ref[half, index]
            for block in range(2):
                up[block, index * rows : (index + 1) * rows, :] = pick(slot, held, got, block)
    chunk_rows = 256
    for block in range(2):
        for chunk in range(SEQ // chunk_rows):
            at = slice(chunk * chunk_rows, (chunk + 1) * chunk_rows)
            pre = dot_nn(second_in[at, :], up[block]) + bias[block]
            square = pre * pre
            bent = jnp.tanh(pre * (GELU_COEF + GELU_COEF * GELU_CUBE * square))
            half_up = 0.5 + 0.5 * bent
            gelu = pre * half_up
            act[block, at, :] = gelu.astype(BF)
            inner = pre * (2.0 * GELU_COEF + 6.0 * GELU_COEF * GELU_CUBE * square)
            slope[block, at, :] = (half_up + half_up * (inner - half_up * inner)).astype(BF)
        grad = dot_tn(act[block], low_grad[...]).astype(BF)
        if placed:
            grad_down[block] = grad
            continue
        for index in range(count // 2):
            piece = grad[index * 2 * rows : (index + 1) * 2 * rows, :]
            put(slot_ref[half, block * (count // 2) + index], grad_kept, grad_sent, piece, 0)


def down_kernel(
    placed, half, count, slot_ref, late_ref, turned_in, low_grad, vectors, act, slope, up, before_out, *rest
):
    rows = D // count
    rest = list(rest)
    take = lambda amount: [rest.pop(0) for _ in range(amount)]
    if half == 0:
        (before_grad,) = take(1)
    if placed:
        down, out, grad_second, grad_hidden, grad_up = rest
    else:
        held, got, out, grad_second, grad_hidden, grad_kept, grad_sent, down = rest
    parts_out = []
    for block in range(2):
        if not placed:
            for index in range(count // 2):
                slot = late_ref[half, block * (count // 2) + index]
                at = slice(index * 2 * rows, (index + 1) * 2 * rows)
                down[block, at, :] = pick(slot, held, got)
        grad_pre = dot_nt(low_grad[...], down[block]) * slope[block].astype(F32)
        grad_hidden[block] = column_sum(grad_pre)
        pre_low = grad_pre.astype(BF)
        grad = dot_nn(turned_in[...], pre_low).astype(BF)
        part_out = dot_nn(act[block], down[block])
        part_grad = dot_nt(pre_low, up[block])
        if half == 1 and block == 0:
            out[...] = before_out[...] + vectors[5:6, :] + part_out
            grad_second[...] = part_grad
        elif half == 1:
            out[...] += part_out
            grad_second[...] += part_grad
        elif block == 0:
            parts_out.append(part_out)
            grad_second[...] = before_grad[...] + part_grad
        else:
            out[...] = (before_out[...] + (parts_out[0] + part_out)).astype(BF)
            grad_second[...] += part_grad
        if placed:
            grad_up[block] = grad
            continue
        for index in range(count):
            piece = grad[index * rows : (index + 1) * rows, :]
            put(slot_ref[half, index], grad_kept, grad_sent, piece, block * rows)


def attend_back(proj, log_total, mixed, attn, bias, grad_low, proj_low, grad_attn, head_lines):
    lane = lax.broadcasted_iota(jnp.int32, (SEQ, PAIR), 1)
    grad_attn[...] = dot_tn(mixed[...], grad_low).astype(BF)
    grad_mixed = dot_nt(grad_low, attn[...]).astype(BF)
    for pair in range(HALF // PAIR):
        at = slice(pair * PAIR, (pair + 1) * PAIR)
        q_pair, k_pair, v_pair = proj[0, :, at], proj[1, :, at], proj[2, :, at]
        g_pair = grad_mixed[:, at]
        k_turned = k_pair.T
        grad_key = jnp.zeros((SEQ, PAIR), F32)
        grad_value = jnp.zeros((SEQ, PAIR), F32)
        turned = []
        for side in range(2):
            mine = (lane < HD) if side == 0 else (lane >= HD)
            q_side = jnp.where(mine, q_pair, jnp.zeros_like(q_pair))
            g_side = jnp.where(mine, g_pair, jnp.zeros_like(g_pair))
            index = pair * 2 + side
            scores = dot_nt(k_pair, q_side) + bias[...]
            probs = jnp.exp(scores - log_total[index : index + 1, :])
            grad_probs = dot_nt(v_pair, g_side)
            row_dot = column_sum(probs * grad_probs)
            grad_scores = (probs * (grad_probs - row_dot)).astype(BF)
            grad_value = grad_value + dot_nn(probs.astype(BF), g_side)
            grad_key = grad_key + dot_nn(grad_scores, q_side)
            turned.append(dot_nn(k_turned[side * HD : (side + 1) * HD], grad_scores))
        grad_query = jnp.concatenate(turned, axis=0).T * SCORE_SCALE
        head_lines[0:1, at] = column_sum(grad_query)
        head_lines[1:2, at] = column_sum(grad_value)
        proj_low[0, :, at] = grad_query.astype(BF)
        proj_low[1, :, at] = grad_key.astype(BF)
        proj_low[2, :, at] = grad_value.astype(BF)


def first_part(proj_low, qkv):
    total = dot_nt(proj_low[0], qkv[0])
    for kind in range(1, 3):
        total = total + dot_nt(proj_low[kind], qkv[kind])
    return total


def pieces_out(half, count, slot_ref, turned_first, proj_low, grad_attn, lines, head_lines, grad_hidden, out, small):
    rows = D // count
    part = rows // 2
    for kind in range(3):
        grad_qkv = dot_nn(turned_first[...], proj_low[kind]).astype(BF)
        for index in range(count):
            out[slot_ref[half, index], kind * rows : (kind + 1) * rows, :] = grad_qkv[
                index * rows : (index + 1) * rows, :
            ]
    small[...] = jnp.zeros_like(small)
    whole = grad_attn[...].astype(F32)
    for index in range(count):
        start = (index % (count // 2)) * 2 * rows
        slot = slot_ref[half, index]
        piece = whole[index * part : (index + 1) * part, :]
        piece = jnp.concatenate([piece[:, :HALF], piece[:, HALF:]], axis=0)
        out[slot, 3 * rows : 4 * rows, :] = piece.astype(BF)
        small[0:6, :rows] = lines[0:6, index * rows : (index + 1) * rows]
        small[6:8, :part] = head_lines[:, index * part : (index + 1) * part]
        small[8:9, : 2 * rows] = grad_hidden[index // (count // 2), :, start : start + 2 * rows]
        out[slot, 4 * rows :, :] = small[...].astype(BF)


def back_own_kernel(
    low_grad,
    vectors,
    grad_second,
    hidden_one,
    proj,
    log_total,
    mixed,
    attn,
    qkv,
    bias,
    grad_one_out,
    grad_low_out,
    proj_low,
    grad_attn,
    lines,
    head_lines,
    grad_first,
):
    grad_out = low_grad[...].astype(F32)
    normed, inv_std = norm_parts(hidden_one[...])
    grads = grad_second[...]
    lines[2:3, :], lines[3:4, :] = column_sum(grads * normed), column_sum(grads)
    grad_one = grad_out + norm_back(grads, normed, inv_std, vectors[2:3, :])
    grad_one_out[...] = grad_one
    lines[4:5, :], lines[5:6, :] = column_sum(grad_one), column_sum(grad_out)
    grad_low = grad_one.astype(BF)
    grad_low_out[...] = grad_low
    attend_back(proj, log_total, mixed, attn, bias, grad_low, proj_low, grad_attn, head_lines)
    grad_first[...] = first_part(proj_low, qkv)


def back_other_kernel(
    placed,
    count,
    slot_ref,
    grad_low,
    vectors,
    proj,
    log_total,
    mixed,
    attn,
    qkv,
    bias,
    before_first,
    grad_one,
    before_lines,
    normed,
    inv_std,
    first_in,
    grad_hidden,
    input_grad,
    turned_first,
    lines,
    *rest,
):
    if placed:
        proj_low, grad_attn, head_lines = rest
    else:
        out, proj_low, grad_attn, head_lines, small = rest
    attend_back(proj, log_total, mixed, attn, bias, grad_low[...], proj_low, grad_attn, head_lines)
    grad_first = before_first[...] + first_part(proj_low, qkv)
    lines[...] = before_lines[...]
    lines[0:1, :] = column_sum(grad_first * normed[...])
    lines[1:2, :] = column_sum(grad_first)
    back = norm_back(grad_first, normed[...], inv_std[...], vectors[0:1, :])
    input_grad[...] = grad_one[...] + back
    turned_first[...] = first_in[...].T
    if not placed:
        pieces_out(
            1, count, slot_ref, turned_first, proj_low, grad_attn, lines, head_lines, grad_hidden, out, small
        )


def pieces_kernel(count, slot_ref, turned_first, proj_low, grad_attn, lines, head_lines, grad_hidden, out, small):
    pieces_out(
        0, count, slot_ref, turned_first, proj_low, grad_attn, lines, head_lines, grad_hidden, out, small
    )


def close_kernel(rows, total_down, total_up, kept, got, total, squares):
    value = kept[...] + got[...].astype(F32)
    total[...] = value
    part = jnp.sum(total_down[...] * total_down[...]) + jnp.sum(total_up[...] * total_up[...])
    row = lax.broadcasted_iota(jnp.int32, value.shape, 0)
    weight = jnp.where((row >= 4 * rows) & (row < 4 * rows + 6), 0.5, 1.0)
    part = part + jnp.sum(value * value * weight)
    squares[...] = jnp.full(squares.shape, part, F32)


def adam_step(gradient, master, first, second, average, factor, decay_rate, step_rate):
    clipped = gradient * factor
    first_new = BETA_ONE * first + (1.0 - BETA_ONE) * clipped
    second_new = BETA_TWO * second + (1.0 - BETA_TWO) * clipped * clipped
    first_hat = first_new / (1.0 - BETA_ONE**STEP)
    second_hat = second_new / (1.0 - BETA_TWO**STEP)
    master_new = master - step_rate * (
        first_hat / (jnp.sqrt(second_hat) + ADAM_EPS) + decay_rate * master
    )
    average_new = EMA_RATE * average + (1.0 - EMA_RATE) * master_new
    return (first_new, second_new, master_new, average_new)


def update_kernel(rows, spread, total_down, total_up, total, *rest):
    state, norm, results = rest[:28], rest[28], rest[29:]
    grad_norm = jnp.sqrt(jnp.sum(spread[...], axis=0))[0:1, 0:1]
    norm[...] = grad_norm
    factor = CLIP_NORM / jnp.maximum(grad_norm, CLIP_NORM)
    part = rows // 2

    def apply(index, at, gradient):
        decay, rate = (WEIGHT_DECAY, LEARN_RATE) if index < 4 else (0.0, VECTOR_RATE)
        values = adam_step(
            gradient, *[state[4 * index + k][at] for k in range(4)], factor, decay, rate
        )
        for k in range(4):
            results[4 * index + k][at] = values[k]

    for kind in range(3):
        apply(0, (kind,), total[kind * rows : (kind + 1) * rows, :])
    for side in range(2):
        start = 3 * rows + side * part
        columns = slice(side * HALF, (side + 1) * HALF)
        apply(1, (slice(None), columns), total[start : start + part, :])
        columns = slice(side * D, (side + 1) * D)
        apply(2, (slice(None), columns), total_up[side * rows : (side + 1) * rows, :])
    every = (slice(None), slice(None))
    apply(3, every, total_down[...])
    apply(4, every, total[4 * rows + 6 : 4 * rows + 8, :part])
    apply(5, every, total[4 * rows + 8 : 4 * rows + 9, : 2 * rows])
    apply(6, every, total[4 * rows : 4 * rows + 6, :rows])


def vmem(*shapes):
    return [pltpu.VMEM(shape, dtype) for shape, dtype in shapes]


def shape(dims, dtype):
    return jax.ShapeDtypeStruct(dims, dtype)


def whole_spec(dims):
    return pl.BlockSpec(dims, lambda *_: (0,) * len(dims))


VECTOR = pl.BlockSpec(memory_space=pltpu.VMEM)
SCALAR = pl.BlockSpec(memory_space=pltpu.SMEM)
ANYWHERE = pl.BlockSpec(memory_space=pl.ANY)


def call(body, name, args, specs, outs, scratch, mib, cost, streamed=False):
    flops, touched, special = cost
    if streamed:
        more = {
            "grid": (1,),
            "in_specs": [whole_spec(one.shape) for one in args],
            "out_specs": [whole_spec(one.shape) for one in outs],
        }
    else:
        more = {"in_specs": specs, "out_specs": [VECTOR] * len(outs)}
    return pl.pallas_call(
        body,
        out_shape=outs,
        scratch_shapes=scratch,
        compiler_params=pltpu.CompilerParams(vmem_limit_bytes=mib << 20),
        cost_estimate=pl.CostEstimate(
            flops=flops, bytes_accessed=touched, transcendentals=special
        ),
        name=name,
        **more,
    )(*args)


def both_halves(own, core):
    other = swap_cores(own)
    first = jnp.where(core == 0, own, other)
    second = jnp.where(core == 0, other, own)
    return jnp.concatenate([first, second], axis=0)


def body(force_plain, *args):
    (tokens, cotangent, seg_lengths, pad_counts) = args[:4]
    groups = [args[4 + 4 * i : 8 + 4 * i] for i in range(7)]
    qkv_w, attn_w, up_w, down_w, head_w, hidden_w, vector_w = (group[0] for group in groups)
    rows = qkv_w.shape[1]
    part = rows // 2
    count = D // rows
    placed = bool(rows % 16) or force_plain
    here, core = lax.axis_index("dp"), lax.axis_index("mp")
    steps, late_steps = step_bits(count), late_bits(count)
    slot, late_slot = (
        jnp.stack([slots(count, here, core, one), slots(count, here, 1 - core, one)], axis=0)
        for one in (steps, late_steps)
    )
    core_at = core.reshape(1).astype(jnp.int32)

    packed = [shape((4 * rows + 16, HALF), BF), shape((2, rows, D), BF), shape((2 * rows, D), BF)]
    pack_args = (qkv_w, attn_w, up_w, down_w, head_w, hidden_w.reshape(1, -1), vector_w)
    piece, up_piece, down_piece = call(
        pack_kernel,
        "pack",
        pack_args,
        None,
        packed,
        vmem(((16, HALF), F32)),
        60,
        (1, 1_400_000, 0),
        True,
    )
    front_hops, up_hops, down_hops = (
        Gatherer(one, count, order)
        for one, order in ((piece, steps), (up_piece, steps), (down_piece, late_steps))
    )
    lengths = lax.dynamic_index_in_dim(seg_lengths, core, 0, keepdims=False)
    padding = lax.dynamic_index_in_dim(pad_counts, core, 0, keepdims=False)
    upto = jnp.arange(lengths.shape[0])[:, None] >= jnp.arange(lengths.shape[0])[None, :]
    bounds = jnp.sum(jnp.where(upto, lengths[None, :], 0), axis=1)
    position = jnp.arange(SEQ, dtype=jnp.int32)
    row_code = jnp.sum((position[None, :] >= bounds[:, None]).astype(jnp.int32), axis=0)[None, :]
    key_code = jnp.sum((position[:, None] >= bounds[None, :]).astype(jnp.int32), axis=1)[:, None]
    key_code = jnp.where(position[:, None] >= SEQ - padding, -1, key_code)

    rows_bf, rows_f32 = shape((SEQ, D), BF), shape((SEQ, D), F32)
    half_bf = shape((SEQ, HALF), BF)

    high = len(front_hops.bits) - 2
    front_got, down_got = front_hops.send(), down_hops.send()
    prepared = call(
        prepare_kernel,
        "prepare",
        (core_at, pad_counts, tokens, cotangent, row_code, key_code),
        [SCALAR] * 2 + [ANYWHERE] * 2 + [VECTOR] * 2,
        [rows_bf, rows_f32, shape((SEQ, 1), F32), rows_bf, shape((SEQ, SEQ), F32)],
        vmem(((SEQ, D), BF)) + [pltpu.SemaphoreType.DMA((2,))],
        12,
        (3_000_000, 9_000_000, 0),
    )
    prepared, front_got, down_got, slot, late_slot = join(
        prepared, front_got, down_got, slot, late_slot
    )
    down_hops.take(down_got)
    x_own, normed, inv_std, low_grad, bias = prepared
    front_hops.take(front_got)
    for _ in range(high):
        front_got, up_got = front_hops.send(), up_hops.send(front_hops.held)
        _, front_got, up_got = join((), front_got, up_got)
        front_hops.take(front_got)
        up_hops.take(up_got)
    front_got, up_got = front_hops.send(), up_hops.send()
    for _ in range(high - 1):
        down_hops.take(down_hops.send(up_hops.held))
    front_swap = swap_cores(front_hops.held)
    _, front_got, up_got, front_swap, down_hops.held = join(
        (), front_got, up_got, front_swap, down_hops.held
    )
    up_hops.take(up_got)
    front_swap_got = swap_cores(front_got)
    up_got, down_got = up_hops.send(), down_hops.send()

    if placed:
        index = jnp.arange(count, dtype=jnp.int32)[None, :]
        picks, late_picks = (
            [(one[half][:, None] == index).astype(BF) for half in range(2)]
            for one in (slot, late_slot)
        )
        turned = [one.T for one in picks]

    def spread(held, got, pick):
        return reorder(jnp.concatenate([held, got], axis=0), pick)

    def front_more(held, got, half):
        if not placed:
            return (), (held, got), [VECTOR] * 2
        one = spread(held, got, picks[half])
        tail = one[:, 4 * rows :].astype(F32)
        vectors = tail[:, :6, :rows].transpose(1, 0, 2).reshape(6, D)
        heads = tail[:, 6:8, :part].transpose(1, 0, 2).reshape(2, HALF)
        hidden = tail[:, 8, : 2 * rows].reshape(2, 1, D)
        qkv = one[:, : 3 * rows].reshape(count, 3, rows, HALF).transpose(1, 0, 2, 3)
        attn = one[:, 3 * rows : 4 * rows].reshape(count, 2, part, HALF).transpose(0, 2, 1, 3)
        more = (heads, qkv.reshape(3, D, HALF), attn.reshape(HALF, D))
        return (jnp.pad(vectors, ((0, 2), (0, 0))), hidden), more, [VECTOR] * 3

    extra_outs = [
        shape((2, HALF), F32),
        shape((2, 1, D), F32),
        shape((3, D, HALF), BF),
        shape((HALF, D), BF),
    ]
    attend_outs = [shape((3, SEQ, HALF), BF), shape((HALF // HD, SEQ), F32), half_bf]
    front_cost = (3_000_000_000, 9_000_000, 1_600_000)

    early, more, more_specs = front_more(front_hops.held, front_got, 0)
    done = call(
        functools.partial(front_kernel, placed, 0, count, rows),
        "front_own",
        (slot, x_own, normed, bias) + early[:1] + more,
        [SCALAR] + [VECTOR] * (3 + len(early[:1])) + more_specs,
        [rows_bf, rows_f32] + attend_outs + ([] if placed else [shape((8, D), F32)] + extra_outs),
        [],
        12,
        front_cost,
    )
    done, front_swap_got = join(done, front_swap_got)
    first_in, before = done[:2]
    proj, log_total, mixed = [done[2]], [done[3]], [done[4]]
    if placed:
        vectors, hidden = early[0], [early[1]]
        qkv_all, attn_all = [more[1]], [more[2]]
    else:
        vectors, hidden = done[5], [done[7]]
        qkv_all, attn_all = [done[8]], [done[9]]

    early, more, more_specs = front_more(front_swap, front_swap_got, 1)
    up_swap = swap_cores(up_hops.held)
    done = call(
        functools.partial(front_kernel, placed, 1, count, rows),
        "front_other",
        (slot, first_in, before, bias, vectors) + more,
        [SCALAR] + [VECTOR] * 4 + more_specs,
        [rows_f32, rows_bf, shape((D, SEQ), BF)] + attend_outs + ([] if placed else extra_outs),
        [],
        12,
        front_cost,
    )
    done, up_got, down_got, up_swap = join(done, up_got, down_got, up_swap)
    hidden_one, second_in, turned_in = done[:3]
    proj.append(done[3])
    log_total.append(done[4])
    mixed.append(done[5])
    if placed:
        hidden.append(early[1])
        qkv_all.append(more[1])
        attn_all.append(more[2])
    else:
        hidden.append(done[7])
        qkv_all.append(done[8])
        attn_all.append(done[9])
    down_hops.take(down_got)
    down_got = down_hops.send()
    down_swap = swap_cores(down_hops.held)
    up_parts = [(up_hops.held, up_got), (up_swap, swap_cores(up_got))]

    blocks = shape((2, SEQ, D), BF)
    pieces = shape((count, 2 * rows, D), BF)
    squares_of = shape((2, D, D), BF)
    act, slope, up_all, down_grad = {}, {}, {}, {}
    for half in (1, 0):
        if placed:
            one = spread(*up_parts[half], picks[half])
            up_all[half] = one.transpose(1, 0, 2, 3).reshape(2, D, D)
            more, more_specs, outs = (up_all[half],), [VECTOR], [blocks, blocks, squares_of]
        else:
            more, more_specs = up_parts[half], [VECTOR] * 2
            outs = [blocks, blocks, squares_of] + [shape((count // 2, 2 * rows, D), BF)] * 2
        done = call(
            functools.partial(up_kernel, placed, half, count),
            ("up_own", "up_other")[half],
            (slot, second_in, low_grad, hidden[half]) + tuple(more),
            [SCALAR] + [VECTOR] * 3 + more_specs,
            outs,
            [],
            8,
            (1_000_000_000, 4_000_000, 100_000),
        )
        if half == 1:
            done, down_swap = join(done, down_swap)
            second_in = after(second_in, done[0])
        else:
            done, down_got = join(done, down_got)
        act[half], slope[half] = done[:2]
        if placed:
            value = reorder(done[2].reshape(count, 2 * rows, D), turned[half])
            down_grad[half] = (value[: count // 2], value[count // 2 :])
        else:
            up_all[half], down_grad[half] = done[2], tuple(done[3:])
        if half == 1:
            swapped = tuple(swap_cores(one) for one in down_grad[1])
    down_sum = Reducer(down_grad[0], swapped, count)
    down_parts = [(down_hops.held, down_got), (down_swap, swap_cores(down_got))]
    down_got = down_sum.send()

    grad_hidden, up_grad = {}, {}
    before = (hidden_one,)
    for half in (1, 0):
        if placed:
            more = (spread(*down_parts[half], late_picks[half]).reshape(2, D, D),)
            more_specs = [VECTOR]
        else:
            more, more_specs = down_parts[half], [VECTOR] * 2
        done = call(
            functools.partial(down_kernel, placed, half, count),
            ("down_own", "down_other")[half],
            (slot, late_slot, turned_in, low_grad, vectors, act[half], slope[half], up_all[half])
            + before
            + tuple(more),
            [SCALAR] * 2 + [VECTOR] * (6 + len(before)) + more_specs,
            [
                rows_f32 if half else rows_bf,
                rows_f32,
                shape((2, 1, D), F32),
            ]
            + ([squares_of] if placed else [shape((count // 2, 2 * rows, D), BF)] * 2),
            [] if placed else vmem(((2, D, D), BF)),
            14,
            (1_000_000_000, 4_000_000, 0),
        )
        if half == 1:
            done, kept_got = join(done, swapped[0])
            down_sum.keep(down_grad[0][0], kept_got)
        else:
            done, down_got = join(done, down_got)
        before = tuple(done[:2])
        grad_hidden[half] = done[2]
        up_grad[half] = tuple(done[3:])
        if placed:
            value = done[3].reshape(2, count, rows, D).transpose(1, 0, 2, 3)
            value = reorder(value.reshape(count, 2 * rows, D), turned[half])
            up_grad[half] = (value[: count // 2], value[count // 2 :])
        if half == 1:
            swapped = tuple(swap_cores(one) for one in up_grad[1])
    layer_half, grad_second = before
    up_sum = Reducer(up_grad[0], swapped, count)
    up_got = up_sum.send()
    down_sum.take(down_got)

    proj_outs = [shape((3, SEQ, HALF), BF), shape((HALF, D), BF)]
    line_outs = [shape((8, D), F32), shape((2, HALF), F32)]
    done = call(
        back_own_kernel,
        "back_own",
        (
            low_grad,
            vectors,
            grad_second,
            hidden_one,
            proj[0],
            log_total[0],
            mixed[0],
            attn_all[0],
            qkv_all[0],
            bias,
        ),
        [VECTOR] * 10,
        [rows_f32, rows_bf] + proj_outs + line_outs + [rows_f32],
        [],
        12,
        (3_900_000_000, 9_000_000, 1_600_000),
    )
    done, down_sum.sent, kept_got = join(done, down_sum.sent, swapped[0])
    up_sum.keep(up_grad[0][0], kept_got)
    grad_one, grad_low, proj_low_own, grad_attn_own, lines, head_lines_own, grad_first = done
    down_got = down_sum.send()
    front_pieces = shape((count, 4 * rows + 16, HALF), BF)
    small_scratch = vmem(((16, HALF), F32))
    outs = [rows_f32, shape((D, SEQ), BF), line_outs[0]]
    if placed:
        outs += proj_outs + line_outs[1:]
        scratch = []
    else:
        outs += [front_pieces]
        scratch = vmem(((3, SEQ, HALF), BF), ((HALF, D), BF), ((2, HALF), F32)) + small_scratch
    done = call(
        functools.partial(back_other_kernel, placed, count),
        "back_other",
        (
            slot,
            grad_low,
            vectors,
            proj[1],
            log_total[1],
            mixed[1],
            attn_all[1],
            qkv_all[1],
            bias,
            grad_first,
            grad_one,
            lines,
            normed,
            inv_std,
            first_in,
            grad_hidden[1],
        ),
        [SCALAR] + [VECTOR] * 15,
        outs,
        scratch,
        12,
        (5_000_000_000, 12_000_000, 1_600_000),
    )
    done, up_got, down_got = join(done, up_got, down_got)
    input_half, turned_first, lines = done[:3]
    up_sum.take(up_got)
    up_got = up_sum.send()
    down_sum.take(down_got)
    if placed:

        def widen(value):
            return jnp.pad(value, ((0, 0), (0, 0), (0, HALF - value.shape[2])))

        def front_pieces_of(half, proj_low, grad_attn, head_lines):
            grads = [dot_nn(turned_first, proj_low[kind]) for kind in range(3)]
            grads = jnp.stack([one.reshape(count, rows, HALF) for one in grads], axis=1)
            attn_part = grad_attn.reshape(count, part, 2, HALF).transpose(0, 2, 1, 3)
            parts = [
                grads.astype(BF).reshape(count, 3 * rows, HALF),
                attn_part.reshape(count, rows, HALF),
                widen(lines[:6].reshape(6, count, rows).transpose(1, 0, 2)).astype(BF),
                widen(head_lines.reshape(2, count, part).transpose(1, 0, 2)).astype(BF),
                widen(grad_hidden[half].reshape(count, 1, 2 * rows)).astype(BF),
                jnp.zeros((count, 7, HALF), BF),
            ]
            return reorder(jnp.concatenate(parts, axis=1), turned[half])

        front_own = front_pieces_of(0, proj_low_own, grad_attn_own, head_lines_own)
        swapped = swap_cores(front_pieces_of(1, *done[3:]))
    else:
        swapped = swap_cores(done[3])
        (front_own,) = call(
            functools.partial(pieces_kernel, count),
            "pieces",
            (slot, turned_first, proj_low_own, grad_attn_own, lines, head_lines_own, grad_hidden[0]),
            [SCALAR] + [VECTOR] * 6,
            [front_pieces],
            small_scratch,
            8,
            (1_000_000_000, 6_000_000, 0),
        )
        front_own, swapped = lax.optimization_barrier((front_own, swapped))
    front_sum = Reducer(front_own, swapped, count)
    high_got, low_got = front_sum.send_parts()
    front_sum.take_high(high_got)
    front_got = front_sum.send()
    front_sum.take_low(low_got)
    front_sum.take(front_got)
    layer_output = both_halves(layer_half, core)
    input_grad = both_halves(input_half, core)

    up_sum.take(up_got)
    kept, got = down_sum.finish()
    total_down = kept + got.astype(F32)
    kept, got = up_sum.finish()
    total_up = kept + got.astype(F32)
    kept, got = front_sum.finish()
    outs = [shape(kept.shape, F32), shape((2 * count, 8, 128), F32)]
    close_args = (total_down, total_up, kept, got)
    total, squares = call(
        functools.partial(close_kernel, rows),
        "close",
        close_args,
        [VECTOR] * 4,
        outs,
        [],
        16,
        (1_000_000, 1_200_000, 0),
    )
    spread_squares = lax.all_to_all(squares, BOTH, 0, 0, tiled=True)
    state = []
    for index, group in enumerate(groups):
        state += [one.reshape(1, -1) if index == 5 else one for one in group]
    update_args = (spread_squares, total_down, total_up, total) + tuple(state)
    outs = [shape((1, 1), F32)] + [shape(one.shape, F32) for one in state]
    results = call(
        functools.partial(update_kernel, rows),
        "update",
        update_args,
        None,
        outs,
        [],
        60,
        (5_000_000, 8_000_000, 500_000),
        True,
    )
    grad_norm = results[0].reshape(())
    results = [
        one.reshape(-1) if 20 <= index < 24 else one for index, one in enumerate(results[1:])
    ]
    return (layer_output, input_grad, grad_norm, *results)


FORCE_PLAIN = False


def solution(mesh):
    row, late, wide = P("dp", None), P(("mp", "dp"), None), P("dp", "mp")
    kinds = (
        P(None, "dp", "mp"),
        late,
        wide,
        late,
        P(None, ("mp", "dp")),
        P(("mp", "dp")),
        P(None, "dp"),
    )
    per_parameter = tuple(kind for kind in kinds for _ in range(4))
    return jax.shard_map(
        functools.partial(body, FORCE_PLAIN),
        mesh=mesh,
        in_specs=(row, row, row, P("dp")) + per_parameter,
        out_specs=(row, row, P()) + per_parameter,
        check_vma=False,
    )
```

```python
import functools

import jax
import jax.numpy as jnp
from jax import lax
from jax.experimental import pallas as pl
from jax.experimental.pallas import tpu as pltpu
from jax.sharding import PartitionSpec as P

HD = 64
PAIR = 128
SEQ = 512
D = 768
HALF = 384
STEP = 7
SMALL = 8
ASIDE = 128

NORM_EPS = 1e-05
SCORE_SCALE = 0.125
LEARN_RATE = 0.03
VECTOR_RATE = 0.4
BETA_ONE = 0.9
BETA_TWO = 0.95
ADAM_EPS = 1e-08
WEIGHT_DECAY = 0.1
EMA_RATE = 0.8
CLIP_NORM = 1.0
GELU_COEF = 0.7978845608028654
GELU_CUBE = 0.044715
MASKED = -1e30

BF = jnp.bfloat16
F32 = jnp.float32
BOTH = ("dp", "mp")


def dot_nn(left, right):
    return lax.dot_general(left, right, (((1,), (0,)), ((), ())), preferred_element_type=F32)


def dot_nt(left, right):
    return lax.dot_general(left, right, (((1,), (1,)), ((), ())), preferred_element_type=F32)


def dot_tn(left, right):
    return lax.dot_general(left, right, (((0,), (0,)), ((), ())), preferred_element_type=F32)


def norm_parts(rows):
    row_mean = jnp.mean(rows, axis=1, keepdims=True)
    centered = rows - row_mean
    inv_std = lax.rsqrt(jnp.mean(centered * centered, axis=1, keepdims=True) + NORM_EPS)
    return (centered * inv_std, inv_std)


def norm_back(grad_in, normed, inv_std, gain):
    scaled = grad_in * gain
    return inv_std * (
        scaled
        - jnp.mean(scaled, axis=1, keepdims=True)
        - normed * jnp.mean(scaled * normed, axis=1, keepdims=True)
    )


def column_sum(value):
    return jnp.sum(value, axis=0, keepdims=True)


def step_bits(count):
    length = count.bit_length() - 1
    high = [(bit, bit) for bit in reversed(range(2, length))]
    return high + [(0, 1), (1, 0)]


def late_bits(count):
    bits = step_bits(count)
    return bits[-2:-1] + bits[:-2] + bits[-1:]


def step_pairs(count, bits):
    return [
        (index * 2 + core, (index ^ (1 << bits[core])) * 2 + core)
        for index in range(count)
        for core in range(2)
    ]


def slots(count, here, core, steps):
    apart = jnp.arange(count, dtype=jnp.int32) ^ here
    place = jnp.zeros_like(apart)
    for at, bits in enumerate(steps):
        bit = jnp.where(core == 0, (apart >> bits[0]) & 1, (apart >> bits[1]) & 1)
        place = place | (bit << at)
    return place


def reorder(value, pick):
    flat = dot_nn(pick, value.reshape(value.shape[0], -1)).astype(BF)
    return flat.reshape(value.shape)


def swap_cores(value):
    return lax.ppermute(value, "mp", [(0, 1), (1, 0)])


def after(value, *others):
    return lax.optimization_barrier((value,) + others)[0]


def join(made, *gots):
    joined = lax.optimization_barrier(tuple(made) + gots)
    return (list(joined[: len(made)]), *joined[len(made) :])


class Gatherer:
    def __init__(self, piece, count, steps):
        self.count, self.held, self.got = count, piece[None], None
        self.bits = list(steps)

    def send(self, *others):
        if others:
            self.held = after(self.held, *others)
        return lax.ppermute(self.held, BOTH, step_pairs(self.count, self.bits.pop(0)))

    def take(self, got):
        if self.bits:
            self.held = jnp.concatenate([self.held, got], axis=0)
        else:
            self.got = got


class Reducer:
    def __init__(self, own, got, count):
        self.count = count
        self.bits = list(reversed(step_bits(count)))
        self.half = count // 2
        if not isinstance(own, tuple):
            own, got = (own[: self.half], own[self.half :]), (got[: self.half], got[self.half :])
        self.keep(own[0], got[0])
        self.sent = (own[1].astype(F32) + got[1].astype(F32)).astype(BF)

    def keep(self, own, got):
        self.kept = own.astype(F32) + got.astype(F32)

    def pairs(self):
        return step_pairs(self.count, self.bits.pop(0))

    def send(self):
        return lax.ppermute(self.sent, BOTH, self.pairs())

    def take(self, got):
        self.half //= 2
        total = self.kept + got.astype(F32)
        self.kept, self.sent = total[: self.half], total[self.half :].astype(BF)

    def send_parts(self):
        pairs, half = self.pairs(), self.half // 2
        return [lax.ppermute(one, BOTH, pairs) for one in (self.sent[half:], self.sent[:half])]

    def take_high(self, got):
        self.half //= 2
        self.sent = (self.kept[self.half :] + got.astype(F32)).astype(BF)

    def take_low(self, got):
        self.kept = self.kept[: self.half] + got.astype(F32)

    def finish(self):
        while len(self.bits) > 1:
            self.take(self.send())
        return (self.kept[0], self.send()[0])


def pick(slot, held, got, *at):
    half = held.shape[0]
    inner = slot & (half - 1)
    return jnp.where(slot < half, held[(inner, *at)], got[(inner, *at)])


def put(slot, kept, sent, piece, start):
    half = kept.shape[0]
    at = slice(start, start + piece.shape[0])

    @pl.when(slot < half)
    def _():
        kept[slot, at, :] = piece

    @pl.when(slot >= half)
    def _():
        sent[slot - half, at, :] = piece


def pack_kernel(qkv_w, attn_w, up_w, down_w, head_w, hidden_w, vector_w, piece, up, down, small):
    rows = qkv_w.shape[1]
    part = rows // 2
    for kind in range(3):
        piece[kind * rows : (kind + 1) * rows, :] = qkv_w[kind].astype(BF)
    both = jnp.concatenate([attn_w[:, :HALF], attn_w[:, HALF:]], axis=0)
    piece[3 * rows : 3 * rows + 2 * part, :] = both.astype(BF)
    small[...] = jnp.zeros_like(small)
    small[0:6, :rows] = vector_w[...]
    small[6:8, :part] = head_w[...]
    small[6:7, ASIDE : ASIDE + 2 * rows] = hidden_w[...]
    piece[4 * rows :, :] = small[...].astype(BF)
    up[0] = up_w[:, :D].astype(BF)
    up[1] = up_w[:, D:].astype(BF)
    down[...] = down_w[...].astype(BF)


def prepare_kernel(
    core_ref, pads_ref, tokens, cotangent, row_code, key_code, x_out, normed_out, inv_out, low_grad, bias, buffer, sem
):
    at = pl.ds(pl.multiple_of(core_ref[0] * SEQ, SEQ), SEQ)
    copies = [
        pltpu.make_async_copy(tokens.at[at], x_out, sem.at[0]),
        pltpu.make_async_copy(cotangent.at[at], buffer, sem.at[1]),
    ]
    for copy in copies:
        copy.start()
    key_at = lax.broadcasted_iota(jnp.int32, (SEQ, SEQ), 0)
    row_at = lax.broadcasted_iota(jnp.int32, (SEQ, SEQ), 1)
    seen = (key_code[...] == row_code[...]) | (key_at == row_at)
    bias[...] = jnp.where(seen, 0.0, MASKED)
    copies[0].wait()
    normed, inv_std = norm_parts(x_out[...].astype(F32))
    normed_out[...], inv_out[...] = normed, inv_std
    copies[1].wait()
    position = lax.broadcasted_iota(jnp.int32, (SEQ, D), 0)
    kept = position < SEQ - pads_ref[core_ref[0]]
    low_grad[...] = jnp.where(kept, buffer[...].astype(F32), 0.0).astype(BF)


def attend(proj, bias, log_total, mixed):
    lane = lax.broadcasted_iota(jnp.int32, (SEQ, PAIR), 1)
    for pair in range(HALF // PAIR):
        at = slice(pair * PAIR, (pair + 1) * PAIR)
        q_pair, k_pair, v_pair = proj[0, :, at], proj[1, :, at], proj[2, :, at]
        v_turned = v_pair.T
        turned = []
        for side in range(2):
            mine = (lane < HD) if side == 0 else (lane >= HD)
            q_side = jnp.where(mine, q_pair, jnp.zeros_like(q_pair))
            scores = dot_nt(k_pair, q_side) + bias[...]
            top = jnp.max(scores, axis=0, keepdims=True)
            exponent = jnp.exp(scores - top)
            total = jnp.sum(exponent, axis=0, keepdims=True)
            index = pair * 2 + side
            log_total[index : index + 1, :] = top + jnp.log(total)
            part = dot_nn(v_turned[side * HD : (side + 1) * HD], exponent.astype(BF))
            turned.append(part * (1.0 / total))
        mixed[:, at] = jnp.concatenate(turned, axis=0).T.astype(BF)


def front_kernel(placed, half, count, rows, slot_ref, *rest):
    rest = list(rest)
    take = lambda amount: [rest.pop(0) for _ in range(amount)]
    if half == 0:
        x, normed, bias = take(3)
        if placed:
            (vectors,) = take(1)
    else:
        first_in, before, bias, vectors = take(4)
    if placed:
        heads, qkv, attn = take(3)
    else:
        parts = take(2)
    if half == 0:
        first_in, after_out = take(2)
    else:
        after_out, second_in, turned_in = take(3)
    proj, log_total, mixed = take(3)
    if not placed:
        if half == 0:
            (vectors,) = take(1)
        heads, hidden, qkv, attn = take(4)
        held, got = parts
        part = rows // 2
        sides = []
        for index in range(count):
            slot = slot_ref[half, index]
            for kind in range(3):
                qkv[kind, index * rows : (index + 1) * rows, :] = pick(
                    slot, held, got, slice(kind * rows, (kind + 1) * rows)
                )
            sides.append(pick(slot, held, got, slice(3 * rows, 4 * rows)).astype(F32))
            tail = pick(slot, held, got, slice(4 * rows, 4 * rows + SMALL)).astype(F32)
            if half == 0:
                vectors[0:6, index * rows : (index + 1) * rows] = tail[0:6, :rows]
            heads[:, index * part : (index + 1) * part] = tail[6:8, :part]
            start = (index % (count // 2)) * 2 * rows
            at = slice(ASIDE, ASIDE + 2 * rows)
            hidden[index // (count // 2), :, start : start + 2 * rows] = tail[6:7, at]
            if index % 2:
                at = slice((index - 1) * part, (index + 1) * part)
                left = jnp.concatenate([one[:part] for one in sides], axis=0)
                right = jnp.concatenate([one[part:] for one in sides], axis=0)
                attn[at, :HALF] = left.astype(BF)
                attn[at, HALF:] = right.astype(BF)
                sides = []
    if half == 0:
        first_in[...] = (normed[...] * vectors[0:1, :] + vectors[1:2, :]).astype(BF)
    value = dot_nn(first_in[...], qkv[0]) + heads[0:1, :]
    proj[0] = (value.astype(BF).astype(F32) * SCORE_SCALE).astype(BF)
    proj[1] = dot_nn(first_in[...], qkv[1]).astype(BF)
    proj[2] = (dot_nn(first_in[...], qkv[2]) + heads[1:2, :]).astype(BF)
    attend(proj, bias, log_total, mixed)
    value = dot_nn(mixed[...], attn[...])
    if half == 0:
        after_out[...] = x[...].astype(F32) + value + vectors[4:5, :]
        return
    value = before[...] + value
    after_out[...] = value
    normed, _ = norm_parts(value)
    entered = (normed * vectors[2:3, :] + vectors[3:4, :]).astype(BF)
    second_in[...] = entered
    turned_in[...] = entered.T


def up_kernel(placed, half, count, slot_ref, second_in, low_grad, bias, *rest):
    rows = D // count
    if placed:
        up, act, slope, grad_down = rest
    else:
        held, got, act, slope, up, grad_kept, grad_sent = rest
        for index in range(count):
            slot = slot_ref[half, index]
            for block in range(2):
                up[block, index * rows : (index + 1) * rows, :] = pick(slot, held, got, block)
    chunk_rows = 256
    for block in range(2):
        for chunk in range(SEQ // chunk_rows):
            at = slice(chunk * chunk_rows, (chunk + 1) * chunk_rows)
            pre = dot_nn(second_in[at, :], up[block]) + bias[block]
            square = pre * pre
            bent = jnp.tanh(pre * (GELU_COEF + GELU_COEF * GELU_CUBE * square))
            half_up = 0.5 + 0.5 * bent
            gelu = pre * half_up
            act[block, at, :] = gelu.astype(BF)
            inner = pre * (2.0 * GELU_COEF + 6.0 * GELU_COEF * GELU_CUBE * square)
            slope[block, at, :] = (half_up + half_up * (inner - half_up * inner)).astype(BF)
        grad = dot_tn(act[block], low_grad[...]).astype(BF)
        if placed:
            grad_down[block] = grad
            continue
        for index in range(count // 2):
            piece = grad[index * 2 * rows : (index + 1) * 2 * rows, :]
            put(slot_ref[half, block * (count // 2) + index], grad_kept, grad_sent, piece, 0)


def down_kernel(
    placed, half, count, slot_ref, late_ref, turned_in, low_grad, vectors, act, slope, up, before_out, *rest
):
    rows = D // count
    rest = list(rest)
    take = lambda amount: [rest.pop(0) for _ in range(amount)]
    if half == 0:
        (before_grad,) = take(1)
    if placed:
        down, out, grad_second, grad_hidden, grad_up = rest
    else:
        held, got, out, grad_second, grad_hidden, grad_kept, grad_sent, down = rest
    parts_out = []
    for block in range(2):
        if not placed:
            for index in range(count // 2):
                slot = late_ref[half, block * (count // 2) + index]
                at = slice(index * 2 * rows, (index + 1) * 2 * rows)
                down[block, at, :] = pick(slot, held, got)
        grad_pre = dot_nt(low_grad[...], down[block]) * slope[block].astype(F32)
        grad_hidden[block] = column_sum(grad_pre)
        pre_low = grad_pre.astype(BF)
        grad = dot_nn(turned_in[...], pre_low).astype(BF)
        part_out = dot_nn(act[block], down[block])
        part_grad = dot_nt(pre_low, up[block])
        if half == 1 and block == 0:
            out[...] = before_out[...] + vectors[5:6, :] + part_out
            grad_second[...] = part_grad
        elif half == 1:
            out[...] += part_out
            grad_second[...] += part_grad
        elif block == 0:
            parts_out.append(part_out)
            grad_second[...] = before_grad[...] + part_grad
        else:
            out[...] = (before_out[...] + (parts_out[0] + part_out)).astype(BF)
            grad_second[...] += part_grad
        if placed:
            grad_up[block] = grad
            continue
        for index in range(count):
            piece = grad[index * rows : (index + 1) * rows, :]
            put(slot_ref[half, index], grad_kept, grad_sent, piece, block * rows)


def attend_back(proj, log_total, mixed, attn, bias, grad_low, proj_low, grad_attn, head_lines):
    lane = lax.broadcasted_iota(jnp.int32, (SEQ, PAIR), 1)
    grad_attn[...] = dot_tn(mixed[...], grad_low).astype(BF)
    grad_mixed = dot_nt(grad_low, attn[...]).astype(BF)
    for pair in range(HALF // PAIR):
        at = slice(pair * PAIR, (pair + 1) * PAIR)
        q_pair, k_pair, v_pair = proj[0, :, at], proj[1, :, at], proj[2, :, at]
        g_pair = grad_mixed[:, at]
        k_turned = k_pair.T
        grad_key = jnp.zeros((SEQ, PAIR), F32)
        grad_value = jnp.zeros((SEQ, PAIR), F32)
        turned = []
        for side in range(2):
            mine = (lane < HD) if side == 0 else (lane >= HD)
            q_side = jnp.where(mine, q_pair, jnp.zeros_like(q_pair))
            g_side = jnp.where(mine, g_pair, jnp.zeros_like(g_pair))
            index = pair * 2 + side
            scores = dot_nt(k_pair, q_side) + bias[...]
            probs = jnp.exp(scores - log_total[index : index + 1, :])
            grad_probs = dot_nt(v_pair, g_side)
            row_dot = column_sum(probs * grad_probs)
            grad_scores = (probs * (grad_probs - row_dot)).astype(BF)
            grad_value = grad_value + dot_nn(probs.astype(BF), g_side)
            grad_key = grad_key + dot_nn(grad_scores, q_side)
            turned.append(dot_nn(k_turned[side * HD : (side + 1) * HD], grad_scores))
        grad_query = jnp.concatenate(turned, axis=0).T * SCORE_SCALE
        head_lines[0:1, at] = column_sum(grad_query)
        head_lines[1:2, at] = column_sum(grad_value)
        proj_low[0, :, at] = grad_query.astype(BF)
        proj_low[1, :, at] = grad_key.astype(BF)
        proj_low[2, :, at] = grad_value.astype(BF)


def first_part(proj_low, qkv):
    total = dot_nt(proj_low[0], qkv[0])
    for kind in range(1, 3):
        total = total + dot_nt(proj_low[kind], qkv[kind])
    return total


def pieces_out(half, count, slot_ref, turned_first, proj_low, grad_attn, lines, head_lines, grad_hidden, out, small):
    rows = D // count
    part = rows // 2
    for kind in range(3):
        grad_qkv = dot_nn(turned_first[...], proj_low[kind]).astype(BF)
        for index in range(count):
            out[slot_ref[half, index], kind * rows : (kind + 1) * rows, :] = grad_qkv[
                index * rows : (index + 1) * rows, :
            ]
    small[...] = jnp.zeros_like(small)
    whole = grad_attn[...].astype(F32)
    for index in range(count):
        start = (index % (count // 2)) * 2 * rows
        slot = slot_ref[half, index]
        piece = whole[index * part : (index + 1) * part, :]
        piece = jnp.concatenate([piece[:, :HALF], piece[:, HALF:]], axis=0)
        out[slot, 3 * rows : 4 * rows, :] = piece.astype(BF)
        small[0:6, :rows] = lines[0:6, index * rows : (index + 1) * rows]
        small[6:8, :part] = head_lines[:, index * part : (index + 1) * part]
        small[6:7, ASIDE : ASIDE + 2 * rows] = grad_hidden[
            index // (count // 2), :, start : start + 2 * rows
        ]
        out[slot, 4 * rows :, :] = small[...].astype(BF)


def back_own_kernel(
    low_grad,
    vectors,
    grad_second,
    hidden_one,
    proj,
    log_total,
    mixed,
    attn,
    qkv,
    bias,
    grad_one_out,
    grad_low_out,
    proj_low,
    grad_attn,
    lines,
    head_lines,
    grad_first,
):
    grad_out = low_grad[...].astype(F32)
    normed, inv_std = norm_parts(hidden_one[...])
    grads = grad_second[...]
    lines[2:3, :], lines[3:4, :] = column_sum(grads * normed), column_sum(grads)
    grad_one = grad_out + norm_back(grads, normed, inv_std, vectors[2:3, :])
    grad_one_out[...] = grad_one
    lines[4:5, :], lines[5:6, :] = column_sum(grad_one), column_sum(grad_out)
    grad_low = grad_one.astype(BF)
    grad_low_out[...] = grad_low
    attend_back(proj, log_total, mixed, attn, bias, grad_low, proj_low, grad_attn, head_lines)
    grad_first[...] = first_part(proj_low, qkv)


def back_other_kernel(
    placed,
    count,
    slot_ref,
    grad_low,
    vectors,
    proj,
    log_total,
    mixed,
    attn,
    qkv,
    bias,
    before_first,
    grad_one,
    before_lines,
    normed,
    inv_std,
    first_in,
    grad_hidden,
    input_grad,
    turned_first,
    lines,
    *rest,
):
    if placed:
        proj_low, grad_attn, head_lines = rest
    else:
        out, proj_low, grad_attn, head_lines, small = rest
    attend_back(proj, log_total, mixed, attn, bias, grad_low[...], proj_low, grad_attn, head_lines)
    grad_first = before_first[...] + first_part(proj_low, qkv)
    lines[...] = before_lines[...]
    lines[0:1, :] = column_sum(grad_first * normed[...])
    lines[1:2, :] = column_sum(grad_first)
    back = norm_back(grad_first, normed[...], inv_std[...], vectors[0:1, :])
    input_grad[...] = grad_one[...] + back
    turned_first[...] = first_in[...].T
    if not placed:
        pieces_out(
            1, count, slot_ref, turned_first, proj_low, grad_attn, lines, head_lines, grad_hidden, out, small
        )


def pieces_kernel(count, slot_ref, turned_first, proj_low, grad_attn, lines, head_lines, grad_hidden, out, small):
    pieces_out(
        0, count, slot_ref, turned_first, proj_low, grad_attn, lines, head_lines, grad_hidden, out, small
    )


def close_kernel(rows, total_down, total_up, kept, got, total, squares):
    value = kept[...] + got[...].astype(F32)
    total[...] = value
    part = jnp.sum(total_down[...] * total_down[...]) + jnp.sum(total_up[...] * total_up[...])
    row = lax.broadcasted_iota(jnp.int32, value.shape, 0)
    weight = jnp.where((row >= 4 * rows) & (row < 4 * rows + 6), 0.5, 1.0)
    part = part + jnp.sum(value * value * weight)
    squares[...] = jnp.full(squares.shape, part, F32)


def adam_step(gradient, master, first, second, average, factor, decay_rate, step_rate):
    clipped = gradient * factor
    first_new = BETA_ONE * first + (1.0 - BETA_ONE) * clipped
    second_new = BETA_TWO * second + (1.0 - BETA_TWO) * clipped * clipped
    first_hat = first_new / (1.0 - BETA_ONE**STEP)
    second_hat = second_new / (1.0 - BETA_TWO**STEP)
    master_new = master - step_rate * (
        first_hat / (jnp.sqrt(second_hat) + ADAM_EPS) + decay_rate * master
    )
    average_new = EMA_RATE * average + (1.0 - EMA_RATE) * master_new
    return (first_new, second_new, master_new, average_new)


def update_kernel(rows, spread, total_down, total_up, total, *rest):
    state, norm, results = rest[:28], rest[28], rest[29:]
    grad_norm = jnp.sqrt(jnp.sum(spread[...], axis=0))[0:1, 0:1]
    norm[...] = grad_norm
    factor = CLIP_NORM / jnp.maximum(grad_norm, CLIP_NORM)
    part = rows // 2

    def apply(index, at, gradient):
        decay, rate = (WEIGHT_DECAY, LEARN_RATE) if index < 4 else (0.0, VECTOR_RATE)
        values = adam_step(
            gradient, *[state[4 * index + k][at] for k in range(4)], factor, decay, rate
        )
        for k in range(4):
            results[4 * index + k][at] = values[k]

    for kind in range(3):
        apply(0, (kind,), total[kind * rows : (kind + 1) * rows, :])
    for side in range(2):
        start = 3 * rows + side * part
        columns = slice(side * HALF, (side + 1) * HALF)
        apply(1, (slice(None), columns), total[start : start + part, :])
        columns = slice(side * D, (side + 1) * D)
        apply(2, (slice(None), columns), total_up[side * rows : (side + 1) * rows, :])
    every = (slice(None), slice(None))
    apply(3, every, total_down[...])
    apply(4, every, total[4 * rows + 6 : 4 * rows + 8, :part])
    apply(5, every, total[4 * rows + 6 : 4 * rows + 7, ASIDE : ASIDE + 2 * rows])
    apply(6, every, total[4 * rows : 4 * rows + 6, :rows])


def vmem(*shapes):
    return [pltpu.VMEM(shape, dtype) for shape, dtype in shapes]


def shape(dims, dtype):
    return jax.ShapeDtypeStruct(dims, dtype)


def whole_spec(dims):
    return pl.BlockSpec(dims, lambda *_: (0,) * len(dims))


VECTOR = pl.BlockSpec(memory_space=pltpu.VMEM)
SCALAR = pl.BlockSpec(memory_space=pltpu.SMEM)
ANYWHERE = pl.BlockSpec(memory_space=pl.ANY)


def call(body, name, args, specs, outs, scratch, mib, cost, streamed=False):
    flops, touched, special = cost
    if streamed:
        more = {
            "grid": (1,),
            "in_specs": [whole_spec(one.shape) for one in args],
            "out_specs": [whole_spec(one.shape) for one in outs],
        }
    else:
        more = {"in_specs": specs, "out_specs": [VECTOR] * len(outs)}
    return pl.pallas_call(
        body,
        out_shape=outs,
        scratch_shapes=scratch,
        compiler_params=pltpu.CompilerParams(vmem_limit_bytes=mib << 20),
        cost_estimate=pl.CostEstimate(
            flops=flops, bytes_accessed=touched, transcendentals=special
        ),
        name=name,
        **more,
    )(*args)


def both_halves(own, core):
    other = swap_cores(own)
    first = jnp.where(core == 0, own, other)
    second = jnp.where(core == 0, other, own)
    return jnp.concatenate([first, second], axis=0)


def body(force_plain, *args):
    (tokens, cotangent, seg_lengths, pad_counts) = args[:4]
    groups = [args[4 + 4 * i : 8 + 4 * i] for i in range(7)]
    qkv_w, attn_w, up_w, down_w, head_w, hidden_w, vector_w = (group[0] for group in groups)
    rows = qkv_w.shape[1]
    part = rows // 2
    count = D // rows
    placed = bool(rows % 16) or force_plain
    here, core = lax.axis_index("dp"), lax.axis_index("mp")
    steps, late_steps = step_bits(count), late_bits(count)
    slot, late_slot = (
        jnp.stack([slots(count, here, core, one), slots(count, here, 1 - core, one)], axis=0)
        for one in (steps, late_steps)
    )
    core_at = core.reshape(1).astype(jnp.int32)

    packed = [shape((4 * rows + SMALL, HALF), BF), shape((2, rows, D), BF), shape((2 * rows, D), BF)]
    pack_args = (qkv_w, attn_w, up_w, down_w, head_w, hidden_w.reshape(1, -1), vector_w)
    piece, up_piece, down_piece = call(
        pack_kernel,
        "pack",
        pack_args,
        None,
        packed,
        vmem(((SMALL, HALF), F32)),
        60,
        (1, 1_400_000, 0),
        True,
    )
    front_hops, up_hops, down_hops = (
        Gatherer(one, count, order)
        for one, order in ((piece, steps), (up_piece, steps), (down_piece, late_steps))
    )
    lengths = lax.dynamic_index_in_dim(seg_lengths, core, 0, keepdims=False)
    padding = lax.dynamic_index_in_dim(pad_counts, core, 0, keepdims=False)
    upto = jnp.arange(lengths.shape[0])[:, None] >= jnp.arange(lengths.shape[0])[None, :]
    bounds = jnp.sum(jnp.where(upto, lengths[None, :], 0), axis=1)
    position = jnp.arange(SEQ, dtype=jnp.int32)
    row_code = jnp.sum((position[None, :] >= bounds[:, None]).astype(jnp.int32), axis=0)[None, :]
    key_code = jnp.sum((position[:, None] >= bounds[None, :]).astype(jnp.int32), axis=1)[:, None]
    key_code = jnp.where(position[:, None] >= SEQ - padding, -1, key_code)

    rows_bf, rows_f32 = shape((SEQ, D), BF), shape((SEQ, D), F32)
    half_bf = shape((SEQ, HALF), BF)

    high = len(front_hops.bits) - 2
    front_got = front_hops.send()
    prepared = call(
        prepare_kernel,
        "prepare",
        (core_at, pad_counts, tokens, cotangent, row_code, key_code),
        [SCALAR] * 2 + [ANYWHERE] * 2 + [VECTOR] * 2,
        [rows_bf, rows_f32, shape((SEQ, 1), F32), rows_bf, shape((SEQ, SEQ), F32)],
        vmem(((SEQ, D), BF)) + [pltpu.SemaphoreType.DMA((2,))],
        12,
        (3_000_000, 9_000_000, 0),
    )
    prepared, front_got, slot, late_slot = join(prepared, front_got, slot, late_slot)
    x_own, normed, inv_std, low_grad, bias = prepared
    front_hops.take(front_got)
    for hop in range(high):
        gots = [front_hops.send(), up_hops.send(front_hops.held)]
        if hop == 0:
            gots.append(down_hops.send(front_hops.held))
        _, *gots = join((), *gots)
        for hops, got in zip((front_hops, up_hops, down_hops), gots):
            hops.take(got)
    front_got, up_got = front_hops.send(), up_hops.send()
    for _ in range(high - 1):
        down_hops.take(down_hops.send(up_hops.held))
    front_swap = swap_cores(front_hops.held)
    _, front_got, up_got, front_swap, down_hops.held = join(
        (), front_got, up_got, front_swap, down_hops.held
    )
    up_hops.take(up_got)
    front_swap_got = swap_cores(front_got)
    up_got, down_got = up_hops.send(), down_hops.send()

    if placed:
        index = jnp.arange(count, dtype=jnp.int32)[None, :]
        picks, late_picks = (
            [(one[half][:, None] == index).astype(BF) for half in range(2)]
            for one in (slot, late_slot)
        )
        turned = [one.T for one in picks]

    def spread(held, got, pick):
        return reorder(jnp.concatenate([held, got], axis=0), pick)

    def front_more(held, got, half):
        if not placed:
            return (), (held, got), [VECTOR] * 2
        one = spread(held, got, picks[half])
        tail = one[:, 4 * rows :].astype(F32)
        vectors = tail[:, :6, :rows].transpose(1, 0, 2).reshape(6, D)
        heads = tail[:, 6:8, :part].transpose(1, 0, 2).reshape(2, HALF)
        hidden = tail[:, 6, ASIDE : ASIDE + 2 * rows].reshape(2, 1, D)
        qkv = one[:, : 3 * rows].reshape(count, 3, rows, HALF).transpose(1, 0, 2, 3)
        attn = one[:, 3 * rows : 4 * rows].reshape(count, 2, part, HALF).transpose(0, 2, 1, 3)
        more = (heads, qkv.reshape(3, D, HALF), attn.reshape(HALF, D))
        return (jnp.pad(vectors, ((0, 2), (0, 0))), hidden), more, [VECTOR] * 3

    extra_outs = [
        shape((2, HALF), F32),
        shape((2, 1, D), F32),
        shape((3, D, HALF), BF),
        shape((HALF, D), BF),
    ]
    attend_outs = [shape((3, SEQ, HALF), BF), shape((HALF // HD, SEQ), F32), half_bf]
    front_cost = (3_000_000_000, 9_000_000, 1_600_000)

    early, more, more_specs = front_more(front_hops.held, front_got, 0)
    done = call(
        functools.partial(front_kernel, placed, 0, count, rows),
        "front_own",
        (slot, x_own, normed, bias) + early[:1] + more,
        [SCALAR] + [VECTOR] * (3 + len(early[:1])) + more_specs,
        [rows_bf, rows_f32] + attend_outs + ([] if placed else [shape((8, D), F32)] + extra_outs),
        [],
        12,
        front_cost,
    )
    done, front_swap_got = join(done, front_swap_got)
    first_in, before = done[:2]
    proj, log_total, mixed = [done[2]], [done[3]], [done[4]]
    if placed:
        vectors, hidden = early[0], [early[1]]
        qkv_all, attn_all = [more[1]], [more[2]]
    else:
        vectors, hidden = done[5], [done[7]]
        qkv_all, attn_all = [done[8]], [done[9]]

    early, more, more_specs = front_more(front_swap, front_swap_got, 1)
    up_swap = swap_cores(up_hops.held)
    done = call(
        functools.partial(front_kernel, placed, 1, count, rows),
        "front_other",
        (slot, first_in, before, bias, vectors) + more,
        [SCALAR] + [VECTOR] * 4 + more_specs,
        [rows_f32, rows_bf, shape((D, SEQ), BF)] + attend_outs + ([] if placed else extra_outs),
        [],
        12,
        front_cost,
    )
    done, up_got, down_got, up_swap = join(done, up_got, down_got, up_swap)
    hidden_one, second_in, turned_in = done[:3]
    proj.append(done[3])
    log_total.append(done[4])
    mixed.append(done[5])
    if placed:
        hidden.append(early[1])
        qkv_all.append(more[1])
        attn_all.append(more[2])
    else:
        hidden.append(done[7])
        qkv_all.append(done[8])
        attn_all.append(done[9])
    down_hops.take(down_got)
    down_got = down_hops.send()
    down_swap = swap_cores(down_hops.held)
    up_parts = [(up_hops.held, up_got), (up_swap, swap_cores(up_got))]

    blocks = shape((2, SEQ, D), BF)
    pieces = shape((count, 2 * rows, D), BF)
    squares_of = shape((2, D, D), BF)
    act, slope, up_all, down_grad = {}, {}, {}, {}
    for half in (1, 0):
        if placed:
            one = spread(*up_parts[half], picks[half])
            up_all[half] = one.transpose(1, 0, 2, 3).reshape(2, D, D)
            more, more_specs, outs = (up_all[half],), [VECTOR], [blocks, blocks, squares_of]
        else:
            more, more_specs = up_parts[half], [VECTOR] * 2
            outs = [blocks, blocks, squares_of] + [shape((count // 2, 2 * rows, D), BF)] * 2
        done = call(
            functools.partial(up_kernel, placed, half, count),
            ("up_own", "up_other")[half],
            (slot, second_in, low_grad, hidden[half]) + tuple(more),
            [SCALAR] + [VECTOR] * 3 + more_specs,
            outs,
            [],
            8,
            (1_000_000_000, 4_000_000, 100_000),
        )
        if half == 1:
            done, down_swap = join(done, down_swap)
            second_in = after(second_in, done[0])
        else:
            done, down_got = join(done, down_got)
        act[half], slope[half] = done[:2]
        if placed:
            value = reorder(done[2].reshape(count, 2 * rows, D), turned[half])
            down_grad[half] = (value[: count // 2], value[count // 2 :])
        else:
            up_all[half], down_grad[half] = done[2], tuple(done[3:])
        if half == 1:
            swapped = tuple(swap_cores(one) for one in down_grad[1])
    down_sum = Reducer(down_grad[0], swapped, count)
    down_parts = [(down_hops.held, down_got), (down_swap, swap_cores(down_got))]
    down_got = down_sum.send()

    grad_hidden, up_grad = {}, {}
    before = (hidden_one,)
    for half in (1, 0):
        if placed:
            more = (spread(*down_parts[half], late_picks[half]).reshape(2, D, D),)
            more_specs = [VECTOR]
        else:
            more, more_specs = down_parts[half], [VECTOR] * 2
        done = call(
            functools.partial(down_kernel, placed, half, count),
            ("down_own", "down_other")[half],
            (slot, late_slot, turned_in, low_grad, vectors, act[half], slope[half], up_all[half])
            + before
            + tuple(more),
            [SCALAR] * 2 + [VECTOR] * (6 + len(before)) + more_specs,
            [
                rows_f32 if half else rows_bf,
                rows_f32,
                shape((2, 1, D), F32),
            ]
            + ([squares_of] if placed else [shape((count // 2, 2 * rows, D), BF)] * 2),
            [] if placed else vmem(((2, D, D), BF)),
            14,
            (1_000_000_000, 4_000_000, 0),
        )
        if half == 1:
            done, kept_got = join(done, swapped[0])
            down_sum.keep(down_grad[0][0], kept_got)
        else:
            done, down_got = join(done, down_got)
        before = tuple(done[:2])
        grad_hidden[half] = done[2]
        up_grad[half] = tuple(done[3:])
        if placed:
            value = done[3].reshape(2, count, rows, D).transpose(1, 0, 2, 3)
            value = reorder(value.reshape(count, 2 * rows, D), turned[half])
            up_grad[half] = (value[: count // 2], value[count // 2 :])
        if half == 1:
            swapped = tuple(swap_cores(one) for one in up_grad[1])
    layer_half, grad_second = before
    up_sum = Reducer(up_grad[0], swapped, count)
    up_got = up_sum.send()
    down_sum.take(down_got)

    proj_outs = [shape((3, SEQ, HALF), BF), shape((HALF, D), BF)]
    line_outs = [shape((8, D), F32), shape((2, HALF), F32)]
    done = call(
        back_own_kernel,
        "back_own",
        (
            low_grad,
            vectors,
            grad_second,
            hidden_one,
            proj[0],
            log_total[0],
            mixed[0],
            attn_all[0],
            qkv_all[0],
            bias,
        ),
        [VECTOR] * 10,
        [rows_f32, rows_bf] + proj_outs + line_outs + [rows_f32],
        [],
        12,
        (3_900_000_000, 9_000_000, 1_600_000),
    )
    done, down_sum.sent, kept_got = join(done, down_sum.sent, swapped[0])
    up_sum.keep(up_grad[0][0], kept_got)
    grad_one, grad_low, proj_low_own, grad_attn_own, lines, head_lines_own, grad_first = done
    down_got = down_sum.send()
    front_pieces = shape((count, 4 * rows + SMALL, HALF), BF)
    small_scratch = vmem(((SMALL, HALF), F32))
    outs = [rows_f32, shape((D, SEQ), BF), line_outs[0]]
    if placed:
        outs += proj_outs + line_outs[1:]
        scratch = []
    else:
        outs += [front_pieces]
        scratch = vmem(((3, SEQ, HALF), BF), ((HALF, D), BF), ((2, HALF), F32)) + small_scratch
    done = call(
        functools.partial(back_other_kernel, placed, count),
        "back_other",
        (
            slot,
            grad_low,
            vectors,
            proj[1],
            log_total[1],
            mixed[1],
            attn_all[1],
            qkv_all[1],
            bias,
            grad_first,
            grad_one,
            lines,
            normed,
            inv_std,
            first_in,
            grad_hidden[1],
        ),
        [SCALAR] + [VECTOR] * 15,
        outs,
        scratch,
        12,
        (5_000_000_000, 12_000_000, 1_600_000),
    )
    done, up_got, down_got = join(done, up_got, down_got)
    input_half, turned_first, lines = done[:3]
    up_sum.take(up_got)
    up_got = up_sum.send()
    down_sum.take(down_got)
    if placed:

        def widen(value):
            return jnp.pad(value, ((0, 0), (0, 0), (0, HALF - value.shape[2])))

        def front_pieces_of(half, proj_low, grad_attn, head_lines):
            grads = [dot_nn(turned_first, proj_low[kind]) for kind in range(3)]
            grads = jnp.stack([one.reshape(count, rows, HALF) for one in grads], axis=1)
            attn_part = grad_attn.reshape(count, part, 2, HALF).transpose(0, 2, 1, 3)
            parts = [
                grads.astype(BF).reshape(count, 3 * rows, HALF),
                attn_part.reshape(count, rows, HALF),
                widen(lines[:6].reshape(6, count, rows).transpose(1, 0, 2)).astype(BF),
                (
                    widen(head_lines.reshape(2, count, part).transpose(1, 0, 2))
                    + jnp.pad(
                        grad_hidden[half].reshape(count, 1, 2 * rows),
                        ((0, 0), (0, 1), (ASIDE, HALF - ASIDE - 2 * rows)),
                    )
                ).astype(BF),
            ]
            return reorder(jnp.concatenate(parts, axis=1), turned[half])

        front_own = front_pieces_of(0, proj_low_own, grad_attn_own, head_lines_own)
        swapped = swap_cores(front_pieces_of(1, *done[3:]))
    else:
        swapped = swap_cores(done[3])
        (front_own,) = call(
            functools.partial(pieces_kernel, count),
            "pieces",
            (slot, turned_first, proj_low_own, grad_attn_own, lines, head_lines_own, grad_hidden[0]),
            [SCALAR] + [VECTOR] * 6,
            [front_pieces],
            small_scratch,
            8,
            (1_000_000_000, 6_000_000, 0),
        )
        front_own, swapped = lax.optimization_barrier((front_own, swapped))
    front_sum = Reducer(front_own, swapped, count)
    high_got, low_got = front_sum.send_parts()
    front_sum.take_high(high_got)
    front_got = front_sum.send()
    front_sum.take_low(low_got)
    front_sum.take(front_got)
    layer_output = both_halves(layer_half, core)
    input_grad = both_halves(input_half, core)

    up_sum.take(up_got)
    kept, got = down_sum.finish()
    total_down = kept + got.astype(F32)
    kept, got = up_sum.finish()
    total_up = kept + got.astype(F32)
    kept, got = front_sum.finish()
    outs = [shape(kept.shape, F32), shape((2 * count, 8, 128), F32)]
    close_args = (total_down, total_up, kept, got)
    total, squares = call(
        functools.partial(close_kernel, rows),
        "close",
        close_args,
        [VECTOR] * 4,
        outs,
        [],
        16,
        (1_000_000, 1_200_000, 0),
    )
    spread_squares = lax.all_to_all(squares, BOTH, 0, 0, tiled=True)
    state = []
    for index, group in enumerate(groups):
        state += [one.reshape(1, -1) if index == 5 else one for one in group]
    update_args = (spread_squares, total_down, total_up, total) + tuple(state)
    outs = [shape((1, 1), F32)] + [shape(one.shape, F32) for one in state]
    results = call(
        functools.partial(update_kernel, rows),
        "update",
        update_args,
        None,
        outs,
        [],
        60,
        (5_000_000, 8_000_000, 500_000),
        True,
    )
    grad_norm = results[0].reshape(())
    results = [
        one.reshape(-1) if 20 <= index < 24 else one for index, one in enumerate(results[1:])
    ]
    return (layer_output, input_grad, grad_norm, *results)


FORCE_PLAIN = False


def solution(mesh):
    row, late, wide = P("dp", None), P(("mp", "dp"), None), P("dp", "mp")
    kinds = (
        P(None, "dp", "mp"),
        late,
        wide,
        late,
        P(None, ("mp", "dp")),
        P(("mp", "dp")),
        P(None, "dp"),
    )
    per_parameter = tuple(kind for kind in kinds for _ in range(4))
    return jax.shard_map(
        functools.partial(body, FORCE_PLAIN),
        mesh=mesh,
        in_specs=(row, row, row, P("dp")) + per_parameter,
        out_specs=(row, row, P()) + per_parameter,
        check_vma=False,
    )
```
